32 devices in a mesh: dp: 8 (over y, x, core), mp: 4 (over z).
Axes of the slice: x: 2, y: 2, z: 4, core: 2. Of those that a mesh axis runs over, the one named last changes fastest.
Arguments:
- tokens: bfloat16 [768, 32768], P('mp', 'dp'), may hold values from -6 to 6
- bucket: int32 [64], P('dp'), may hold values from 0 to 2
- w_in: bfloat16 [768, 3072], P(None, 'mp'), may hold values from -0.21875 to 0.21875
- b_in: float32 [3072], P('mp'), may hold values from -3 to 3
- w_out: bfloat16 [3072, 768], P('mp'), may hold values from -0.15625 to 0.15625
- b_out: float32 [768], P('mp'), may hold values from -3 to 3
- gain_one: float32 [768], P('mp'), may hold values from 0.1 to 1.9
- shift_one: float32 [768], P('mp'), may hold values from -3 to 3
- gain_two: float32 [768], P('mp'), may hold values from 0.1 to 1.9
- shift_two: float32 [768], P('mp'), may hold values from -4 to 4
- mask: int32 [32768], P('dp'), may hold values from 0 to 1, as said below
- labels: int32 [32768], P('dp'), may hold values from 0 to 767
- cotangent: bfloat16 [768, 32768], P('mp', 'dp'), may hold values from -6 to 6
Outputs:
- output: bfloat16 [768, 32768], P('mp', 'dp')
- d_tokens: float32 [768, 32768], P('mp', 'dp')
- d_w_in: float32 [768, 3072], P(None, 'mp')
- d_b_in: float32 [3072], P('mp')
- d_w_out: float32 [3072, 768], P('mp')
- d_b_out: float32 [768], P('mp')
- d_gain_one: float32 [768], P('mp')
- d_shift_one: float32 [768], P('mp')
- d_gain_two: float32 [768], P('mp')
- d_shift_two: float32 [768], P('mp')
- hits: float32 [], replicated
The draws below stay inside these ranges and needn't reach their ends.
Inputs may be any that keep to these rules, and one draw needn't show every extreme that they name: `mask`: 1 marks a masked token, 0 an unmasked one. `labels`: a feature index of the model width.
All inputs are finite; a program needn't handle non-finite values.
Results may differ from the reference program's by a relative error of at most 0.0071.
Values may be sent and summed in bfloat16 or wider, within the bound.
A program may use at most 192 MiB of HBM per device.

```python
import math
import jax
import jax.numpy as jnp
import numpy as np
from jax import lax

D = 768
FF = 3072
SLOT_LEN = 512
SLOTS = 64
TOKENS = 32768


def draw_mask(key, part):
    places = jnp.arange(TOKENS, dtype=jnp.int32)
    rolled = jax.random.randint(key, (TOKENS,), 0, 8 * TOKENS, dtype=jnp.int32)
    return (rolled < TOKENS + 3 * places).astype(jnp.int32)


def plant(entries, key, smallest, top_value):
    place = [jax.random.randint(jax.random.fold_in(key, axis), (), 0, length) for axis, length in enumerate(entries.shape)]
    main_axis = entries.shape.index(max(entries.shape))
    neighbour = place[:main_axis] + [(place[main_axis] + 1) % entries.shape[main_axis]] + place[main_axis + 1:]
    return entries.at[tuple(place)].set(smallest).at[tuple(neighbour)].set(top_value)


def block_scale(own_key, dims, pieces, smallest, largest):
    def one(axis_at, shards_of):
        draws = jax.random.uniform(jax.random.fold_in(jax.random.fold_in(own_key, 6), axis_at), (shards_of,), jnp.float32, smallest / len(pieces), largest / len(pieces))
        return jnp.repeat(jnp.exp(draws), dims[axis_at] // shards_of).reshape((-1,) + (1,) * (len(dims) - axis_at - 1))

    level = one(*pieces[0])
    for cut in pieces[1:]:
        level = level * one(*cut)
    return level


def rank_table(number_of, skew):
    weights = [(1 << 20) // math.isqrt(rank ** skew) + 1 for rank in range(1, number_of + 1)]
    scale = 1 + sum(weights) // (1 << 30)
    return np.cumsum(np.array([max(1, weight // scale) for weight in weights]))


def ranked_ids(own_key, extent, count, lean):
    listing = rank_table(count, lean)
    ticket = jax.random.randint(jax.random.fold_in(own_key, 1), extent, 0, int(listing[count - 1]))
    standing = jnp.searchsorted(jnp.asarray(listing, jnp.int32), ticket, side="right")
    return jax.random.permutation(jax.random.fold_in(own_key, 2), count)[standing].astype(jnp.int32)


def scatter_about(key, extent, scale, limit, pieces=(), kind=jnp.bfloat16):
    values = jax.random.normal(key, extent, jnp.float32) * scale
    if len(pieces) > 0:
        values = block_scale(key, extent, pieces, -0.22, 0.18) * values
    return jnp.clip(values, min=-limit, max=limit).astype(kind)


def setup_inputs(seed: int = 0) -> dict:
    arg_keys = jax.random.split(jax.random.key(seed), 14)
    return {
        "tokens": scatter_about(arg_keys[0], (D, TOKENS), 1.0, 6.0, ((0, 4), (1, 8))),
        "bucket": plant(jax.random.randint(arg_keys[1], (SLOTS,), 0, 3), jax.random.fold_in(arg_keys[1], 1), 0, 2).astype(jnp.int32),
        "w_in": scatter_about(arg_keys[2], (D, FF), D ** -0.5, 0.21875, ((1, 4),)),
        "b_in": scatter_about(arg_keys[3], (FF,), 0.5, 3.0, ((0, 4),), jnp.float32),
        "w_out": scatter_about(arg_keys[4], (FF, D), (FF // 2) ** -0.5, 0.15625, ((0, 4),)),
        "b_out": scatter_about(arg_keys[5], (D,), 0.5, 3.0, ((0, 4),), jnp.float32),
        "gain_one": jnp.clip(1.0 + 0.18 * jax.random.normal(arg_keys[6], (D,), jnp.float32), 0.1, 1.9),
        "shift_one": scatter_about(arg_keys[7], (D,), 0.5, 3.0, ((0, 4),), jnp.float32),
        "gain_two": jnp.clip(1.0 + 0.18 * jax.random.normal(arg_keys[8], (D,), jnp.float32), 0.1, 1.9),
        "shift_two": scatter_about(arg_keys[9], (D,), 1.0, 4.0, ((0, 4),), jnp.float32),
        "mask": draw_mask(jax.random.fold_in(arg_keys[13], 71), 0),
        "labels": plant(ranked_ids(arg_keys[11], (TOKENS,), D, 3), jax.random.fold_in(arg_keys[11], 3), 0, D - 1).astype(jnp.int32),
        "cotangent": scatter_about(arg_keys[12], (D, TOKENS), 1.0, 6.0, ((0, 4), (1, 8))),
    }


EPSILON = 1e-05
HIGHEST = lax.Precision.HIGHEST

@jax.custom_vjp
def low(v):
    return lax.optimization_barrier(v.astype(jnp.bfloat16)).astype(jnp.float32)

@jax.custom_vjp
def low_back(v):
    return v

def low_keep(v):
    return (low(v), None)

def low_pass(kept, grad):
    return (grad,)

def back_keep(v):
    return (v, None)

def back_low(kept, grad):
    return (low(grad),)
low.defvjp(low_keep, low_pass)
low_back.defvjp(back_keep, back_low)

def seq_tables(bucket, slot_length):
    lengths = slot_length // 4 * jnp.left_shift(jnp.ones_like(bucket), bucket)
    lengths = lengths[:, None, None]
    places = jnp.arange(slot_length, dtype=jnp.int32)
    row_index = places[None, :, None]
    col_index = places[None, None, :]
    together = row_index // lengths == col_index // lengths
    phases = row_index % lengths * (col_index % lengths) % lengths
    length_float = lengths.astype(jnp.float32)
    angles = phases.astype(jnp.float32) * (2.0 * math.pi) / length_float
    scaling = lax.rsqrt(length_float)
    cosine = jnp.where(together, jnp.cos(angles) * scaling, 0.0)
    sine = jnp.where(together, jnp.sin(angles) * scaling, 0.0)
    return (cosine, sine)

def hid_tables(first_row, row_count, width):
    row_index = first_row + jnp.arange(row_count, dtype=jnp.int32)[:, None]
    col_index = jnp.arange(width, dtype=jnp.int32)[None, :]
    phases = row_index * col_index % width
    angles = phases.astype(jnp.float32) * (2.0 * math.pi) / width
    scaling = 1.0 / math.sqrt(width)
    return (jnp.cos(angles) * scaling, jnp.sin(angles) * scaling)

def layer_norm(residual, gain, shift):
    means = lax.optimization_barrier(jnp.mean(residual, axis=1, keepdims=True))
    centered = residual - means
    spread = lax.optimization_barrier(jnp.mean(centered * centered, axis=1, keepdims=True))
    return centered * lax.rsqrt(spread + EPSILON) * gain + shift

def forward(block_x, w_in, b_in, w_out, b_out, gain_one, shift_one, gain_two, shift_two, cos_seq, sin_seq, cos_hid, sin_hid):
    seq_cos = low(low_back(jnp.einsum('sjk,skd->sjd', cos_seq, block_x, precision=HIGHEST)))
    seq_sin = low(low_back(jnp.einsum('sjk,skd->sjd', sin_seq, block_x, precision=HIGHEST)))
    row_total = block_x.shape[0] * block_x.shape[1]
    seq_cos = seq_cos.reshape(row_total, -1)
    seq_sin = seq_sin.reshape(row_total, -1)
    mixing = jnp.dot(seq_cos, cos_hid, precision=HIGHEST) - jnp.dot(seq_sin, sin_hid, precision=HIGHEST)
    mixing = low_back(mixing)
    hidden_one = layer_norm(block_x.reshape(row_total, -1) + mixing, gain_one, shift_one)
    pre_act = low_back(jnp.dot(low(hidden_one), w_in, precision=HIGHEST) + b_in)
    activation = low(jax.nn.gelu(pre_act, approximate=False))
    ffn_out = low_back(jnp.dot(activation, w_out, precision=HIGHEST) + b_out)
    return layer_norm(hidden_one + ffn_out, gain_two, shift_two)

def reference(tokens, bucket, w_in, b_in, w_out, b_out, gain_one, shift_one, gain_two, shift_two, mask, labels, cotangent):
    group_slots = 1
    for attempt in range(16):
        if group_slots * 2 * SLOT_LEN <= 4096 and SLOTS % (group_slots * 2) == 0:
            group_slots = group_slots * 2
    groups = SLOTS // group_slots
    group_rows = group_slots * SLOT_LEN
    weights = tuple((parameter.astype(jnp.float32) for parameter in (w_in, b_in, w_out, b_out, gain_one, shift_one, gain_two, shift_two)))
    cos_hid, sin_hid = hid_tables(0, D, D)
    cos_hid = low(cos_hid)
    sin_hid = low(sin_hid)
    inputs_all = jnp.transpose(tokens.astype(jnp.float32)).reshape(groups, group_slots, SLOT_LEN, D)
    upstream_all = jnp.transpose(cotangent.astype(jnp.float32)).reshape(groups, group_rows, D)
    buckets_all = bucket.reshape(groups, group_slots)
    masks_all = mask.reshape(groups, group_rows)
    labels_all = labels.reshape(groups, group_rows)

    def one_group(carry, item):
        grads, total_hits = carry
        block_x, block_up, block_bucket, block_mask, block_labels = item
        cos_seq, sin_seq = seq_tables(block_bucket, SLOT_LEN)
        cos_seq = low(cos_seq)
        sin_seq = low(sin_seq)

        def run_block(inputs_x, *params):
            return forward(inputs_x, *params, cos_seq, sin_seq, cos_hid, sin_hid)
        result, pullback = jax.vjp(run_block, block_x, *weights)
        backward = pullback(block_up)
        grads = tuple((total + extra for total, extra in zip(grads, backward[1:])))
        picked = jnp.take_along_axis(result, block_labels[:, None], axis=1)[:, 0]
        total_hits = total_hits + jnp.sum(jnp.where(block_mask == 1, jax.nn.sigmoid(2.0 * picked), 0.0))
        return ((grads, total_hits), (result.astype(jnp.bfloat16), backward[0].reshape(group_rows, D)))
    start_state = (tuple((jnp.zeros_like(parameter) for parameter in weights)), jnp.zeros((), jnp.float32))
    (grads, total_hits), (results, input_grads) = lax.scan(one_group, start_state, (inputs_all, upstream_all, buckets_all, masks_all, labels_all))
    return (jnp.transpose(results.reshape(TOKENS, D)), jnp.transpose(input_grads.reshape(TOKENS, D)), grads[0], grads[1], grads[2], grads[3], grads[4], grads[5], grads[6], grads[7], total_hits * 8.0 / TOKENS)
```

```python
import math

import jax
import jax.numpy as jnp
import numpy as np
from jax import lax
from jax.sharding import PartitionSpec as P

EPSILON = 1e-05


def dft_pair(length):
    places = np.arange(length)
    angles = (places[:, None] * places[None, :] % length) * (2.0 * math.pi / length)
    scale = 1.0 / math.sqrt(length)
    return (np.cos(angles) * scale).astype(np.float32), (np.sin(angles) * scale).astype(np.float32)


def seq_tables(slot_length):
    cosines, sines = [], []
    for bucket in range(3):
        length = slot_length // 4 << bucket
        cosine, sine = dft_pair(length)
        copies = np.eye(slot_length // length, dtype=np.float32)
        cosines.append(np.kron(copies, cosine))
        sines.append(np.kron(copies, sine))
    return (
        jnp.asarray(np.stack(cosines), jnp.bfloat16),
        jnp.asarray(np.stack(sines), jnp.bfloat16),
    )


def dot(left, right, left_dim, right_dim):
    return lax.dot_general(
        left,
        right,
        (((left_dim,), (right_dim,)), ((), ())),
        preferred_element_type=jnp.float32,
    )


def shift_pairs(shards, step):
    return [(i, (i + step) % shards) for i in range(shards)]


def to_tokens(local, me, shards):
    width, tokens = local.shape
    chunk = tokens // shards
    whole = jnp.zeros((width * shards, chunk), local.dtype)
    for step in range(shards):
        target = (me + step) % shards
        piece = lax.dynamic_slice(local, (0, target * chunk), (width, chunk))
        if step:
            piece = lax.ppermute(piece, "mp", shift_pairs(shards, step))
        source = (me - step) % shards
        whole = lax.dynamic_update_slice(whole, piece, (source * width, 0))
    return whole


def to_features(whole, me, shards):
    full, chunk = whole.shape
    width = full // shards
    local = jnp.zeros((width, chunk * shards), whole.dtype)
    for step in range(shards):
        target = (me + step) % shards
        piece = lax.dynamic_slice(whole, (target * width, 0), (width, chunk))
        if step:
            piece = lax.ppermute(piece, "mp", shift_pairs(shards, step))
        source = (me - step) % shards
        local = lax.dynamic_update_slice(local, piece, (0, source * chunk))
    return local


def norm(residual, gain, shift):
    means = jnp.mean(residual, axis=0)
    centered = residual - means[None, :]
    inverse = lax.rsqrt(jnp.mean(centered * centered, axis=0) + EPSILON)
    normed = centered * inverse[None, :]
    return normed * gain[:, None] + shift[:, None], normed, inverse


def norm_back(upstream, normed, inverse, gain):
    scaled = upstream * gain[:, None]
    first = jnp.mean(scaled, axis=0)
    second = jnp.mean(scaled * normed, axis=0)
    grad = inverse[None, :] * (scaled - first[None, :] - normed * second[None, :])
    return grad, jnp.sum(upstream * normed, axis=1), jnp.sum(upstream, axis=1)


def gelu_exact(values):
    return jax.nn.gelu(values, approximate=False)


def body(
    tokens,
    bucket,
    w_in,
    b_in,
    w_out,
    b_out,
    gain_one,
    shift_one,
    gain_two,
    shift_two,
    mask,
    labels,
    cotangent,
):
    shards = lax.axis_size("mp")
    groups = lax.axis_size("dp")
    me = lax.axis_index("mp")
    mine = lax.axis_index("dp")
    local_width, token_count = tokens.shape
    width = local_width * shards
    units = w_in.shape[1]
    chunk = token_count // shards
    slot_length = token_count // bucket.shape[0]
    slots = chunk // slot_length

    small = jnp.concatenate([b_in, b_out, gain_one, shift_one, gain_two, shift_two])
    small = lax.all_gather(small, "mp")
    b_in_all = small[:, :units].reshape(-1)
    b_out, gain_one, shift_one, gain_two, shift_two = [
        small[:, units + i * local_width : units + (i + 1) * local_width].reshape(-1)
        for i in range(5)
    ]

    x_low = to_tokens(tokens, me, shards)
    cot_in, x_low = lax.optimization_barrier((cotangent, x_low))

    pair = jnp.concatenate([w_in, w_out.T], axis=0)
    part = pair.shape[0] // groups
    own = lax.dynamic_slice(pair, (mine * part, 0), (part, units))
    own = lax.all_gather(own, "mp")
    pair_all = lax.all_gather(own, "dp")

    cos_tables, sin_tables = seq_tables(slot_length)
    my_buckets = lax.dynamic_slice(bucket, (me * slots,), (slots,))
    cos_hid, sin_hid = (jnp.asarray(t, jnp.bfloat16) for t in dft_pair(width))

    seq_cos, seq_sin, tables = [], [], []
    for slot in range(slots):
        cosine = lax.dynamic_index_in_dim(cos_tables, my_buckets[slot], 0, False)
        sine = lax.dynamic_index_in_dim(sin_tables, my_buckets[slot], 0, False)
        cosine, sine = lax.optimization_barrier((cosine, sine))
        tables.append((cosine, sine))
        block = x_low[:, slot * slot_length : (slot + 1) * slot_length]
        seq_cos.append(dot(block, cosine, 1, 0).astype(jnp.bfloat16))
        seq_sin.append(dot(block, sine, 1, 0).astype(jnp.bfloat16))
    seq_cos = jnp.concatenate(seq_cos, axis=1)
    seq_sin = jnp.concatenate(seq_sin, axis=1)
    mixing = dot(cos_hid, seq_cos, 0, 0) - dot(sin_hid, seq_sin, 0, 0)
    first_res = x_low.astype(jnp.float32) + mixing
    hidden_one, normed_one, inverse_one = norm(first_res, gain_one, shift_one)
    hidden_low = hidden_one.astype(jnp.bfloat16)

    pair_all = pair_all.transpose(1, 0, 2, 3).reshape(shards, 2, width, units)
    win_all = pair_all[:, 0]
    wout_all = pair_all[:, 1]
    acts, pulls = [], []
    ffn_out = b_out[:, None]
    for s in range(shards):
        pre = dot(win_all[s], hidden_low, 0, 0) + b_in_all[s * units : (s + 1) * units, None]
        act, pull = jax.vjp(gelu_exact, pre)
        act = act.astype(jnp.bfloat16)
        acts.append(act)
        pulls.append(pull)
        ffn_out = ffn_out + dot(wout_all[s], act, 1, 0)
    second_res = hidden_one + ffn_out
    result, normed_two, inverse_two = norm(second_res, gain_two, shift_two)

    my_labels = lax.dynamic_slice(labels, (me * chunk,), (chunk,))
    my_mask = lax.dynamic_slice(mask, (me * chunk,), (chunk,))
    chosen = jnp.arange(width, dtype=jnp.int32)[:, None] == my_labels[None, :]
    picked = jnp.sum(jnp.where(chosen, result, 0.0), axis=0)
    own_hits = jnp.sum(jnp.where(my_mask == 1, jax.nn.sigmoid(2.0 * picked), 0.0))

    cot_low = to_tokens(cot_in, me, shards)
    upstream = cot_low.astype(jnp.float32)
    grad_two, d_gain_two, d_shift_two = norm_back(upstream, normed_two, inverse_two, gain_two)
    ffn_grad = grad_two.astype(jnp.bfloat16)
    d_b_out = jnp.sum(ffn_grad.astype(jnp.float32), axis=1)
    out_low, ffn_grad = lax.optimization_barrier((result.astype(jnp.bfloat16), ffn_grad))
    output = to_features(out_low, me, shards)

    grad_hidden = grad_two
    d_b_in, d_w_in, d_w_out = [], [], []
    for s in range(shards):
        grad_act = dot(wout_all[s], ffn_grad, 0, 0)
        grad_pre = pulls[s](grad_act)[0].astype(jnp.bfloat16)
        d_b_in.append(jnp.sum(grad_pre.astype(jnp.float32), axis=1))
        d_w_out.append(dot(acts[s], ffn_grad, 1, 1))
        d_w_in.append(dot(hidden_low, grad_pre, 1, 1))
        grad_hidden = grad_hidden + dot(win_all[s], grad_pre, 1, 0)
    grad_one, d_gain_one, d_shift_one = norm_back(grad_hidden, normed_one, inverse_one, gain_one)
    mix_grad = grad_one.astype(jnp.bfloat16)
    grad_cos = dot(cos_hid, mix_grad, 0, 0).astype(jnp.bfloat16)
    grad_sin = -dot(sin_hid, mix_grad, 0, 0).astype(jnp.bfloat16)
    back = []
    for slot in range(slots):
        cosine, sine = tables[slot]
        columns = slice(slot * slot_length, (slot + 1) * slot_length)
        back.append(dot(grad_cos[:, columns], cosine, 1, 0) + dot(grad_sin[:, columns], sine, 1, 0))
    d_x = (grad_one + jnp.concatenate(back, axis=1)).astype(jnp.bfloat16)
    d_tokens = to_features(d_x, me, shards).astype(jnp.float32)

    grads = jnp.concatenate([jnp.stack(d_w_in), jnp.stack(d_w_out)], axis=1)
    grads = lax.psum_scatter(grads.astype(jnp.bfloat16), "dp", scatter_dimension=1, tiled=True)
    grads = lax.psum_scatter(grads.astype(jnp.float32), "mp", scatter_dimension=0, tiled=True)
    grads = lax.all_gather(grads[0], "dp", axis=0, tiled=True)
    d_w_in = grads[:width]
    d_w_out = grads[width:]

    sums = jnp.concatenate(
        d_b_in + [d_b_out, d_gain_one, d_shift_one, d_gain_two, d_shift_two, own_hits[None]]
    )
    sums = lax.psum(sums, ("dp", "mp"))
    d_b_in = lax.dynamic_slice(sums, (me * units,), (units,))
    rest = [
        lax.dynamic_slice(sums, (shards * units + i * width + me * local_width,), (local_width,))
        for i in range(5)
    ]
    score = sums[-1] * 8.0 / (token_count * groups)
    return (output, d_tokens, d_w_in, d_b_in, d_w_out, *rest, score)


def solution(mesh):
    in_specs = (
        P("mp", "dp"),
        P("dp"),
        P(None, "mp"),
        P("mp"),
        P("mp", None),
        P("mp"),
        P("mp"),
        P("mp"),
        P("mp"),
        P("mp"),
        P("dp"),
        P("dp"),
        P("mp", "dp"),
    )
    out_specs = (
        P("mp", "dp"),
        P("mp", "dp"),
        P(None, "mp"),
        P("mp"),
        P("mp", None),
        P("mp"),
        P("mp"),
        P("mp"),
        P("mp"),
        P("mp"),
        P(),
    )
    return jax.shard_map(body, mesh=mesh, in_specs=in_specs, out_specs=out_specs, check_vma=False)
```

```python
import functools
import math

import jax
import jax.numpy as jnp
import numpy as np
from jax import lax
from jax.experimental import pallas as pl
from jax.experimental.pallas import tpu as pltpu
from jax.sharding import PartitionSpec as P

EPSILON = 1e-05
BF = jnp.bfloat16
F32 = jnp.float32
ANY = pl.BlockSpec(memory_space=pl.ANY)
VMEM = pl.BlockSpec(memory_space=pltpu.VMEM)
SMEM = pl.BlockSpec(memory_space=pltpu.SMEM)
VMEM_LIMIT = 66_000_000


def dft_pair(length):
    places = np.arange(length)
    angles = (places[:, None] * places[None, :] % length) * (2.0 * math.pi / length)
    scale = 1.0 / math.sqrt(length)
    return (np.cos(angles) * scale).astype(np.float32), (np.sin(angles) * scale).astype(np.float32)


def seq_tables(slot_length):
    cosines, sines = [], []
    for bucket in range(3):
        length = slot_length // 4 << bucket
        cosine, sine = dft_pair(length)
        copies = np.eye(slot_length // length, dtype=np.float32)
        cosines.append(np.kron(copies, cosine))
        sines.append(np.kron(copies, sine))
    return jnp.asarray(np.stack(cosines), BF), jnp.asarray(np.stack(sines), BF)


def dot(left, right, left_dim=1, right_dim=0):
    return lax.dot_general(
        left, right, (((left_dim,), (right_dim,)), ((), ())), preferred_element_type=F32
    )


def remote(source, target, send_sem, recv_sem, device):
    return pltpu.make_async_remote_copy(
        src_ref=source,
        dst_ref=target,
        send_sem=send_sem,
        recv_sem=recv_sem,
        device_id=device,
        device_id_type=pl.DeviceIdType.MESH,
    )


def greet(peers):
    barrier = pltpu.get_barrier_semaphore()
    for peer in peers:
        pl.semaphore_signal(barrier, inc=1, device_id=peer, device_id_type=pl.DeviceIdType.MESH)
    pl.semaphore_wait(barrier, len(peers))


def lanes(values):
    return sum(values[:, i : i + 128] for i in range(128, values.shape[1], 128)) + values[:, :128]


def layer_kernel(
    shards,
    groups,
    tok,
    cot,
    w_in,
    w_out,
    small,
    bucket,
    labels,
    mask,
    cos_seq,
    sin_seq,
    cos_hid,
    sin_hid,
    out,
    dx,
    d_w,
    sums,
    x_all,
    c_all,
    w_all,
    small_all,
    cos_tab,
    sin_tab,
    cos_h,
    sin_h,
    n_one,
    inv_one,
    hid,
    act,
    slope,
    n_two,
    inv_two,
    grad,
    seq_c,
    seq_s,
    vecs,
    bias,
    acc,
    bias_acc,
    hits,
    stage,
    load_sem,
    own_sem,
    tok_send,
    tok_recv,
    cot_send,
    cot_recv,
    small_send,
    small_recv,
    wz_send,
    wz_recv,
    wp_send,
    wp_recv,
    ws_send,
    ws_recv,
    out_send,
    out_recv,
    dx_send,
    dx_recv,
    stage_sem,
):
    me = lax.axis_index("mp")
    group = lax.axis_index("dp")
    width_local = tok.shape[0]
    width = width_local * shards
    units = w_in.shape[1]
    chunk = tok.shape[1] // shards
    slot_length = cos_seq.shape[1]
    slots = chunk // slot_length
    part = 2 * width // groups
    chips = groups // 2
    rows = min(256, width)
    cols = min(256, slot_length)
    ring = range(1, shards)
    others = range(1, chips)

    def mp_peer(step):
        return lax.rem(me + step, shards)

    def dp_peer(step):
        return lax.rem(group + 2 * step, groups)

    sibling = {"dp": group + 1 - 2 * lax.rem(group, 2)}
    greet(
        [{"mp": mp_peer(d)} for d in ring] + [{"dp": dp_peer(k)} for k in others] + [sibling]
    )

    own_w = [
        pltpu.make_async_copy(w_in, w_all.at[0, :width], own_sem.at[0]),
        pltpu.make_async_copy(w_out, w_all.at[0, width:], own_sem.at[1]),
    ]
    my_cols = pl.ds(pl.multiple_of(me * chunk, 128), chunk)
    my_rows = pl.ds(pl.multiple_of(me * width_local, 16), width_local)
    loads = [
        pltpu.make_async_copy(source, target, load_sem.at[i])
        for i, (source, target) in enumerate(
            [
                (small, small_all.at[0]),
                (cos_seq, cos_tab),
                (sin_seq, sin_tab),
                (cos_hid, cos_h),
                (sin_hid, sin_h),
                (tok.at[:, my_cols], x_all.at[my_rows]),
                (cot.at[:, my_cols], c_all.at[my_rows]),
            ]
        )
    ]
    for copy in own_w + loads:
        copy.start()

    def exchange(source, target, send, recv):
        copies = []
        for d in ring:
            peer = mp_peer(d)
            copies.append(
                remote(
                    source.at[:, pl.ds(pl.multiple_of(peer * chunk, 128), chunk)],
                    target.at[my_rows],
                    send.at[d],
                    recv.at[d],
                    {"mp": peer},
                )
            )
        return copies

    small_copies = [
        remote(
            small,
            small_all.at[shards - d],
            small_send.at[d],
            small_recv.at[d],
            {"mp": mp_peer(d)},
        )
        for d in ring
    ]
    for copy in small_copies:
        copy.start()
    for copy in own_w:
        copy.wait()
    my_part = pl.ds(pl.multiple_of(group * part, 16), part)
    wz = [
        remote(
            w_all.at[0, my_part],
            w_all.at[shards - d, my_part],
            wz_send.at[d],
            wz_recv.at[d],
            {"mp": mp_peer(d)},
        )
        for d in ring
    ]
    for copy in wz:
        copy.start()
    tok_copies = exchange(tok, x_all, tok_send, tok_recv)
    for copy in tok_copies:
        copy.start()

    for copy in loads:
        copy.wait()
    for copy in small_copies:
        copy.wait_recv()
    for r in range(shards):
        shard = lax.rem(me + r, shards)
        at = pl.ds(pl.multiple_of(shard * width_local, 8), width_local)
        bias[r] = jnp.broadcast_to(small_all[r, 0:1, :units], (128, units)).T
        for i in range(5):
            line = small_all[r, i + 1 : i + 2, : (width_local + 127) // 128 * 128]
            vecs[i, at] = jnp.broadcast_to(line, (128, line.shape[1])).T[:width_local]

    for copy in wz:
        copy.wait_recv()

    def weights_from(who):
        return w_all.at[pl.ds(1, shards - 1), pl.ds(pl.multiple_of(who * part, 16), part)]

    wp = [
        remote(
            weights_from(group),
            weights_from(group),
            wp_send.at[k],
            wp_recv.at[k],
            {"dp": dp_peer(k)},
        )
        for k in others
    ]
    ws = [
        remote(
            weights_from(lax.rem(group + groups - 2 * k, groups)),
            weights_from(lax.rem(group + groups - 2 * k, groups)),
            ws_send.at[k],
            ws_recv.at[k],
            sibling,
        )
        for k in range(chips)
    ]
    for copy in wp:
        copy.start()
    ws[0].start()
    for copy in tok_copies:
        copy.wait_recv()
    cot_copies = exchange(cot, c_all, cot_send, cot_recv)
    for copy in cot_copies:
        copy.start()

    @pl.loop(0, slots)
    def _(slot):
        at = pl.ds(pl.multiple_of(slot * slot_length, 128), slot_length)
        which = bucket[me * slots + slot]
        seq_c[...] = dot(x_all[:, at], cos_tab[which]).astype(BF)
        seq_s[...] = dot(x_all[:, at], sin_tab[which]).astype(BF)

        @pl.loop(0, width // rows)
        def _(i):
            row = pl.ds(pl.multiple_of(i * rows, rows), rows)
            mixing = dot(cos_h[row], seq_c[...]) - dot(sin_h[row], seq_s[...])
            n_one[row, at] = x_all[row, at].astype(F32) + mixing

        @pl.loop(0, slot_length // 128)
        def _(i):
            col = pl.ds(pl.multiple_of(slot * slot_length + i * 128, 128), 128)
            value = n_one[:, col]
            centered = value - jnp.mean(value, axis=0, keepdims=True)
            inverse = lax.rsqrt(jnp.mean(centered * centered, axis=0, keepdims=True) + EPSILON)
            normed = centered * inverse
            n_one[:, col] = normed
            inv_one[:, col] = inverse
            hid[:, col] = (normed * vecs[1] + vecs[2]).astype(BF)

    for k in others:
        wp[k - 1].wait_recv()
        ws[k].start()

    def first_matmul(r):
        @pl.loop(0, units // rows)
        def _(i):
            row = pl.ds(pl.multiple_of(i * rows, rows), rows)
            pre = dot(w_all[r, pl.ds(0, width), row], hid[...], 0, 0) + bias[r, row, 0:1]
            cdf = 0.5 + 0.5 * lax.erf(pre * (1.0 / math.sqrt(2.0)))
            pdf = jnp.exp(-0.5 * pre * pre) * (1.0 / math.sqrt(2.0 * math.pi))
            act[r, row] = (pre * cdf).astype(BF)
            slope[r, row] = (cdf + pre * pdf).astype(BF)

    first_matmul(0)
    for copy in ws:
        copy.wait_recv()
    pl.loop(1, shards)(first_matmul)

    hits[...] = jnp.zeros_like(hits)
    acc[...] = jnp.zeros_like(acc)

    @pl.loop(0, chunk // cols)
    def _(i):
        col = pl.ds(pl.multiple_of(i * cols, cols), cols)
        second = n_one[:, col] * vecs[1, :, 0:1] + vecs[2, :, 0:1] + vecs[0, :, 0:1]
        total = dot(w_all[0, pl.ds(width, units)], act[0, :, col], 0, 0)
        for r in ring:
            total += dot(w_all[r, pl.ds(width, units)], act[r, :, col], 0, 0)
        second += total
        centered = second - jnp.mean(second, axis=0, keepdims=True)
        inverse = lax.rsqrt(jnp.mean(centered * centered, axis=0, keepdims=True) + EPSILON)
        normed = centered * inverse
        n_two[:, col] = normed
        inv_two[:, col] = inverse
        result = normed * vecs[3, :, 0:1] + vecs[4, :, 0:1]
        x_all[:, col] = result.astype(BF)
        feature = lax.broadcasted_iota(jnp.int32, (width, cols), 0)
        chosen = feature == labels[pl.ds(me, 1), col]
        picked = jnp.sum(jnp.where(chosen, result, 0.0), axis=0, keepdims=True)
        soft = 1.0 / (1.0 + jnp.exp(-2.0 * picked))
        hits[...] += jnp.where(mask[pl.ds(me, 1), col] == 1, soft, 0.0)

    def send_back(source, target, send, recv, first, length):
        copies = []
        for d in ring:
            peer = mp_peer(d)
            copies.append(
                remote(
                    source.at[
                        pl.ds(pl.multiple_of(peer * width_local, 16), width_local),
                        pl.ds(first, length),
                    ],
                    target.at[:, pl.ds(pl.multiple_of(me * chunk + first, 128), length)],
                    send.at[d],
                    recv.at[d],
                    {"mp": peer},
                )
            )
        return copies

    out_copies = send_back(x_all, out, out_send, out_recv, 0, chunk)
    out_own = pltpu.make_async_copy(x_all.at[my_rows], out.at[:, my_cols], own_sem.at[0])
    for copy in out_copies + [out_own]:
        copy.start()

    for copy in cot_copies:
        copy.wait_recv()

    @pl.loop(0, chunk // cols)
    def _(i):
        col = pl.ds(pl.multiple_of(i * cols, cols), cols)
        upstream = c_all[:, col].astype(F32)
        normed = n_two[:, col]
        scaled = upstream * vecs[3, :, 0:1]
        first = jnp.mean(scaled, axis=0, keepdims=True)
        both = jnp.mean(scaled * normed, axis=0, keepdims=True)
        grad_two = inv_two[:, col] * (scaled - first - normed * both)
        n_two[:, col] = grad_two
        low = grad_two.astype(BF)
        grad[:, col] = low
        acc[0] += lanes(low.astype(F32))
        acc[3] += lanes(upstream * normed)
        acc[4] += lanes(upstream)

    @pl.loop(0, shards)
    def _(r):
        @pl.loop(0, units // rows)
        def _(i):
            row = pl.ds(pl.multiple_of(i * rows, rows), rows)
            grad_act = dot(w_all[r, pl.ds(pl.multiple_of(width + i * rows, rows), rows)], grad[...])
            low = (grad_act * slope[r, row].astype(F32)).astype(BF)
            slope[r, row] = low
            bias_acc[r, row] = lanes(low.astype(F32))

    @pl.loop(0, chunk // cols)
    def _(i):
        col = pl.ds(pl.multiple_of(i * cols, cols), cols)
        total = dot(w_all[0, pl.ds(0, width)], slope[0, :, col])
        for r in ring:
            total += dot(w_all[r, pl.ds(0, width)], slope[r, :, col])
        upstream = n_two[:, col] + total
        normed = n_one[:, col]
        scaled = upstream * vecs[1, :, 0:1]
        first = jnp.mean(scaled, axis=0, keepdims=True)
        both = jnp.mean(scaled * normed, axis=0, keepdims=True)
        grad_one = inv_one[:, col] * (scaled - first - normed * both)
        n_two[:, col] = grad_one
        c_all[:, col] = grad_one.astype(BF)
        acc[1] += lanes(upstream * normed)
        acc[2] += lanes(upstream)

    dx_copies = []
    for slot in range(slots):
        at = pl.ds(slot * slot_length, slot_length)
        which = bucket[me * slots + slot]

        @pl.loop(0, width // rows)
        def _(i):
            row = pl.ds(pl.multiple_of(i * rows, rows), rows)
            seq_c[row] = dot(cos_h[row], c_all[:, at]).astype(BF)
            seq_s[row] = -dot(sin_h[row], c_all[:, at]).astype(BF)

        @pl.loop(0, width // rows)
        def _(i):
            row = pl.ds(pl.multiple_of(i * rows, rows), rows)
            back = dot(seq_c[row], cos_tab[which]) + dot(seq_s[row], sin_tab[which])
            c_all[row, at] = (n_two[row, at] + back).astype(BF)

        copies = send_back(
            c_all, dx, dx_send.at[slot], dx_recv.at[slot], slot * slot_length, slot_length
        )
        copies.append(
            pltpu.make_async_copy(
                c_all.at[my_rows, at],
                dx.at[
                    :,
                    pl.ds(pl.multiple_of(me * chunk + slot * slot_length, 128), slot_length),
                ],
                own_sem.at[1 + slot],
            )
        )
        for copy in copies:
            copy.start()
        dx_copies += copies

    def put(r, half):
        return pltpu.make_async_copy(stage.at[half], d_w.at[r, half], stage_sem.at[half])

    @pl.loop(0, shards)
    def _(r):
        @pl.when(r > 0)
        def _():
            put(r, 0).wait()

        @pl.loop(0, width // rows)
        def _(i):
            row = pl.ds(pl.multiple_of(i * rows, rows), rows)
            stage[0, row] = dot(hid[row], slope[r], 1, 1).astype(BF)

        put(r, 0).start()

        @pl.when(r > 0)
        def _():
            put(r, 1).wait()

        @pl.loop(0, units // rows)
        def _(i):
            row = pl.ds(pl.multiple_of(i * rows, rows), rows)
            stage[1, row] = dot(act[r, row], grad[...], 1, 1).astype(BF)

        put(r, 1).start()

    put(0, 0).wait()
    put(0, 1).wait()

    lane = lax.broadcasted_iota(jnp.int32, (width_local, 128), 1)
    total_hits = jnp.sum(hits[...], axis=1, keepdims=True)
    for r in range(shards):
        shard = lax.rem(me + r, shards)
        at = pl.ds(pl.multiple_of(shard * width_local, 8), width_local)
        sums[r, 0:1] = jnp.broadcast_to(
            jnp.sum(bias_acc[r], axis=1, keepdims=True), (units, 128)
        ).T[0:1]
        line = jnp.where(lane == 6, total_hits, 0.0)
        for i in range(5):
            line += jnp.where(lane == i + 1, jnp.sum(acc[i, at], axis=1, keepdims=True), 0.0)
        spare = (-width_local) % 128
        if spare:
            line = jnp.concatenate([line, jnp.zeros((spare, 128), F32)], axis=0)
        sums[r, 1:8, : width_local + spare] = line.T[1:8]
        sums[r, 1:8, width_local + spare :] = jnp.zeros((7, units - width_local - spare), F32)

    for copy in small_copies + wz + wp + ws + tok_copies + cot_copies:
        copy.wait_send()
    for copy in out_copies + [out_own] + dx_copies:
        copy.wait()


def layer_call(shards, groups, tok, cot, w_in, w_out, small, bucket, labels, mask):
    width_local, tokens = tok.shape
    width = width_local * shards
    units = w_in.shape[1]
    chunk = tokens // shards
    slot_length = tokens // bucket.shape[0]
    slots = chunk // slot_length
    cols = min(256, slot_length)
    cos_seq, sin_seq = seq_tables(slot_length)
    cos_hid, sin_hid = (jnp.asarray(t, BF) for t in dft_pair(width))
    dma = pltpu.SemaphoreType.DMA
    chips = groups // 2
    return pl.pallas_call(
        functools.partial(layer_kernel, shards, groups),
        out_shape=[
            jax.ShapeDtypeStruct((width_local, tokens), BF),
            jax.ShapeDtypeStruct((width_local, tokens), BF),
            jax.ShapeDtypeStruct((shards, 2, width, units), BF),
            jax.ShapeDtypeStruct((shards, 8, units), F32),
        ],
        in_specs=[ANY] * 5 + [SMEM, VMEM, VMEM] + [ANY] * 4,
        out_specs=[ANY, ANY, ANY, VMEM],
        scratch_shapes=[
            pltpu.VMEM((width, chunk), BF),
            pltpu.VMEM((width, chunk), BF),
            pltpu.VMEM((shards, 2 * width, units), BF),
            pltpu.VMEM((shards, 8, units), F32),
            pltpu.VMEM((3, slot_length, slot_length), BF),
            pltpu.VMEM((3, slot_length, slot_length), BF),
            pltpu.VMEM((width, width), BF),
            pltpu.VMEM((width, width), BF),
            pltpu.VMEM((width, chunk), F32),
            pltpu.VMEM((1, chunk), F32),
            pltpu.VMEM((width, chunk), BF),
            pltpu.VMEM((shards, units, chunk), BF),
            pltpu.VMEM((shards, units, chunk), BF),
            pltpu.VMEM((width, chunk), F32),
            pltpu.VMEM((1, chunk), F32),
            pltpu.VMEM((width, chunk), BF),
            pltpu.VMEM((width, slot_length), BF),
            pltpu.VMEM((width, slot_length), BF),
            pltpu.VMEM((5, width, 128), F32),
            pltpu.VMEM((shards, units, 128), F32),
            pltpu.VMEM((5, width, 128), F32),
            pltpu.VMEM((shards, units, 128), F32),
            pltpu.VMEM((1, cols), F32),
            pltpu.VMEM((2, width, units), BF),
            dma((7,)),
            dma((1 + slots,)),
        ]
        + [dma((shards,))] * 8
        + [dma((chips,))] * 4
        + [dma((shards,))] * 2
        + [dma((slots, shards))] * 2
        + [dma((2,))],
        compiler_params=pltpu.CompilerParams(
            collective_id=0, has_side_effects=True, vmem_limit_bytes=VMEM_LIMIT
        ),
        name="layer",
    )(tok, cot, w_in, w_out, small, bucket, labels, mask, cos_seq, sin_seq, cos_hid, sin_hid)


def body(
    tokens,
    bucket,
    w_in,
    b_in,
    w_out,
    b_out,
    gain_one,
    shift_one,
    gain_two,
    shift_two,
    mask,
    labels,
    cotangent,
):
    shards = lax.axis_size("mp")
    groups = lax.axis_size("dp")
    width_local, token_count = tokens.shape
    width = width_local * shards
    units = w_in.shape[1]
    vectors = jnp.stack([b_out, gain_one, shift_one, gain_two, shift_two])
    small = jnp.concatenate(
        [b_in[None, :], jnp.pad(vectors, ((0, 2), (0, units - width_local)))], axis=0
    )
    output, d_x, grads, sums = layer_call(
        shards,
        groups,
        tokens,
        cotangent,
        w_in,
        w_out,
        small,
        bucket,
        labels.reshape(shards, -1),
        mask.reshape(shards, -1),
    )
    d_tokens = d_x.astype(F32)
    me = lax.axis_index("mp")
    grads = jnp.roll(grads, me, axis=0).reshape(shards, 2 * width, units)
    grads = lax.psum_scatter(grads, "dp", scatter_dimension=1, tiled=True)
    grads = lax.psum_scatter(grads.astype(F32), "mp", scatter_dimension=0, tiled=True)
    grads = lax.all_gather(grads[0], "dp", axis=0, tiled=True)
    sums = lax.psum(jnp.roll(sums, me, axis=0), ("dp", "mp"))
    sums = lax.dynamic_index_in_dim(sums, me, 0, False)
    rest = [sums[i + 1, :width_local] for i in range(5)]
    score = sums[6, 0] * 8.0 / (token_count * groups)
    return (output, d_tokens, grads[:width], sums[0], grads[width:], *rest, score)


def solution(mesh):
    in_specs = (
        P("mp", "dp"),
        P("dp"),
        P(None, "mp"),
        P("mp"),
        P("mp", None),
        P("mp"),
        P("mp"),
        P("mp"),
        P("mp"),
        P("mp"),
        P("dp"),
        P("dp"),
        P("mp", "dp"),
    )
    out_specs = (
        P("mp", "dp"),
        P("mp", "dp"),
        P(None, "mp"),
        P("mp"),
        P("mp", None),
        P("mp"),
        P("mp"),
        P("mp"),
        P("mp"),
        P("mp"),
        P(),
    )
    return jax.shard_map(body, mesh=mesh, in_specs=in_specs, out_specs=out_specs, check_vma=False)
```

```python
import functools
import math

import jax
import jax.numpy as jnp
import numpy as np
from jax import lax
from jax.experimental import pallas as pl
from jax.experimental.pallas import tpu as pltpu
from jax.sharding import PartitionSpec as P

EPSILON = 1e-05
BF = jnp.bfloat16
F32 = jnp.float32
ANY = pl.BlockSpec(memory_space=pl.ANY)
VMEM = pl.BlockSpec(memory_space=pltpu.VMEM)
SMEM = pl.BlockSpec(memory_space=pltpu.SMEM)
VMEM_LIMIT = 66_000_000


def dft_pair(length):
    places = np.arange(length)
    angles = (places[:, None] * places[None, :] % length) * (2.0 * math.pi / length)
    scale = 1.0 / math.sqrt(length)
    return (np.cos(angles) * scale).astype(np.float32), (np.sin(angles) * scale).astype(np.float32)


def seq_tables(slot_length):
    cosines, sines = [], []
    for bucket in range(3):
        length = slot_length // 4 << bucket
        cosine, sine = dft_pair(length)
        copies = np.eye(slot_length // length, dtype=np.float32)
        cosines.append(np.kron(copies, cosine))
        sines.append(np.kron(copies, sine))
    return jnp.asarray(np.stack(cosines), BF), jnp.asarray(np.stack(sines), BF)


def dot(left, right, left_dim=1, right_dim=0):
    return lax.dot_general(
        left, right, (((left_dim,), (right_dim,)), ((), ())), preferred_element_type=F32
    )


def remote(source, target, send_sem, recv_sem, device):
    return pltpu.make_async_remote_copy(
        src_ref=source,
        dst_ref=target,
        send_sem=send_sem,
        recv_sem=recv_sem,
        device_id=device,
        device_id_type=pl.DeviceIdType.MESH,
    )


def greet(peers):
    barrier = pltpu.get_barrier_semaphore()
    for peer in peers:
        pl.semaphore_signal(barrier, inc=1, device_id=peer, device_id_type=pl.DeviceIdType.MESH)
    pl.semaphore_wait(barrier, len(peers))


def lanes(values):
    return sum(values[:, i : i + 128] for i in range(128, values.shape[1], 128)) + values[:, :128]


def layer_kernel(
    shards,
    groups,
    tok,
    cot,
    w_in,
    w_out,
    small,
    bucket,
    labels,
    mask,
    cos_seq,
    sin_seq,
    cos_hid,
    sin_hid,
    out,
    dx,
    d_w,
    sums,
    x_all,
    c_all,
    w_all,
    small_all,
    cos_tab,
    sin_tab,
    cos_h,
    sin_h,
    n_one,
    inv_one,
    hid,
    act,
    slope,
    n_two,
    inv_two,
    grad,
    seq_c,
    seq_s,
    vecs,
    bias,
    acc,
    hits,
    near,
    far,
    part_low,
    line_in,
    own_part,
    done_low,
    sums_own,
    sums_mp,
    sums_mid,
    sums_dp,
    load_sem,
    own_sem,
    tok_send,
    tok_recv,
    cot_send,
    cot_recv,
    small_send,
    small_recv,
    wz_send,
    wz_recv,
    wp_send,
    wp_recv,
    ws_send,
    ws_recv,
    out_send,
    out_recv,
    dx_send,
    dx_recv,
    near_send,
    near_recv,
    far_send,
    far_recv,
    line_send,
    line_recv,
    done_send,
    done_recv,
    share_send,
    share_recv,
    mp_send,
    mp_recv,
    dp_send,
    dp_recv,
):
    me = lax.axis_index("mp")
    group = lax.axis_index("dp")
    width_local = tok.shape[0]
    width = width_local * shards
    units = w_in.shape[1]
    chunk = tok.shape[1] // shards
    slot_length = cos_seq.shape[1]
    slots = chunk // slot_length
    part = 2 * width // groups
    chips = groups // 2
    rows = min(256, width)
    cols = min(256, slot_length)
    ring = range(1, shards)
    others = range(1, chips)

    def mp_peer(step):
        return lax.rem(me + step, shards)

    def dp_peer(step):
        return lax.rem(group + 2 * step, groups)

    core = lax.rem(group, 2)
    sibling = {"dp": group + 1 - 2 * core}
    plane = [{"dp": lax.rem(group + q, groups)} for q in range(1, groups)]
    greet([{"mp": mp_peer(d)} for d in ring] + plane)

    own_w = [
        pltpu.make_async_copy(w_in, w_all.at[0, :width], own_sem.at[0]),
        pltpu.make_async_copy(w_out, w_all.at[0, width:], own_sem.at[1]),
    ]
    my_cols = pl.ds(pl.multiple_of(me * chunk, 128), chunk)
    my_rows = pl.ds(pl.multiple_of(me * width_local, 16), width_local)
    loads = [
        pltpu.make_async_copy(source, target, load_sem.at[i])
        for i, (source, target) in enumerate(
            [
                (small, small_all.at[0]),
                (cos_seq, cos_tab),
                (sin_seq, sin_tab),
                (cos_hid, cos_h),
                (sin_hid, sin_h),
                (tok.at[:, my_cols], x_all.at[my_rows]),
                (cot.at[:, my_cols], c_all.at[my_rows]),
            ]
        )
    ]
    for copy in own_w + loads:
        copy.start()

    def exchange(source, target, send, recv):
        copies = []
        for d in ring:
            peer = mp_peer(d)
            copies.append(
                remote(
                    source.at[:, pl.ds(pl.multiple_of(peer * chunk, 128), chunk)],
                    target.at[my_rows],
                    send.at[d],
                    recv.at[d],
                    {"mp": peer},
                )
            )
        return copies

    small_copies = [
        remote(
            small,
            small_all.at[shards - d],
            small_send.at[d],
            small_recv.at[d],
            {"mp": mp_peer(d)},
        )
        for d in ring
    ]
    for copy in small_copies:
        copy.start()
    for copy in own_w:
        copy.wait()
    my_part = pl.ds(pl.multiple_of(group * part, 16), part)
    wz = [
        remote(
            w_all.at[0, my_part],
            w_all.at[shards - d, my_part],
            wz_send.at[d],
            wz_recv.at[d],
            {"mp": mp_peer(d)},
        )
        for d in ring
    ]
    for copy in wz:
        copy.start()
    tok_copies = exchange(tok, x_all, tok_send, tok_recv)
    for copy in tok_copies:
        copy.start()

    for copy in loads:
        copy.wait()
    for copy in small_copies:
        copy.wait_recv()
    for r in range(shards):
        shard = lax.rem(me + r, shards)
        at = pl.ds(pl.multiple_of(shard * width_local, 8), width_local)
        bias[r] = jnp.broadcast_to(small_all[r, 0:1, :units], (128, units)).T
        for i in range(5):
            line = small_all[r, i + 1 : i + 2, : (width_local + 127) // 128 * 128]
            vecs[i, at] = jnp.broadcast_to(line, (128, line.shape[1])).T[:width_local]

    for copy in wz:
        copy.wait_recv()

    def weights_from(who):
        return w_all.at[pl.ds(1, shards - 1), pl.ds(pl.multiple_of(who * part, 16), part)]

    wp = [
        remote(
            weights_from(group),
            weights_from(group),
            wp_send.at[k],
            wp_recv.at[k],
            {"dp": dp_peer(k)},
        )
        for k in others
    ]
    ws = [
        remote(
            weights_from(lax.rem(group + groups - 2 * k, groups)),
            weights_from(lax.rem(group + groups - 2 * k, groups)),
            ws_send.at[k],
            ws_recv.at[k],
            sibling,
        )
        for k in range(chips)
    ]
    for copy in wp:
        copy.start()
    ws[0].start()
    for copy in tok_copies:
        copy.wait_recv()
    cot_copies = exchange(cot, c_all, cot_send, cot_recv)
    for copy in cot_copies:
        copy.start()

    @pl.loop(0, slots)
    def _(slot):
        at = pl.ds(pl.multiple_of(slot * slot_length, 128), slot_length)
        which = bucket[me * slots + slot]
        seq_c[...] = dot(x_all[:, at], cos_tab[which]).astype(BF)
        seq_s[...] = dot(x_all[:, at], sin_tab[which]).astype(BF)

        @pl.loop(0, width // rows)
        def _(i):
            row = pl.ds(pl.multiple_of(i * rows, rows), rows)
            mixing = dot(cos_h[row], seq_c[...]) - dot(sin_h[row], seq_s[...])
            n_one[row, at] = x_all[row, at].astype(F32) + mixing

        @pl.loop(0, slot_length // 128)
        def _(i):
            col = pl.ds(pl.multiple_of(slot * slot_length + i * 128, 128), 128)
            value = n_one[:, col]
            centered = value - jnp.mean(value, axis=0, keepdims=True)
            inverse = lax.rsqrt(jnp.mean(centered * centered, axis=0, keepdims=True) + EPSILON)
            normed = centered * inverse
            n_one[:, col] = normed
            inv_one[:, col] = inverse
            hid[:, col] = (normed * vecs[1] + vecs[2]).astype(BF)

    for k in others:
        wp[k - 1].wait_recv()
        ws[k].start()

    def first_matmul(r):
        @pl.loop(0, units // rows)
        def _(i):
            row = pl.ds(pl.multiple_of(i * rows, rows), rows)
            pre = dot(w_all[r, pl.ds(0, width), row], hid[...], 0, 0) + bias[r, row, 0:1]
            cdf = 0.5 + 0.5 * lax.erf(pre * (1.0 / math.sqrt(2.0)))
            pdf = jnp.exp(-0.5 * pre * pre) * (1.0 / math.sqrt(2.0 * math.pi))
            act[r, row] = (pre * cdf).astype(BF)
            slope[r, row] = (cdf + pre * pdf).astype(BF)

    first_matmul(0)
    for copy in ws:
        copy.wait_recv()
    pl.loop(1, shards)(first_matmul)

    hits[...] = jnp.zeros_like(hits)
    acc[...] = jnp.zeros_like(acc)

    @pl.loop(0, chunk // cols)
    def _(i):
        col = pl.ds(pl.multiple_of(i * cols, cols), cols)
        second = n_one[:, col] * vecs[1, :, 0:1] + vecs[2, :, 0:1] + vecs[0, :, 0:1]
        total = dot(w_all[0, pl.ds(width, units)], act[0, :, col], 0, 0)
        for r in ring:
            total += dot(w_all[r, pl.ds(width, units)], act[r, :, col], 0, 0)
        second += total
        centered = second - jnp.mean(second, axis=0, keepdims=True)
        inverse = lax.rsqrt(jnp.mean(centered * centered, axis=0, keepdims=True) + EPSILON)
        normed = centered * inverse
        n_two[:, col] = normed
        inv_two[:, col] = inverse
        result = normed * vecs[3, :, 0:1] + vecs[4, :, 0:1]
        x_all[:, col] = result.astype(BF)
        feature = lax.broadcasted_iota(jnp.int32, (width, cols), 0)
        chosen = feature == labels[pl.ds(me, 1), col]
        picked = jnp.sum(jnp.where(chosen, result, 0.0), axis=0, keepdims=True)
        soft = 1.0 / (1.0 + jnp.exp(-2.0 * picked))
        hits[...] += jnp.where(mask[pl.ds(me, 1), col] == 1, soft, 0.0)

    def send_back(source, target, send, recv, first, length):
        copies = []
        for d in ring:
            peer = mp_peer(d)
            copies.append(
                remote(
                    source.at[
                        pl.ds(pl.multiple_of(peer * width_local, 16), width_local),
                        pl.ds(first, length),
                    ],
                    target.at[:, pl.ds(pl.multiple_of(me * chunk + first, 128), length)],
                    send.at[d],
                    recv.at[d],
                    {"mp": peer},
                )
            )
        return copies

    out_copies = send_back(x_all, out, out_send, out_recv, 0, chunk)
    out_own = pltpu.make_async_copy(x_all.at[my_rows], out.at[:, my_cols], own_sem.at[0])
    for copy in out_copies + [out_own]:
        copy.start()

    for copy in cot_copies:
        copy.wait_recv()

    @pl.loop(0, chunk // cols)
    def _(i):
        col = pl.ds(pl.multiple_of(i * cols, cols), cols)
        upstream = c_all[:, col].astype(F32)
        normed = n_two[:, col]
        scaled = upstream * vecs[3, :, 0:1]
        first = jnp.mean(scaled, axis=0, keepdims=True)
        both = jnp.mean(scaled * normed, axis=0, keepdims=True)
        grad_two = inv_two[:, col] * (scaled - first - normed * both)
        n_two[:, col] = grad_two
        low = grad_two.astype(BF)
        grad[:, col] = low
        acc[0] += lanes(low.astype(F32))
        acc[3] += lanes(upstream * normed)
        acc[4] += lanes(upstream)

    half = width // 2
    split = 1 if half // chips % 16 == 0 else 2
    piece_rows = half * split // chips
    piece_cols = width // split
    keep = pl.ds(pl.multiple_of(core * half, 16), half)
    give = pl.ds(pl.multiple_of((1 - core) * half, 16), half)

    def piece(who):
        chip = who // 2
        first = core * half + chip // split * piece_rows
        return (
            pl.ds(pl.multiple_of(first, 16), piece_rows),
            pl.ds(pl.multiple_of(lax.rem(chip, split) * piece_cols, 128), piece_cols),
        )

    d_out = act.at[:, :, pl.ds(0, width)]
    d_in = w_all.at[:, pl.ds(0, width)]

    def near_copy(x, r):
        source = (d_in, d_out)[x]
        return remote(
            source.at[r, give], near.at[x, r], near_send.at[x, r], near_recv.at[x, r], sibling
        )

    def add_near(x):
        source = (d_in, d_out)[x]

        @pl.loop(0, shards)
        def _(r):
            near_copy(x, r).wait_recv()
            source[r, keep] = (source[r, keep].astype(F32) + near[x, r].astype(F32)).astype(BF)

        copies = []
        for k in others:
            at, across = piece(dp_peer(k))
            copies.append(
                remote(
                    source.at[:, at, across],
                    far.at[x, k - 1],
                    far_send.at[x, k],
                    far_recv.at[x, k],
                    {"dp": dp_peer(k)},
                )
            )
        for copy in copies:
            copy.start()
        return copies

    my_at, my_across = piece(group)

    def add_far(x, copies):
        source = (d_in, d_out)[x]
        for copy in copies:
            copy.wait_recv()

        @pl.loop(0, shards)
        def _(r):
            total = source[r, my_at, my_across].astype(F32)
            for k in others:
                total += far[x, k - 1, r].astype(F32)
            part_low[x, r] = total.astype(BF)

            @pl.when(r == 0)
            def _():
                own_part[x] = total

        copies = [
            remote(
                part_low.at[x, d],
                line_in.at[x, d - 1],
                line_send.at[x, d],
                line_recv.at[x, d],
                {"mp": mp_peer(d)},
            )
            for d in ring
        ]
        for copy in copies:
            copy.start()
        return copies

    def add_line(x, copies):
        for copy in copies:
            copy.wait_recv()
        total = own_part[x]
        for d in ring:
            total += line_in[x, d - 1].astype(F32)
        done_low[x] = total.astype(BF)
        target = d_w.at[x, my_at, my_across]
        copies = [
            remote(
                done_low.at[x], target, done_send.at[x, k], done_recv.at[x, k], {"dp": dp_peer(k)}
            )
            for k in others
        ]
        own = pltpu.make_async_copy(done_low.at[x], target, own_sem.at[1 + slots + x])
        for copy in copies + [own]:
            copy.start()
        return copies, own

    def share(x, copies, own):
        own.wait()
        for copy in copies:
            copy.wait_recv()
        copy = remote(
            d_w.at[x, keep], d_w.at[x, keep], share_send.at[x], share_recv.at[x], sibling
        )
        copy.start()
        return copy

    @pl.loop(0, shards)
    def _(r):
        @pl.loop(0, units // rows)
        def _(i):
            row = pl.ds(pl.multiple_of(i * rows, rows), rows)
            d_out[r, row] = dot(act[r, row], grad[...], 1, 1).astype(BF)

        near_copy(1, r).start()

    @pl.loop(0, shards)
    def _(r):
        @pl.loop(0, units // rows)
        def _(i):
            row = pl.ds(pl.multiple_of(i * rows, rows), rows)
            grad_act = dot(w_all[r, pl.ds(pl.multiple_of(width + i * rows, rows), rows)], grad[...])
            low = (grad_act * slope[r, row].astype(F32)).astype(BF)
            slope[r, row] = low
            bias[r, row] = lanes(low.astype(F32))

    far_out = add_near(1)

    @pl.loop(0, chunk // cols)
    def _(i):
        col = pl.ds(pl.multiple_of(i * cols, cols), cols)
        total = dot(w_all[0, pl.ds(0, width)], slope[0, :, col])
        for r in ring:
            total += dot(w_all[r, pl.ds(0, width)], slope[r, :, col])
        upstream = n_two[:, col] + total
        normed = n_one[:, col]
        scaled = upstream * vecs[1, :, 0:1]
        first = jnp.mean(scaled, axis=0, keepdims=True)
        both = jnp.mean(scaled * normed, axis=0, keepdims=True)
        grad_one = inv_one[:, col] * (scaled - first - normed * both)
        n_two[:, col] = grad_one
        c_all[:, col] = grad_one.astype(BF)
        acc[1] += lanes(upstream * normed)
        acc[2] += lanes(upstream)

    dx_copies = []
    for slot in range(slots):
        at = pl.ds(slot * slot_length, slot_length)
        which = bucket[me * slots + slot]

        @pl.loop(0, width // rows)
        def _(i):
            row = pl.ds(pl.multiple_of(i * rows, rows), rows)
            seq_c[row] = dot(cos_h[row], c_all[:, at]).astype(BF)
            seq_s[row] = -dot(sin_h[row], c_all[:, at]).astype(BF)

        @pl.loop(0, width // rows)
        def _(i):
            row = pl.ds(pl.multiple_of(i * rows, rows), rows)
            back = dot(seq_c[row], cos_tab[which]) + dot(seq_s[row], sin_tab[which])
            c_all[row, at] = (n_two[row, at] + back).astype(BF)

        copies = send_back(
            c_all, dx, dx_send.at[slot], dx_recv.at[slot], slot * slot_length, slot_length
        )
        copies.append(
            pltpu.make_async_copy(
                c_all.at[my_rows, at],
                dx.at[
                    :,
                    pl.ds(pl.multiple_of(me * chunk + slot * slot_length, 128), slot_length),
                ],
                own_sem.at[1 + slot],
            )
        )
        for copy in copies:
            copy.start()
        dx_copies += copies

    lane = lax.broadcasted_iota(jnp.int32, (width_local, 128), 1)
    total_hits = jnp.sum(hits[...], axis=1, keepdims=True)
    for r in range(shards):
        shard = lax.rem(me + r, shards)
        at = pl.ds(pl.multiple_of(shard * width_local, 8), width_local)
        sums_own[r, 0:1] = jnp.broadcast_to(
            jnp.sum(bias[r], axis=1, keepdims=True), (units, 128)
        ).T[0:1]
        line = jnp.where(lane == 6, total_hits, 0.0)
        for i in range(5):
            line += jnp.where(lane == i + 1, jnp.sum(acc[i, at], axis=1, keepdims=True), 0.0)
        spare = (-width_local) % 128
        if spare:
            line = jnp.concatenate([line, jnp.zeros((spare, 128), F32)], axis=0)
        sums_own[r, 1:8, : width_local + spare] = line.T[1:8]
        sums_own[r, 1:8, width_local + spare :] = jnp.zeros((7, units - width_local - spare), F32)
    mp_sums = [
        remote(sums_own.at[d], sums_mp.at[me], mp_send.at[d], mp_recv.at[d], {"mp": mp_peer(d)})
        for d in ring
    ]
    for copy in mp_sums:
        copy.start()
    sums_mp[me] = sums_own[0]

    for copy in wz + wp + ws:
        copy.wait_send()

    @pl.loop(0, shards)
    def _(r):
        @pl.loop(0, width // rows)
        def _(i):
            row = pl.ds(pl.multiple_of(i * rows, rows), rows)
            d_in[r, row] = dot(hid[row], slope[r], 1, 1).astype(BF)

        near_copy(0, r).start()

    line_out = add_far(1, far_out)
    far_in = add_near(0)
    for copy in mp_sums:
        copy.wait_recv()
    sums_mid[...] = sum(sums_mp[s] for s in range(shards))
    dp_sums = [
        remote(sums_mid, sums_dp.at[group], dp_send.at[q], dp_recv.at[q], peer)
        for q, peer in enumerate(plane)
    ]
    for copy in dp_sums:
        copy.start()
    sums_dp[group] = sums_mid[...]
    done_out, own_out = add_line(1, line_out)
    line_from_in = add_far(0, far_in)
    share_out = share(1, done_out, own_out)
    for copy in dp_sums:
        copy.wait_recv()
    sums[...] = sum(sums_dp[q] for q in range(groups))
    done_in, own_in = add_line(0, line_from_in)
    share_in = share(0, done_in, own_in)

    @pl.loop(0, shards)
    def _(r):
        near_copy(0, r).wait_send()
        near_copy(1, r).wait_send()

    for copy in small_copies + tok_copies + cot_copies + mp_sums + dp_sums:
        copy.wait_send()
    for copy in far_out + far_in + line_out + line_from_in + done_out + done_in:
        copy.wait_send()
    for copy in out_copies + [out_own] + dx_copies + [share_out, share_in]:
        copy.wait()


def layer_call(shards, groups, tok, cot, w_in, w_out, small, bucket, labels, mask):
    width_local, tokens = tok.shape
    width = width_local * shards
    units = w_in.shape[1]
    chunk = tokens // shards
    slot_length = tokens // bucket.shape[0]
    slots = chunk // slot_length
    cols = min(256, slot_length)
    cos_seq, sin_seq = seq_tables(slot_length)
    cos_hid, sin_hid = (jnp.asarray(t, BF) for t in dft_pair(width))
    dma = pltpu.SemaphoreType.DMA
    chips = groups // 2
    split = 1 if width // 2 // chips % 16 == 0 else 2
    piece = (width // 2 * split // chips, width // split)
    return pl.pallas_call(
        functools.partial(layer_kernel, shards, groups),
        out_shape=[
            jax.ShapeDtypeStruct((width_local, tokens), BF),
            jax.ShapeDtypeStruct((width_local, tokens), BF),
            jax.ShapeDtypeStruct((2, width, units), BF),
            jax.ShapeDtypeStruct((8, units), F32),
        ],
        in_specs=[ANY] * 5 + [SMEM, VMEM, VMEM] + [ANY] * 4,
        out_specs=[ANY, ANY, ANY, VMEM],
        scratch_shapes=[
            pltpu.VMEM((width, chunk), BF),
            pltpu.VMEM((width, chunk), BF),
            pltpu.VMEM((shards, 2 * width, units), BF),
            pltpu.VMEM((shards, 8, units), F32),
            pltpu.VMEM((3, slot_length, slot_length), BF),
            pltpu.VMEM((3, slot_length, slot_length), BF),
            pltpu.VMEM((width, width), BF),
            pltpu.VMEM((width, width), BF),
            pltpu.VMEM((width, chunk), F32),
            pltpu.VMEM((1, chunk), F32),
            pltpu.VMEM((width, chunk), BF),
            pltpu.VMEM((shards, units, chunk), BF),
            pltpu.VMEM((shards, units, chunk), BF),
            pltpu.VMEM((width, chunk), F32),
            pltpu.VMEM((1, chunk), F32),
            pltpu.VMEM((width, chunk), BF),
            pltpu.VMEM((width, slot_length), BF),
            pltpu.VMEM((width, slot_length), BF),
            pltpu.VMEM((5, width, 128), F32),
            pltpu.VMEM((shards, units, 128), F32),
            pltpu.VMEM((5, width, 128), F32),
            pltpu.VMEM((1, cols), F32),
            pltpu.VMEM((2, shards, width // 2, width), BF),
            pltpu.VMEM((2, chips - 1, shards) + piece, BF),
            pltpu.VMEM((2, shards) + piece, BF),
            pltpu.VMEM((2, shards - 1) + piece, BF),
            pltpu.VMEM((2,) + piece, F32),
            pltpu.VMEM((2,) + piece, BF),
            pltpu.VMEM((shards, 8, units), F32),
            pltpu.VMEM((shards, 8, units), F32),
            pltpu.VMEM((8, units), F32),
            pltpu.VMEM((groups, 8, units), F32),
            dma((7,)),
            dma((3 + slots,)),
        ]
        + [dma((shards,))] * 8
        + [dma((chips,))] * 4
        + [dma((shards,))] * 2
        + [dma((slots, shards))] * 2
        + [dma((2, shards))] * 2
        + [dma((2, chips))] * 2
        + [dma((2, shards))] * 2
        + [dma((2, chips))] * 2
        + [dma((2,))] * 2
        + [dma((shards,))] * 2
        + [dma((groups,))] * 2,
        compiler_params=pltpu.CompilerParams(
            collective_id=0, has_side_effects=True, vmem_limit_bytes=VMEM_LIMIT
        ),
        name="layer",
    )(tok, cot, w_in, w_out, small, bucket, labels, mask, cos_seq, sin_seq, cos_hid, sin_hid)


def body(
    tokens,
    bucket,
    w_in,
    b_in,
    w_out,
    b_out,
    gain_one,
    shift_one,
    gain_two,
    shift_two,
    mask,
    labels,
    cotangent,
):
    shards = lax.axis_size("mp")
    groups = lax.axis_size("dp")
    width_local, token_count = tokens.shape
    units = w_in.shape[1]
    vectors = jnp.stack([b_out, gain_one, shift_one, gain_two, shift_two])
    small = jnp.concatenate(
        [b_in[None, :], jnp.pad(vectors, ((0, 2), (0, units - width_local)))], axis=0
    )
    output, d_x, grads, sums = layer_call(
        shards,
        groups,
        tokens,
        cotangent,
        w_in,
        w_out,
        small,
        bucket,
        labels.reshape(shards, -1),
        mask.reshape(shards, -1),
    )
    d_tokens = d_x.astype(F32)
    grads = grads.astype(F32)
    rest = [sums[i + 1, :width_local] for i in range(5)]
    score = sums[6, 0] * 8.0 / (token_count * groups)
    return (output, d_tokens, grads[0], sums[0], grads[1], *rest, score)


def solution(mesh):
    in_specs = (
        P("mp", "dp"),
        P("dp"),
        P(None, "mp"),
        P("mp"),
        P("mp", None),
        P("mp"),
        P("mp"),
        P("mp"),
        P("mp"),
        P("mp"),
        P("dp"),
        P("dp"),
        P("mp", "dp"),
    )
    out_specs = (
        P("mp", "dp"),
        P("mp", "dp"),
        P(None, "mp"),
        P("mp"),
        P("mp", None),
        P("mp"),
        P("mp"),
        P("mp"),
        P("mp"),
        P("mp"),
        P(),
    )
    return jax.shard_map(body, mesh=mesh, in_specs=in_specs, out_specs=out_specs, check_vma=False)
```

```python
import functools
import math

import jax
import jax.numpy as jnp
from jax import lax
from jax.experimental import pallas as pl
from jax.experimental.pallas import tpu as pltpu
from jax.sharding import PartitionSpec as P

EPSILON = 1e-05
BF = jnp.bfloat16
F32 = jnp.float32
ANY = pl.BlockSpec(memory_space=pl.ANY)
VMEM = pl.BlockSpec(memory_space=pltpu.VMEM)
SMEM = pl.BlockSpec(memory_space=pltpu.SMEM)
VMEM_LIMIT = 66_000_000


def turns(phase):
    quarter = jnp.floor(phase * 4.0 + 0.5)
    angle = (phase - quarter * 0.25) * (2.0 * math.pi)
    square = angle * angle
    cosine = 1.0 + square * (
        -1 / 2 + square * (1 / 24 + square * (-1 / 720 + square * (1 / 40320)))
    )
    sine = angle * (
        1.0
        + square * (-1 / 6 + square * (1 / 120 + square * (-1 / 5040 + square * (1 / 362880))))
    )
    odd = (quarter == 1.0) | (quarter == 3.0)
    first = jnp.where(odd, sine, cosine)
    second = jnp.where(odd, cosine, sine)
    return (
        jnp.where((quarter == 1.0) | (quarter == 2.0), -first, first),
        jnp.where((quarter == 2.0) | (quarter == 3.0), -second, second),
    )


def dot(left, right, left_dim=1, right_dim=0):
    return lax.dot_general(
        left, right, (((left_dim,), (right_dim,)), ((), ())), preferred_element_type=F32
    )


def remote(source, target, send_sem, recv_sem, device):
    return pltpu.make_async_remote_copy(
        src_ref=source,
        dst_ref=target,
        send_sem=send_sem,
        recv_sem=recv_sem,
        device_id=device,
        device_id_type=pl.DeviceIdType.MESH,
    )


def greet(peers):
    barrier = pltpu.get_barrier_semaphore()
    for peer in peers:
        pl.semaphore_signal(barrier, inc=1, device_id=peer, device_id_type=pl.DeviceIdType.MESH)
    pl.semaphore_wait(barrier, len(peers))


def lanes(values):
    return sum(values[:, i : i + 128] for i in range(128, values.shape[1], 128)) + values[:, :128]


def layer_kernel(
    shards,
    groups,
    tok,
    cot,
    w_in,
    w_out,
    small,
    bucket,
    labels,
    mask,
    out,
    dx,
    d_w,
    sums,
    x_all,
    c_all,
    w_all,
    small_all,
    cos_tab,
    sin_tab,
    cos_h,
    sin_h,
    n_one,
    inv_one,
    hid,
    act,
    slope,
    n_two,
    inv_two,
    grad,
    seq_c,
    seq_s,
    vecs,
    bias,
    acc,
    hits,
    near,
    far,
    part_low,
    line_in,
    own_part,
    done_low,
    sums_own,
    sums_mp,
    sums_mid,
    sums_dp,
    load_sem,
    own_sem,
    tok_send,
    tok_recv,
    cot_send,
    cot_recv,
    small_send,
    small_recv,
    wz_send,
    wz_recv,
    wp_send,
    wp_recv,
    ws_send,
    ws_recv,
    out_send,
    out_recv,
    dx_send,
    dx_recv,
    near_send,
    near_recv,
    far_send,
    far_recv,
    line_send,
    line_recv,
    done_send,
    done_recv,
    share_send,
    share_recv,
    mp_send,
    mp_recv,
    dp_send,
    dp_recv,
):
    me = lax.axis_index("mp")
    group = lax.axis_index("dp")
    width_local = tok.shape[0]
    width = width_local * shards
    units = w_in.shape[1]
    chunk = tok.shape[1] // shards
    slots = cos_tab.shape[0]
    slot_length = chunk // slots
    part = 2 * width // groups
    chips = groups // 2
    rows = min(256, width)
    cols = min(256, slot_length)
    ring = range(1, shards)
    others = range(1, chips)

    inner = jnp.where(me < shards // 2, 1, -1)
    at_end = (me == 0) | (me == shards - 1)

    def mp_peer(step):
        return lax.rem(me + step, shards)

    def inward(step):
        return lax.rem(me + step * inner + shards, shards)

    def dp_peer(step):
        return lax.rem(group + 2 * step, groups)

    core = lax.rem(group, 2)
    sibling = {"dp": group + 1 - 2 * core}
    plane = [{"dp": lax.rem(group + q, groups)} for q in range(1, groups)]
    greet([{"mp": mp_peer(d)} for d in ring] + plane)

    own_w = [
        pltpu.make_async_copy(w_in, w_all.at[0, :width], own_sem.at[0]),
        pltpu.make_async_copy(w_out, w_all.at[0, width:], own_sem.at[1]),
    ]
    my_cols = pl.ds(pl.multiple_of(me * chunk, 128), chunk)
    my_rows = pl.ds(pl.multiple_of(me * width_local, 16), width_local)
    loads = [
        pltpu.make_async_copy(source, target, load_sem.at[i])
        for i, (source, target) in enumerate(
            [
                (small, small_all.at[0]),
                (tok.at[:, my_cols], x_all.at[my_rows]),
                (cot.at[:, my_cols], c_all.at[my_rows]),
            ]
        )
    ]
    for copy in own_w + loads:
        copy.start()

    def exchange(source, target, send, recv, slot, steps=(1, 2, 3)):
        copies = []
        for step in steps:
            peer = inward(step)
            d = lax.rem(peer - me + shards, shards)
            first = pl.multiple_of(peer * chunk + slot * slot_length, 128)
            copies.append(
                remote(
                    source.at[:, pl.ds(first, slot_length)],
                    target.at[
                        my_rows, pl.ds(pl.multiple_of(slot * slot_length, 128), slot_length)
                    ],
                    send.at[slot, d],
                    recv.at[slot, d],
                    {"mp": peer},
                )
            )
        return copies

    small_copies = [
        remote(
            small,
            small_all.at[shards - d],
            small_send.at[d],
            small_recv.at[d],
            {"mp": mp_peer(d)},
        )
        for d in ring
    ]
    for copy in small_copies:
        copy.start()
    for copy in own_w:
        copy.wait()
    my_part = pl.ds(pl.multiple_of(group * part, 16), part)

    def weight_copy(shard, target, send):
        place = lax.rem(shard - me + 2 * shards, shards)
        there = lax.rem(shard - target + 2 * shards, shards)
        return remote(
            w_all.at[place, my_part],
            w_all.at[there, my_part],
            wz_send.at[send],
            wz_recv.at[there],
            {"mp": target},
        )

    def weight_wait(place):
        remote(
            w_all.at[0, my_part],
            w_all.at[place, my_part],
            wz_send.at[0],
            wz_recv.at[place],
            {"mp": inward(1)},
        ).wait_recv()

    near_step = jnp.where(at_end, 1, 3)
    far_step = jnp.where(at_end, 2, 1)
    wz = [weight_copy(me, inward(far_step), 0), weight_copy(me, inward(near_step), 1)]
    for copy in wz:
        copy.start()
    for slot in range(slots):
        for copy in exchange(tok, x_all, tok_send, tok_recv, slot, (1, 2)):
            copy.start()

    def pass_on(step, send):
        return weight_copy(inward(step), inward(3), send)

    @pl.when(jnp.logical_not(at_end))
    def _():
        for step, send in ((1, 2), (2, 3)):
            weight_wait(lax.rem(step * inner + shards, shards))
            pass_on(step, send).start()

    for slot in range(slots):
        for copy in exchange(tok, x_all, tok_send, tok_recv, slot, (3,)):
            copy.start()

    @pl.when(at_end)
    def _():
        for place in (1, 2, 3):
            weight_wait(place)

    @pl.when(jnp.logical_not(at_end))
    def _():
        weight_wait(lax.rem(3 * inner + shards, shards))

    side = math.isqrt(chips)
    chip_x, chip_y = lax.rem(group // 2, side), group // 2 // side
    halves = (pl.ds(0, units // 2), pl.ds(units // 2, units // 2))

    def at_chip(x, y):
        return (lax.rem(y + side, side) * side + lax.rem(x + side, side)) * 2 + core

    def weights_of(who, across):
        rows_of = pl.ds(pl.multiple_of(who * part, 16), part)
        return w_all.at[pl.ds(1, shards - 1), rows_of, across]

    def plane_copy(who, across, to, sem):
        return remote(
            weights_of(who, across), weights_of(who, across), wp_send.at[sem], wp_recv.at[sem], to
        )

    first_plane, second_plane = [], []
    for h, across in enumerate(halves):
        for a in range(1, side):
            along = (a, 0) if h == 0 else (0, a)
            first_plane.append(
                (
                    plane_copy(
                        group,
                        across,
                        {"dp": at_chip(chip_x + along[0], chip_y + along[1])},
                        h * chips + a,
                    ),
                    at_chip(chip_x - along[0], chip_y - along[1]),
                    across,
                )
            )
            for b in range(side):
                source = at_chip(chip_x + b, chip_y) if h == 0 else at_chip(chip_x, chip_y + b)
                to = at_chip(chip_x, chip_y + a) if h == 0 else at_chip(chip_x + a, chip_y)
                back = (
                    at_chip(chip_x + b, chip_y - a) if h == 0 else at_chip(chip_x - a, chip_y + b)
                )
                second_plane.append(
                    (
                        plane_copy(source, across, {"dp": to}, h * chips + side * a + b),
                        back,
                        across,
                    )
                )

    def to_sibling(who, across, sem):
        return remote(
            weights_of(who, across),
            weights_of(who, across),
            ws_send.at[sem],
            ws_recv.at[sem],
            sibling,
        )

    ws = [to_sibling(group, pl.ds(0, units), 0)]
    for n, (_, who, across) in enumerate(first_plane + second_plane):
        ws.append(to_sibling(who, across, n + 1))
    for copy, _, _ in first_plane:
        copy.start()
    ws[0].start()

    turn_rows = min(64, slot_length)

    @pl.loop(0, width // turn_rows)
    def _(i):
        row = pl.ds(pl.multiple_of(i * turn_rows, 16), turn_rows)
        shape = (turn_rows, width)
        product = (
            (lax.broadcasted_iota(jnp.int32, shape, 0) + i * turn_rows)
            * lax.broadcasted_iota(jnp.int32, shape, 1)
        ).astype(F32)
        phase = product * (1.0 / width)
        phase = (product - jnp.floor(phase) * width) * (1.0 / width)
        cosine, sine = turns(phase)
        cos_h[row] = (cosine * (1.0 / math.sqrt(width))).astype(BF)
        sin_h[row] = (sine * (1.0 / math.sqrt(width))).astype(BF)

    @pl.loop(0, slots * slot_length // turn_rows)
    def _(i):
        slot = i // (slot_length // turn_rows)
        first = lax.rem(i, slot_length // turn_rows) * turn_rows
        row = pl.ds(pl.multiple_of(first, 16), turn_rows)
        shape = (turn_rows, slot_length)
        which = bucket[me * slots + slot]
        length = jnp.where(which == 0, slot_length // 4, slot_length // 2)
        length = jnp.where(which == 2, slot_length, length)
        at = lax.broadcasted_iota(jnp.int32, shape, 0) + first
        to = lax.broadcasted_iota(jnp.int32, shape, 1)
        inner = length - 1
        phase = ((at & inner) * (to & inner)) & inner
        scale = jnp.full((1, 1), length, jnp.int32).astype(F32)
        cosine, sine = turns(phase.astype(F32) / scale)
        scale = jnp.where((at ^ to) < length, lax.rsqrt(scale), 0.0)
        cos_tab[slot, row] = (cosine * scale).astype(BF)
        sin_tab[slot, row] = (sine * scale).astype(BF)


    for copy in loads:
        copy.wait()
    for copy in small_copies:
        copy.wait_recv()
    for r in range(shards):
        shard = lax.rem(me + r, shards)
        at = pl.ds(pl.multiple_of(shard * width_local, 8), width_local)
        bias[r] = jnp.broadcast_to(small_all[r, 0:1, :units], (128, units)).T
        for i in range(5):
            line = small_all[r, i + 1 : i + 2, : (width_local + 127) // 128 * 128]
            vecs[i, at] = jnp.broadcast_to(line, (128, line.shape[1])).T[:width_local]

    for n, (copy, _, _) in enumerate(first_plane):
        copy.wait_recv()
        ws[n + 1].start()
    for copy, _, _ in second_plane:
        copy.start()

    @pl.loop(0, slots)
    def _(slot):
        at = pl.ds(pl.multiple_of(slot * slot_length, 128), slot_length)
        for copy in exchange(tok, x_all, tok_send, tok_recv, slot):
            copy.wait_recv()

        @pl.when(slot == slots - 1)
        def _():
            for later in range(slots):
                for copy in exchange(cot, c_all, cot_send, cot_recv, later):
                    copy.start()

        seq_c[...] = dot(x_all[:, at], cos_tab[slot]).astype(BF)
        seq_s[...] = dot(x_all[:, at], sin_tab[slot]).astype(BF)

        @pl.loop(0, width // rows)
        def _(i):
            row = pl.ds(pl.multiple_of(i * rows, rows), rows)
            mixing = dot(cos_h[row], seq_c[...]) - dot(sin_h[row], seq_s[...])
            n_one[row, at] = x_all[row, at].astype(F32) + mixing

        @pl.loop(0, slot_length // 128)
        def _(i):
            col = pl.ds(pl.multiple_of(slot * slot_length + i * 128, 128), 128)
            value = n_one[:, col]
            centered = value - jnp.mean(value, axis=0, keepdims=True)
            inverse = lax.rsqrt(jnp.mean(centered * centered, axis=0, keepdims=True) + EPSILON)
            normed = centered * inverse
            n_one[:, col] = normed
            inv_one[:, col] = inverse
            hid[:, col] = (normed * vecs[1] + vecs[2]).astype(BF)

    for n, (copy, _, _) in enumerate(second_plane):
        copy.wait_recv()
        ws[len(first_plane) + n + 1].start()

    def first_matmul(r):
        @pl.loop(0, units // rows)
        def _(i):
            row = pl.ds(pl.multiple_of(i * rows, rows), rows)
            pre = dot(w_all[r, pl.ds(0, width), row], hid[...], 0, 0) + bias[r, row, 0:1]
            cdf = 0.5 + 0.5 * lax.erf(pre * (1.0 / math.sqrt(2.0)))
            pdf = jnp.exp(-0.5 * pre * pre) * (1.0 / math.sqrt(2.0 * math.pi))
            act[r, row] = (pre * cdf).astype(BF)
            slope[r, row] = (cdf + pre * pdf).astype(BF)

    first_matmul(0)
    for copy in ws:
        copy.wait_recv()
    pl.loop(1, shards)(first_matmul)

    hits[...] = jnp.zeros_like(hits)
    acc[...] = jnp.zeros_like(acc)

    @pl.loop(0, chunk // cols)
    def _(i):
        col = pl.ds(pl.multiple_of(i * cols, cols), cols)
        second = n_one[:, col] * vecs[1, :, 0:1] + vecs[2, :, 0:1] + vecs[0, :, 0:1]
        total = dot(w_all[0, pl.ds(width, units)], act[0, :, col], 0, 0)
        for r in ring:
            total += dot(w_all[r, pl.ds(width, units)], act[r, :, col], 0, 0)
        second += total
        centered = second - jnp.mean(second, axis=0, keepdims=True)
        inverse = lax.rsqrt(jnp.mean(centered * centered, axis=0, keepdims=True) + EPSILON)
        normed = centered * inverse
        n_two[:, col] = normed
        inv_two[:, col] = inverse
        result = normed * vecs[3, :, 0:1] + vecs[4, :, 0:1]
        x_all[:, col] = result.astype(BF)
        feature = lax.broadcasted_iota(jnp.int32, (width, cols), 0)
        here = pl.ds(pl.multiple_of(me * chunk + i * cols, cols), cols)
        chosen = feature == labels[here].reshape(1, cols)
        picked = jnp.sum(jnp.where(chosen, result, 0.0), axis=0, keepdims=True)
        soft = 1.0 / (1.0 + jnp.exp(-2.0 * picked))
        hits[...] += jnp.where(mask[here].reshape(1, cols) == 1, soft, 0.0)

    def send_back(source, target, send, recv, first, length):
        copies = []
        for d in ring:
            peer = mp_peer(d)
            copies.append(
                remote(
                    source.at[
                        pl.ds(pl.multiple_of(peer * width_local, 16), width_local),
                        pl.ds(first, length),
                    ],
                    target.at[:, pl.ds(pl.multiple_of(me * chunk + first, 128), length)],
                    send.at[d],
                    recv.at[d],
                    {"mp": peer},
                )
            )
        return copies

    out_copies = send_back(x_all, out, out_send, out_recv, 0, chunk)
    out_own = pltpu.make_async_copy(x_all.at[my_rows], out.at[:, my_cols], own_sem.at[0])
    for copy in out_copies + [out_own]:
        copy.start()

    cot_copies = sum((exchange(cot, c_all, cot_send, cot_recv, s) for s in range(slots)), [])
    tok_copies = sum((exchange(tok, x_all, tok_send, tok_recv, s) for s in range(slots)), [])
    for copy in cot_copies:
        copy.wait_recv()

    @pl.loop(0, chunk // cols)
    def _(i):
        col = pl.ds(pl.multiple_of(i * cols, cols), cols)
        upstream = c_all[:, col].astype(F32)
        normed = n_two[:, col]
        scaled = upstream * vecs[3, :, 0:1]
        first = jnp.mean(scaled, axis=0, keepdims=True)
        both = jnp.mean(scaled * normed, axis=0, keepdims=True)
        grad_two = inv_two[:, col] * (scaled - first - normed * both)
        n_two[:, col] = grad_two
        low = grad_two.astype(BF)
        grad[:, col] = low
        acc[0] += lanes(low.astype(F32))
        acc[3] += lanes(upstream * normed)
        acc[4] += lanes(upstream)

    half = width // 2
    split = 1 if half // chips % 16 == 0 else 2
    piece_rows = half * split // chips
    piece_cols = width // split
    keep = pl.ds(pl.multiple_of(core * half, 16), half)
    give = pl.ds(pl.multiple_of((1 - core) * half, 16), half)

    def piece(who):
        chip = who // 2
        first = core * half + chip // split * piece_rows
        return (
            pl.ds(pl.multiple_of(first, 16), piece_rows),
            pl.ds(pl.multiple_of(lax.rem(chip, split) * piece_cols, 128), piece_cols),
        )

    d_out = act.at[:, :, pl.ds(0, width)]
    d_in = w_all.at[:, pl.ds(width, units)]

    def near_copy(x, r):
        source = (d_in, d_out)[x]
        return remote(
            source.at[r, give], near.at[x, r], near_send.at[x, r], near_recv.at[x, r], sibling
        )

    def add_near(x):
        source = (d_in, d_out)[x]

        @pl.loop(0, shards)
        def _(r):
            near_copy(x, r).wait_recv()
            source[r, keep] = (source[r, keep].astype(F32) + near[x, r].astype(F32)).astype(BF)

        copies = []
        for k in others:
            at, across = piece(dp_peer(k))
            copies.append(
                remote(
                    source.at[:, at, across],
                    far.at[x, k - 1],
                    far_send.at[x, k],
                    far_recv.at[x, k],
                    {"dp": dp_peer(k)},
                )
            )
        for copy in copies:
            copy.start()
        return copies

    my_at, my_across = piece(group)

    def add_far(x, copies):
        source = (d_in, d_out)[x]
        for copy in copies:
            copy.wait_recv()

        @pl.loop(0, shards)
        def _(r):
            total = source[r, my_at, my_across].astype(F32)
            for k in others:
                total += far[x, k - 1, r].astype(F32)
            part_low[x, r] = total.astype(BF)

            @pl.when(r == 0)
            def _():
                own_part[x] = total

        copies = [
            remote(
                part_low.at[x, d],
                line_in.at[x, d - 1],
                line_send.at[x, d],
                line_recv.at[x, d],
                {"mp": mp_peer(d)},
            )
            for d in ring
        ]
        for copy in copies:
            copy.start()
        return copies

    def add_line(x, copies):
        for copy in copies:
            copy.wait_recv()
        total = own_part[x]
        for d in ring:
            total += line_in[x, d - 1].astype(F32)
        done_low[x] = total.astype(BF)
        target = d_w.at[x, my_at, my_across]
        copies = [
            remote(
                done_low.at[x], target, done_send.at[x, k], done_recv.at[x, k], {"dp": dp_peer(k)}
            )
            for k in others
        ]
        own = pltpu.make_async_copy(done_low.at[x], target, own_sem.at[1 + slots + x])
        for copy in copies + [own]:
            copy.start()
        return copies, own

    def share(x, copies, own):
        own.wait()
        for copy in copies:
            copy.wait_recv()
        copy = remote(
            d_w.at[x, keep], d_w.at[x, keep], share_send.at[x], share_recv.at[x], sibling
        )
        copy.start()
        return copy

    @pl.loop(0, shards)
    def _(r):
        @pl.loop(0, units // rows)
        def _(i):
            row = pl.ds(pl.multiple_of(i * rows, rows), rows)
            d_out[r, row] = dot(act[r, row], grad[...], 1, 1).astype(BF)

        near_copy(1, r).start()

    @pl.loop(0, shards)
    def _(r):
        @pl.loop(0, units // rows)
        def _(i):
            row = pl.ds(pl.multiple_of(i * rows, rows), rows)
            grad_act = dot(w_all[r, pl.ds(pl.multiple_of(width + i * rows, rows), rows)], grad[...])
            low = (grad_act * slope[r, row].astype(F32)).astype(BF)
            slope[r, row] = low
            bias[r, row] = lanes(low.astype(F32))

    far_out = add_near(1)

    for copy in wz + [copy for copy, _, _ in first_plane + second_plane] + ws:
        copy.wait_send()

    @pl.when(jnp.logical_not(at_end))
    def _():
        pass_on(1, 2).wait_send()
        pass_on(2, 3).wait_send()

    @pl.loop(0, shards)
    def _(r):
        @pl.loop(0, width // rows)
        def _(i):
            row = pl.ds(pl.multiple_of(i * rows, rows), rows)
            d_in[r, row] = dot(hid[row], slope[r], 1, 1).astype(BF)

        near_copy(0, r).start()

    @pl.loop(0, chunk // cols)
    def _(i):
        col = pl.ds(pl.multiple_of(i * cols, cols), cols)
        total = dot(w_all[0, pl.ds(0, width)], slope[0, :, col])
        for r in ring:
            total += dot(w_all[r, pl.ds(0, width)], slope[r, :, col])
        upstream = n_two[:, col] + total
        normed = n_one[:, col]
        scaled = upstream * vecs[1, :, 0:1]
        first = jnp.mean(scaled, axis=0, keepdims=True)
        both = jnp.mean(scaled * normed, axis=0, keepdims=True)
        grad_one = inv_one[:, col] * (scaled - first - normed * both)
        n_two[:, col] = grad_one
        c_all[:, col] = grad_one.astype(BF)
        acc[1] += lanes(upstream * normed)
        acc[2] += lanes(upstream)

    far_in = add_near(0)
    dx_copies = []
    for slot in range(slots):
        at = pl.ds(slot * slot_length, slot_length)

        @pl.loop(0, width // rows)
        def _(i):
            row = pl.ds(pl.multiple_of(i * rows, rows), rows)
            seq_c[row] = dot(cos_h[row], c_all[:, at]).astype(BF)
            seq_s[row] = -dot(sin_h[row], c_all[:, at]).astype(BF)

        @pl.loop(0, width // rows)
        def _(i):
            row = pl.ds(pl.multiple_of(i * rows, rows), rows)
            back = dot(seq_c[row], cos_tab[slot]) + dot(seq_s[row], sin_tab[slot])
            c_all[row, at] = (n_two[row, at] + back).astype(BF)

        copies = send_back(
            c_all, dx, dx_send.at[slot], dx_recv.at[slot], slot * slot_length, slot_length
        )
        copies.append(
            pltpu.make_async_copy(
                c_all.at[my_rows, at],
                dx.at[
                    :,
                    pl.ds(pl.multiple_of(me * chunk + slot * slot_length, 128), slot_length),
                ],
                own_sem.at[1 + slot],
            )
        )
        dx_copies.append(copies)
        if slot == 0:
            for copy in copies:
                copy.start()

    lane = lax.broadcasted_iota(jnp.int32, (width_local, 128), 1)
    total_hits = jnp.sum(hits[...], axis=1, keepdims=True)
    for r in range(shards):
        shard = lax.rem(me + r, shards)
        at = pl.ds(pl.multiple_of(shard * width_local, 8), width_local)
        sums_own[r, 0:1] = jnp.broadcast_to(
            jnp.sum(bias[r], axis=1, keepdims=True), (units, 128)
        ).T[0:1]
        line = jnp.where(lane == 6, total_hits, 0.0)
        for i in range(5):
            line += jnp.where(lane == i + 1, jnp.sum(acc[i, at], axis=1, keepdims=True), 0.0)
        spare = (-width_local) % 128
        if spare:
            line = jnp.concatenate([line, jnp.zeros((spare, 128), F32)], axis=0)
        sums_own[r, 1:8, : width_local + spare] = line.T[1:8]
        sums_own[r, 1:8, width_local + spare :] = jnp.zeros((7, units - width_local - spare), F32)
    mp_sums = [
        remote(sums_own.at[d], sums_mp.at[me], mp_send.at[d], mp_recv.at[d], {"mp": mp_peer(d)})
        for d in ring
    ]
    for copy in mp_sums:
        copy.start()
    sums_mp[me] = sums_own[0]

    line_out = add_far(1, far_out)
    for copy in mp_sums:
        copy.wait_recv()
    sums_mid[...] = sum(sums_mp[s] for s in range(shards))
    dp_sums = [
        remote(sums_mid, sums_dp.at[group], dp_send.at[q], dp_recv.at[q], peer)
        for q, peer in enumerate(plane)
    ]
    for copy in dp_sums:
        copy.start()
    sums_dp[group] = sums_mid[...]
    line_from_in = add_far(0, far_in)
    for copies in dx_copies[1:]:
        for copy in copies:
            copy.start()
    done_out, own_out = add_line(1, line_out)
    for copy in dp_sums:
        copy.wait_recv()
    sums[...] = sum(sums_dp[q] for q in range(groups))
    done_in, own_in = add_line(0, line_from_in)
    share_out = share(1, done_out, own_out)
    share_in = share(0, done_in, own_in)

    @pl.loop(0, shards)
    def _(r):
        near_copy(0, r).wait_send()
        near_copy(1, r).wait_send()

    for copy in small_copies + tok_copies + cot_copies + mp_sums + dp_sums:
        copy.wait_send()
    for copy in far_out + far_in + line_out + line_from_in + done_out + done_in:
        copy.wait_send()
    for copy in out_copies + [out_own] + sum(dx_copies, []) + [share_out, share_in]:
        copy.wait()


def layer_call(shards, groups, tok, cot, w_in, w_out, small, bucket, labels, mask):
    width_local, tokens = tok.shape
    width = width_local * shards
    units = w_in.shape[1]
    chunk = tokens // shards
    slot_length = tokens // bucket.shape[0]
    slots = chunk // slot_length
    cols = min(256, slot_length)
    dma = pltpu.SemaphoreType.DMA
    chips = groups // 2
    split = 1 if width // 2 // chips % 16 == 0 else 2
    piece = (width // 2 * split // chips, width // split)
    return pl.pallas_call(
        functools.partial(layer_kernel, shards, groups),
        out_shape=[
            jax.ShapeDtypeStruct((width_local, tokens), BF),
            jax.ShapeDtypeStruct((width_local, tokens), BF),
            jax.ShapeDtypeStruct((2, width, units), BF),
            jax.ShapeDtypeStruct((8, units), F32),
        ],
        in_specs=[ANY] * 5 + [SMEM, VMEM, VMEM],
        out_specs=[ANY, ANY, ANY, VMEM],
        scratch_shapes=[
            pltpu.VMEM((width, chunk), BF),
            pltpu.VMEM((width, chunk), BF),
            pltpu.VMEM((shards, 2 * width, units), BF),
            pltpu.VMEM((shards, 8, units), F32),
            pltpu.VMEM((slots, slot_length, slot_length), BF),
            pltpu.VMEM((slots, slot_length, slot_length), BF),
            pltpu.VMEM((width, width), BF),
            pltpu.VMEM((width, width), BF),
            pltpu.VMEM((width, chunk), F32),
            pltpu.VMEM((1, chunk), F32),
            pltpu.VMEM((width, chunk), BF),
            pltpu.VMEM((shards, units, chunk), BF),
            pltpu.VMEM((shards, units, chunk), BF),
            pltpu.VMEM((width, chunk), F32),
            pltpu.VMEM((1, chunk), F32),
            pltpu.VMEM((width, chunk), BF),
            pltpu.VMEM((width, slot_length), BF),
            pltpu.VMEM((width, slot_length), BF),
            pltpu.VMEM((5, width, 128), F32),
            pltpu.VMEM((shards, units, 128), F32),
            pltpu.VMEM((5, width, 128), F32),
            pltpu.VMEM((1, cols), F32),
            pltpu.VMEM((2, shards, width // 2, width), BF),
            pltpu.VMEM((2, chips - 1, shards) + piece, BF),
            pltpu.VMEM((2, shards) + piece, BF),
            pltpu.VMEM((2, shards - 1) + piece, BF),
            pltpu.VMEM((2,) + piece, F32),
            pltpu.VMEM((2,) + piece, BF),
            pltpu.VMEM((shards, 8, units), F32),
            pltpu.VMEM((shards, 8, units), F32),
            pltpu.VMEM((8, units), F32),
            pltpu.VMEM((groups, 8, units), F32),
            dma((3,)),
            dma((3 + slots,)),
        ]
        + [dma((slots, shards))] * 4
        + [dma((shards,))] * 4
        + [dma((2 * chips,))] * 4
        + [dma((shards,))] * 2
        + [dma((slots, shards))] * 2
        + [dma((2, shards))] * 2
        + [dma((2, chips))] * 2
        + [dma((2, shards))] * 2
        + [dma((2, chips))] * 2
        + [dma((2,))] * 2
        + [dma((shards,))] * 2
        + [dma((groups,))] * 2,
        compiler_params=pltpu.CompilerParams(
            collective_id=0, has_side_effects=True, vmem_limit_bytes=VMEM_LIMIT
        ),
        name="layer",
    )(tok, cot, w_in, w_out, small, bucket, labels, mask)


def body(
    tokens,
    bucket,
    w_in,
    b_in,
    w_out,
    b_out,
    gain_one,
    shift_one,
    gain_two,
    shift_two,
    mask,
    labels,
    cotangent,
):
    shards = lax.axis_size("mp")
    groups = lax.axis_size("dp")
    width_local, token_count = tokens.shape
    units = w_in.shape[1]
    vectors = jnp.stack([b_out, gain_one, shift_one, gain_two, shift_two])
    small = jnp.concatenate(
        [b_in[None, :], jnp.pad(vectors, ((0, 2), (0, units - width_local)))], axis=0
    )
    output, d_x, grads, sums = layer_call(
        shards,
        groups,
        tokens,
        cotangent,
        w_in,
        w_out,
        small,
        bucket,
        labels,
        mask,
    )
    d_tokens = d_x.astype(F32)
    grads = grads.astype(F32)
    rest = [sums[i + 1, :width_local] for i in range(5)]
    score = sums[6, 0] * 8.0 / (token_count * groups)
    return (output, d_tokens, grads[0], sums[0], grads[1], *rest, score)


def solution(mesh):
    in_specs = (
        P("mp", "dp"),
        P("dp"),
        P(None, "mp"),
        P("mp"),
        P("mp", None),
        P("mp"),
        P("mp"),
        P("mp"),
        P("mp"),
        P("mp"),
        P("dp"),
        P("dp"),
        P("mp", "dp"),
    )
    out_specs = (
        P("mp", "dp"),
        P("mp", "dp"),
        P(None, "mp"),
        P("mp"),
        P("mp", None),
        P("mp"),
        P("mp"),
        P("mp"),
        P("mp"),
        P("mp"),
        P(),
    )
    return jax.shard_map(body, mesh=mesh, in_specs=in_specs, out_specs=out_specs, check_vma=False)
```

```python
import functools
import math

import jax
import jax.numpy as jnp
from jax import lax
from jax.experimental import pallas as pl
from jax.experimental.pallas import tpu as pltpu
from jax.sharding import PartitionSpec as P

EPSILON = 1e-05
BF = jnp.bfloat16
F32 = jnp.float32
ANY = pl.BlockSpec(memory_space=pl.ANY)
VMEM = pl.BlockSpec(memory_space=pltpu.VMEM)
SMEM = pl.BlockSpec(memory_space=pltpu.SMEM)
VMEM_LIMIT = 67_000_000


def turns(phase):
    quarter = jnp.floor(phase * 4.0 + 0.5)
    angle = (phase - quarter * 0.25) * (2.0 * math.pi)
    square = angle * angle
    cosine = 1.0 + square * (
        -1 / 2 + square * (1 / 24 + square * (-1 / 720 + square * (1 / 40320)))
    )
    sine = angle * (
        1.0
        + square * (-1 / 6 + square * (1 / 120 + square * (-1 / 5040 + square * (1 / 362880))))
    )
    odd = (quarter == 1.0) | (quarter == 3.0)
    first = jnp.where(odd, sine, cosine)
    second = jnp.where(odd, cosine, sine)
    return (
        jnp.where((quarter == 1.0) | (quarter == 2.0), -first, first),
        jnp.where((quarter == 2.0) | (quarter == 3.0), -second, second),
    )


def dot(left, right, left_dim=1, right_dim=0):
    return lax.dot_general(
        left, right, (((left_dim,), (right_dim,)), ((), ())), preferred_element_type=F32
    )


def remote(source, target, send_sem, recv_sem, device):
    return pltpu.make_async_remote_copy(
        src_ref=source,
        dst_ref=target,
        send_sem=send_sem,
        recv_sem=recv_sem,
        device_id=device,
        device_id_type=pl.DeviceIdType.MESH,
    )


def greet(peers):
    barrier = pltpu.get_barrier_semaphore()
    for peer in peers:
        pl.semaphore_signal(barrier, inc=1, device_id=peer, device_id_type=pl.DeviceIdType.MESH)
    pl.semaphore_wait(barrier, len(peers))


def lanes(values):
    return sum(values[:, i : i + 128] for i in range(128, values.shape[1], 128)) + values[:, :128]


def layer_kernel(
    shards,
    groups,
    tok,
    cot,
    w_in,
    w_out,
    small,
    bucket,
    labels,
    mask,
    out,
    dx,
    d_w,
    sums,
    x_all,
    c_all,
    w_all,
    small_all,
    cos_tab,
    sin_tab,
    cos_h,
    sin_h,
    n_one,
    inv_one,
    hid,
    act,
    slope,
    n_two,
    inv_two,
    grad,
    seq_c,
    seq_s,
    vecs,
    bias,
    acc,
    hits,
    near,
    far,
    turn,
    part_low,
    line_in,
    own_part,
    done_low,
    sums_own,
    sums_mp,
    sums_mid,
    sums_dp,
    load_sem,
    own_sem,
    tok_send,
    tok_recv,
    cot_send,
    cot_recv,
    small_send,
    small_recv,
    wz_send,
    wz_recv,
    wp_send,
    wp_recv,
    ws_send,
    ws_recv,
    out_send,
    out_recv,
    dx_send,
    dx_recv,
    near_send,
    near_recv,
    far_send,
    far_recv,
    turn_send,
    turn_recv,
    line_send,
    line_recv,
    done_send,
    done_recv,
    share_send,
    share_recv,
    mp_send,
    mp_recv,
    dp_send,
    dp_recv,
):
    me = lax.axis_index("mp")
    group = lax.axis_index("dp")
    width_local = tok.shape[0]
    width = width_local * shards
    units = w_in.shape[1]
    chunk = tok.shape[1] // shards
    slots = cos_tab.shape[0]
    slot_length = chunk // slots
    part = 2 * width // groups
    chips = groups // 2
    rows = width
    some = width // 2
    cols = slot_length
    ring = range(1, shards)
    others = range(1, chips)

    inner = jnp.where(me < shards // 2, 1, -1)
    at_end = (me == 0) | (me == shards - 1)

    def mp_peer(step):
        return lax.rem(me + step, shards)

    def inward(step):
        return lax.rem(me + step * inner + shards, shards)

    def dp_peer(step):
        return lax.rem(group + 2 * step, groups)

    core = lax.rem(group, 2)
    sibling = {"dp": group + 1 - 2 * core}
    plane = [{"dp": lax.rem(group + q, groups)} for q in range(1, groups)]
    own_w = [
        pltpu.make_async_copy(w_in, w_all.at[0, :width], own_sem.at[0]),
        pltpu.make_async_copy(w_out, w_all.at[0, width:], own_sem.at[1]),
    ]
    my_cols = pl.ds(pl.multiple_of(me * chunk, 128), chunk)
    my_rows = pl.ds(pl.multiple_of(me * width_local, 16), width_local)
    loads = [
        pltpu.make_async_copy(source, target, load_sem.at[i])
        for i, (source, target) in enumerate(
            [
                (small, small_all.at[0]),
                (tok.at[:, my_cols], x_all.at[my_rows]),
                (cot.at[:, my_cols], c_all.at[my_rows]),
            ]
        )
    ]
    for copy in own_w + loads:
        copy.start()

    greet([{"mp": mp_peer(d)} for d in ring] + plane)

    def exchange(source, target, send, recv, slot, steps=(1, 2, 3)):
        copies = []
        for step in steps:
            peer = inward(step)
            d = lax.rem(peer - me + shards, shards)
            first = pl.multiple_of(peer * chunk + slot * slot_length, 128)
            copies.append(
                remote(
                    source.at[:, pl.ds(first, slot_length)],
                    target.at[
                        my_rows, pl.ds(pl.multiple_of(slot * slot_length, 128), slot_length)
                    ],
                    send.at[slot, d],
                    recv.at[slot, d],
                    {"mp": peer},
                )
            )
        return copies

    small_copies = [
        remote(
            small,
            small_all.at[shards - d],
            small_send.at[d],
            small_recv.at[d],
            {"mp": mp_peer(d)},
        )
        for d in ring
    ]
    for copy in small_copies:
        copy.start()
    for copy in own_w:
        copy.wait()
    my_part = pl.ds(pl.multiple_of(group * part, 16), part)

    def weight_copy(shard, target, send):
        place = lax.rem(shard - me + 2 * shards, shards)
        there = lax.rem(shard - target + 2 * shards, shards)
        return remote(
            w_all.at[place, my_part],
            w_all.at[there, my_part],
            wz_send.at[send],
            wz_recv.at[there],
            {"mp": target},
        )

    def weight_wait(place):
        remote(
            w_all.at[0, my_part],
            w_all.at[place, my_part],
            wz_send.at[0],
            wz_recv.at[place],
            {"mp": inward(1)},
        ).wait_recv()

    near_step = jnp.where(at_end, 1, 3)
    far_step = jnp.where(at_end, 2, 1)
    wz = [weight_copy(me, inward(near_step), 1), weight_copy(me, inward(far_step), 0)]
    for copy in wz:
        copy.start()
    for slot in range(slots):
        for copy in exchange(tok, x_all, tok_send, tok_recv, slot, (1, 2)):
            copy.start()

        @pl.when(at_end)
        def _():
            for copy in exchange(tok, x_all, tok_send, tok_recv, slot, (3,)):
                copy.start()

    def pass_on(step, send):
        return weight_copy(inward(step), inward(3), send)

    side = math.isqrt(chips)
    chip_x, chip_y = lax.rem(group // 2, side), group // 2 // side
    halves = (pl.ds(0, units // 2), pl.ds(units // 2, units // 2))
    arrival = [
        lax.rem(step * inner + shards, shards)
        for step in (1, jnp.where(at_end, 2, 3), jnp.where(at_end, 3, 2))
    ]

    def at_chip(x, y):
        return (lax.rem(y + side, side) * side + lax.rem(x + side, side)) * 2 + core

    def weights_of(n, who, across):
        rows_of = pl.ds(pl.multiple_of(who * part, 16), part)
        return w_all.at[arrival[n], rows_of, across]

    def plane_copy(n, who, across, to, sem):
        at = weights_of(n, who, across)
        return remote(at, at, wp_send.at[n, sem], wp_recv.at[n, sem], to)

    def to_sibling(n, who, across, sem):
        at = weights_of(n, who, across)
        return remote(at, at, ws_send.at[n, sem], ws_recv.at[n, sem], sibling)

    first_plane, second_plane = [[], [], []], [[], [], []]
    first_ws, second_ws = [[], [], []], [[], [], []]
    own_ws = [to_sibling(n, group, pl.ds(0, units), 0) for n in range(3)]
    for n in range(3):
        for h, across in enumerate(halves):
            for p in range(1, side):
                step_x, step_y = (p, 0) if h == 0 else (0, p)
                to = {"dp": at_chip(chip_x + step_x, chip_y + step_y)}
                first_plane[n].append(plane_copy(n, group, across, to, h * chips + p))
                who = at_chip(chip_x - step_x, chip_y - step_y)
                first_ws[n].append(to_sibling(n, who, across, 1 + h * (side - 1) + p - 1))
                for q in range(side):
                    if h == 0:
                        source, to = at_chip(chip_x + q, chip_y), at_chip(chip_x, chip_y + p)
                        who = at_chip(chip_x + q, chip_y - p)
                    else:
                        source, to = at_chip(chip_x, chip_y + q), at_chip(chip_x + p, chip_y)
                        who = at_chip(chip_x - p, chip_y + q)
                    sem = h * chips + side * p + q
                    second_plane[n].append(plane_copy(n, source, across, {"dp": to}, sem))
                    sem = 1 + 2 * (side - 1) + (h * (side - 1) + p - 1) * side + q
                    second_ws[n].append(to_sibling(n, who, across, sem))

    def line_arrived(n):
        weight_wait(arrival[n])
        for copy in first_plane[n]:
            copy.start()
        own_ws[n].start()

    def first_arrived(n):
        for copy in first_plane[n]:
            copy.wait_recv()
        for copy in second_plane[n] + first_ws[n]:
            copy.start()

    def second_arrived(n):
        for copy in second_plane[n]:
            copy.wait_recv()
        for copy in second_ws[n]:
            copy.start()

    turn_rows = min(64, slot_length)

    @pl.loop(0, width // turn_rows)
    def _(i):
        row = pl.ds(pl.multiple_of(i * turn_rows, 16), turn_rows)
        shape = (turn_rows, width)
        product = (
            (lax.broadcasted_iota(jnp.int32, shape, 0) + i * turn_rows)
            * lax.broadcasted_iota(jnp.int32, shape, 1)
        ).astype(F32)
        phase = product * (1.0 / width)
        phase = (product - jnp.floor(phase) * width) * (1.0 / width)
        cosine, sine = turns(phase)
        cos_h[row] = (cosine * (1.0 / math.sqrt(width))).astype(BF)
        sin_h[row] = (sine * (1.0 / math.sqrt(width))).astype(BF)

    @pl.loop(0, slots * slot_length // turn_rows)
    def _(i):
        slot = i // (slot_length // turn_rows)
        first = lax.rem(i, slot_length // turn_rows) * turn_rows
        row = pl.ds(pl.multiple_of(first, 16), turn_rows)
        shape = (turn_rows, slot_length)
        which = bucket[me * slots + slot]
        length = jnp.where(which == 0, slot_length // 4, slot_length // 2)
        length = jnp.where(which == 2, slot_length, length)
        at = lax.broadcasted_iota(jnp.int32, shape, 0) + first
        to = lax.broadcasted_iota(jnp.int32, shape, 1)
        inner = length - 1
        phase = ((at & inner) * (to & inner)) & inner
        scale = jnp.full((1, 1), length, jnp.int32).astype(F32)
        cosine, sine = turns(phase.astype(F32) / scale)
        scale = jnp.where((at ^ to) < length, lax.rsqrt(scale), 0.0)
        cos_tab[slot, row] = (cosine * scale).astype(BF)
        sin_tab[slot, row] = (sine * scale).astype(BF)


    line_arrived(0)

    @pl.when(jnp.logical_not(at_end))
    def _():
        pass_on(1, 2).start()

    line_arrived(1)
    first_arrived(0)
    line_arrived(2)

    @pl.when(jnp.logical_not(at_end))
    def _():
        pass_on(2, 3).start()
        for slot in range(slots):
            for copy in exchange(tok, x_all, tok_send, tok_recv, slot, (3,)):
                copy.start()

    first_arrived(1)
    first_arrived(2)

    for copy in loads:
        copy.wait()
    for copy in small_copies:
        copy.wait_recv()
    for r in range(shards):
        shard = lax.rem(me + r, shards)
        at = pl.ds(pl.multiple_of(shard * width_local, 8), width_local)
        bias[r] = jnp.broadcast_to(small_all[r, 0:1, :units], (128, units)).T
        for i in range(5):
            line = small_all[r, i + 1 : i + 2, : (width_local + 127) // 128 * 128]
            vecs[i, at] = jnp.broadcast_to(line, (128, line.shape[1])).T[:width_local]

    for slot in range(slots):
        at = pl.ds(pl.multiple_of(slot * slot_length, 128), slot_length)
        for copy in exchange(tok, x_all, tok_send, tok_recv, slot):
            copy.wait_recv()

        if slot == slots - 1:
            for later in range(slots):
                for copy in exchange(cot, c_all, cot_send, cot_recv, later):
                    copy.start()

        seq_c[...] = dot(x_all[:, at], cos_tab[slot]).astype(BF)
        seq_s[...] = dot(x_all[:, at], sin_tab[slot]).astype(BF)

        @pl.loop(0, width // rows)
        def _(i):
            row = pl.ds(pl.multiple_of(i * rows, rows), rows)
            mixing = dot(cos_h[row], seq_c[...]) - dot(sin_h[row], seq_s[...])
            n_one[row, at] = x_all[row, at].astype(F32) + mixing

        @pl.loop(0, slot_length // 128)
        def _(i):
            col = pl.ds(pl.multiple_of(slot * slot_length + i * 128, 128), 128)
            value = n_one[:, col]
            centered = value - jnp.mean(value, axis=0, keepdims=True)
            inverse = lax.rsqrt(jnp.mean(centered * centered, axis=0, keepdims=True) + EPSILON)
            normed = centered * inverse
            n_one[:, col] = normed
            inv_one[:, col] = inverse
            hid[:, col] = (normed * vecs[1] + vecs[2]).astype(BF)

        if slot == 0:
            for n in range(3):
                second_arrived(n)

    def first_matmul(r):
        @pl.loop(0, units // some)
        def _(i):
            row = pl.ds(pl.multiple_of(i * some, some), some)
            pre = dot(w_all[r, pl.ds(0, width), row], hid[...], 0, 0) + bias[r, row, 0:1]
            cdf = 0.5 + 0.5 * lax.erf(pre * (1.0 / math.sqrt(2.0)))
            pdf = jnp.exp(-0.5 * pre * pre) * (1.0 / math.sqrt(2.0 * math.pi))
            act[r, row] = (pre * cdf).astype(BF)
            slope[r, row] = (cdf + pre * pdf).astype(BF)

    first_matmul(0)
    ws = sum(first_ws + second_ws, own_ws)
    for copy in ws:
        copy.wait_recv()
    pl.loop(1, shards)(first_matmul)

    hits[...] = jnp.zeros_like(hits)
    acc[...] = jnp.zeros_like(acc)

    @pl.loop(0, chunk // cols)
    def _(i):
        col = pl.ds(pl.multiple_of(i * cols, cols), cols)
        second = n_one[:, col] * vecs[1, :, 0:1] + vecs[2, :, 0:1] + vecs[0, :, 0:1]
        total = dot(w_all[0, pl.ds(width, units)], act[0, :, col], 0, 0)
        for r in ring:
            total += dot(w_all[r, pl.ds(width, units)], act[r, :, col], 0, 0)
        second += total
        centered = second - jnp.mean(second, axis=0, keepdims=True)
        inverse = lax.rsqrt(jnp.mean(centered * centered, axis=0, keepdims=True) + EPSILON)
        normed = centered * inverse
        n_two[:, col] = normed
        inv_two[:, col] = inverse
        result = normed * vecs[3, :, 0:1] + vecs[4, :, 0:1]
        x_all[:, col] = result.astype(BF)
        feature = lax.broadcasted_iota(jnp.int32, (width, cols), 0)
        here = pl.ds(pl.multiple_of(me * chunk + i * cols, cols), cols)
        chosen = feature == labels[here].reshape(1, cols)
        picked = jnp.sum(jnp.where(chosen, result, 0.0), axis=0, keepdims=True)
        soft = 1.0 / (1.0 + jnp.exp(-2.0 * picked))
        hits[...] += jnp.where(mask[here].reshape(1, cols) == 1, soft, 0.0)

    def send_back(source, target, send, recv, first, length):
        copies = []
        for d in ring:
            peer = mp_peer(d)
            copies.append(
                remote(
                    source.at[
                        pl.ds(pl.multiple_of(peer * width_local, 16), width_local),
                        pl.ds(first, length),
                    ],
                    target.at[:, pl.ds(pl.multiple_of(me * chunk + first, 128), length)],
                    send.at[d],
                    recv.at[d],
                    {"mp": peer},
                )
            )
        return copies

    out_copies = send_back(x_all, out, out_send, out_recv, 0, chunk)
    out_own = pltpu.make_async_copy(x_all.at[my_rows], out.at[:, my_cols], own_sem.at[0])

    cot_copies = sum((exchange(cot, c_all, cot_send, cot_recv, s) for s in range(slots)), [])
    tok_copies = sum((exchange(tok, x_all, tok_send, tok_recv, s) for s in range(slots)), [])
    for copy in cot_copies:
        copy.wait_recv()
    for copy in out_copies + [out_own]:
        copy.start()

    @pl.loop(0, chunk // cols)
    def _(i):
        col = pl.ds(pl.multiple_of(i * cols, cols), cols)
        upstream = c_all[:, col].astype(F32)
        normed = n_two[:, col]
        scaled = upstream * vecs[3, :, 0:1]
        first = jnp.mean(scaled, axis=0, keepdims=True)
        both = jnp.mean(scaled * normed, axis=0, keepdims=True)
        grad_two = inv_two[:, col] * (scaled - first - normed * both)
        n_two[:, col] = grad_two
        low = grad_two.astype(BF)
        grad[:, col] = low
        acc[0] += lanes(low.astype(F32))
        acc[3] += lanes(upstream * normed)
        acc[4] += lanes(upstream)

    half = width // 2
    split = 1 if half // chips % 16 == 0 else 2
    piece_rows = half * split // chips
    piece_cols = width // split
    keep = pl.ds(pl.multiple_of(core * half, 16), half)
    give = pl.ds(pl.multiple_of((1 - core) * half, 16), half)

    def piece(x, y):
        chip = lax.rem(y, side) * side + lax.rem(x, side)
        first = core * half + chip // split * piece_rows
        return (
            pl.ds(pl.multiple_of(first, 16), piece_rows),
            pl.ds(pl.multiple_of(lax.rem(chip, split) * piece_cols, 128), piece_cols),
        )

    d_out = act.at[:, :, pl.ds(0, width)]
    d_in = w_all.at[:, pl.ds(width, units)]

    def near_copy(x, r):
        source = (d_in, d_out)[x]
        return remote(
            source.at[r, give], near.at[x, r], near_send.at[x, r], near_recv.at[x, r], sibling
        )

    def far_copies(x, r):
        copies = []
        for p in range(1, side):
            peer = at_chip(
                chip_x + jnp.where(r < 2, p, 0), chip_y + jnp.where(r < 2, 0, p)
            )
            for q in range(side):
                at, across = piece(
                    chip_x + jnp.where(r < 2, p, q), chip_y + jnp.where(r < 2, q, p)
                )
                n = (p - 1) * side + q
                copies.append(
                    remote(
                        (d_in, d_out)[x].at[r, at, across],
                        far.at[x, n, r],
                        far_send.at[x, n, r],
                        far_recv.at[x, n, r],
                        {"dp": peer},
                    )
                )
        return copies

    def turn_copies(x, r):
        copies = []
        for q in range(1, side):
            to = chip_x + jnp.where(r < 2, 0, q), chip_y + jnp.where(r < 2, q, 0)
            at, across = piece(*to)
            copies.append(
                remote(
                    (d_in, d_out)[x].at[r, at, across],
                    turn.at[x, q - 1, r],
                    turn_send.at[x, q - 1, r],
                    turn_recv.at[x, q - 1, r],
                    {"dp": at_chip(*to)},
                )
            )
        return copies

    def add_near(x, r):
        source = (d_in, d_out)[x]
        near_copy(x, r).wait_recv()
        source[r, keep] = (source[r, keep].astype(F32) + near[x, r].astype(F32)).astype(BF)
        for copy in far_copies(x, r):
            copy.start()

    def in_turn(i):
        return lax.rem(i, 2) * 2 + i // 2

    def reduce_blocks(x, compute):
        @pl.loop(0, shards)
        def _(i):
            compute(in_turn(i))
            near_copy(x, in_turn(i)).start()

            @pl.when(i > 0)
            def _():
                add_near(x, in_turn(i - 1))

        add_near(x, shards - 1)

    def far_sum(x, r, q):
        at, across = piece(
            chip_x + jnp.where(r < 2, 0, q), chip_y + jnp.where(r < 2, q, 0)
        )
        total = (d_in, d_out)[x][r, at, across].astype(F32)
        for p in range(1, side):
            total += far[x, (p - 1) * side + q, r].astype(F32)
        return total

    def add_far(x):
        @pl.loop(0, shards)
        def _(i):
            r = in_turn(i)
            for copy in far_copies(x, r):
                copy.wait_recv()
            for q in range(1, side):
                at, across = piece(
                    chip_x + jnp.where(r < 2, 0, q), chip_y + jnp.where(r < 2, q, 0)
                )
                (d_in, d_out)[x][r, at, across] = far_sum(x, r, q).astype(BF)
            for copy in turn_copies(x, r):
                copy.start()

    my_at, my_across = piece(chip_x, chip_y)

    def add_turn(x):
        @pl.loop(0, shards)
        def _(r):
            for copy in turn_copies(x, r):
                copy.wait_recv()
            total = far_sum(x, r, 0)
            for q in range(1, side):
                total += turn[x, q - 1, r].astype(F32)
            part_low[x, r] = total.astype(BF)

            @pl.when(r == 0)
            def _():
                own_part[x] = total

        @pl.when(at_end)
        def _():
            for step, place in ((2, 2), (3, 3), (1, 0)):
                line_copy(x, step, inward(1), place).start()

        @pl.when(jnp.logical_not(at_end))
        def _():
            line_copy(x, 3, inward(3), 0).start()

    def line_copy(x, step, target, place):
        return remote(
            part_low.at[x, lax.rem(step * inner + shards, shards)],
            line_in.at[x, place],
            line_send.at[x, step],
            line_recv.at[x, place],
            {"mp": target},
        )

    def line_on(x):
        @pl.when(jnp.logical_not(at_end))
        def _():
            for step in (1, 2):
                line_copy(x, step, inward(step), step + 1).wait_recv()
                r = lax.rem(step * inner + shards, shards)
                part_low[x, r] = (
                    part_low[x, r].astype(F32) + line_in[x, step + 1].astype(F32)
                ).astype(BF)
                line_copy(x, step, inward(step), 1).start()

    def add_line(x):
        for place in (0, 1):
            line_copy(x, 1, inward(1), place).wait_recv()
        total = own_part[x] + line_in[x, 0].astype(F32) + line_in[x, 1].astype(F32)
        done_low[x] = total.astype(BF)
        target = d_w.at[x, my_at, my_across]
        copies = [
            remote(
                done_low.at[x], target, done_send.at[x, k], done_recv.at[x, k], {"dp": dp_peer(k)}
            )
            for k in others
        ]
        own = pltpu.make_async_copy(done_low.at[x], target, own_sem.at[1 + slots + x])
        for copy in copies + [own]:
            copy.start()
        return copies, own

    def share(x, copies, own):
        own.wait()
        for copy in copies:
            copy.wait_recv()
        copy = remote(
            d_w.at[x, keep], d_w.at[x, keep], share_send.at[x], share_recv.at[x], sibling
        )
        copy.start()
        return copy

    def second_weight(r):
        @pl.loop(0, units // rows)
        def _(i):
            row = pl.ds(pl.multiple_of(i * rows, rows), rows)
            d_out[r, row] = dot(act[r, row], grad[...], 1, 1).astype(BF)

    reduce_blocks(1, second_weight)

    @pl.loop(0, shards)
    def _(r):
        @pl.loop(0, units // some)
        def _(i):
            row = pl.ds(pl.multiple_of(i * some, some), some)
            grad_act = dot(w_all[r, pl.ds(pl.multiple_of(width + i * some, some), some)], grad[...])
            low = (grad_act * slope[r, row].astype(F32)).astype(BF)
            slope[r, row] = low
            bias[r, row] = lanes(low.astype(F32))

    for copy in wz + sum(first_plane + second_plane, ws):
        copy.wait_send()

    @pl.when(jnp.logical_not(at_end))
    def _():
        pass_on(1, 2).wait_send()
        pass_on(2, 3).wait_send()

    def first_weight(r):
        @pl.loop(0, width // rows)
        def _(i):
            row = pl.ds(pl.multiple_of(i * rows, rows), rows)
            d_in[r, row] = dot(hid[row], slope[r], 1, 1).astype(BF)

    reduce_blocks(0, first_weight)
    add_far(1)

    @pl.loop(0, chunk // cols)
    def _(i):
        col = pl.ds(pl.multiple_of(i * cols, cols), cols)
        total = dot(w_all[0, pl.ds(0, width)], slope[0, :, col])
        for r in ring:
            total += dot(w_all[r, pl.ds(0, width)], slope[r, :, col])
        upstream = n_two[:, col] + total
        normed = n_one[:, col]
        scaled = upstream * vecs[1, :, 0:1]
        first = jnp.mean(scaled, axis=0, keepdims=True)
        both = jnp.mean(scaled * normed, axis=0, keepdims=True)
        grad_one = inv_one[:, col] * (scaled - first - normed * both)
        n_two[:, col] = grad_one
        c_all[:, col] = grad_one.astype(BF)
        acc[1] += lanes(upstream * normed)
        acc[2] += lanes(upstream)

    dx_copies = []
    for slot in range(slots):
        at = pl.ds(slot * slot_length, slot_length)

        @pl.loop(0, width // rows)
        def _(i):
            row = pl.ds(pl.multiple_of(i * rows, rows), rows)
            seq_c[row] = dot(cos_h[row], c_all[:, at]).astype(BF)
            seq_s[row] = -dot(sin_h[row], c_all[:, at]).astype(BF)

        @pl.loop(0, width // rows)
        def _(i):
            row = pl.ds(pl.multiple_of(i * rows, rows), rows)
            back = dot(seq_c[row], cos_tab[slot]) + dot(seq_s[row], sin_tab[slot])
            c_all[row, at] = (n_two[row, at] + back).astype(BF)

        copies = send_back(
            c_all, dx, dx_send.at[slot], dx_recv.at[slot], slot * slot_length, slot_length
        )
        copies.append(
            pltpu.make_async_copy(
                c_all.at[my_rows, at],
                dx.at[
                    :,
                    pl.ds(pl.multiple_of(me * chunk + slot * slot_length, 128), slot_length),
                ],
                own_sem.at[1 + slot],
            )
        )
        dx_copies.append(copies)
        if slot == 0:
            for copy in copies:
                copy.start()

    add_turn(1)
    add_far(0)

    lane = lax.broadcasted_iota(jnp.int32, (width_local, 128), 1)
    total_hits = jnp.sum(hits[...], axis=1, keepdims=True)
    for r in range(shards):
        shard = lax.rem(me + r, shards)
        at = pl.ds(pl.multiple_of(shard * width_local, 8), width_local)
        sums_own[r, 0:1] = jnp.broadcast_to(
            jnp.sum(bias[r], axis=1, keepdims=True), (units, 128)
        ).T[0:1]
        line = jnp.where(lane == 6, total_hits, 0.0)
        for i in range(5):
            line += jnp.where(lane == i + 1, jnp.sum(acc[i, at], axis=1, keepdims=True), 0.0)
        spare = (-width_local) % 128
        if spare:
            line = jnp.concatenate([line, jnp.zeros((spare, 128), F32)], axis=0)
        sums_own[r, 1:8, : width_local + spare] = line.T[1:8]
        sums_own[r, 1:8, width_local + spare :] = jnp.zeros((7, units - width_local - spare), F32)
    mp_sums = [
        remote(sums_own.at[d], sums_mp.at[me], mp_send.at[d], mp_recv.at[d], {"mp": mp_peer(d)})
        for d in ring
    ]
    for copy in mp_sums:
        copy.start()
    sums_mp[me] = sums_own[0]

    add_turn(0)
    line_on(1)
    line_on(0)
    for copies in dx_copies[1:]:
        for copy in copies:
            copy.start()
    done_out, own_out = add_line(1)
    for copy in mp_sums:
        copy.wait_recv()
    sums_mid[...] = sum(sums_mp[s] for s in range(shards))
    dp_sums = [
        remote(sums_mid, sums_dp.at[group], dp_send.at[q], dp_recv.at[q], peer)
        for q, peer in enumerate(plane)
    ]
    for copy in dp_sums:
        copy.start()
    sums_dp[group] = sums_mid[...]
    done_in, own_in = add_line(0)
    share_out = share(1, done_out, own_out)
    for copy in dp_sums:
        copy.wait_recv()
    sums[...] = sum(sums_dp[q] for q in range(groups))
    share_in = share(0, done_in, own_in)

    @pl.loop(0, shards)
    def _(r):
        for x in range(2):
            for copy in [near_copy(x, r)] + far_copies(x, r) + turn_copies(x, r):
                copy.wait_send()

            @pl.when(r > 0)
            def _():
                line_copy(x, r, inward(1), 0).wait_send()

    for copy in small_copies + tok_copies + cot_copies + mp_sums + dp_sums:
        copy.wait_send()
    for copy in done_out + done_in:
        copy.wait_send()
    for copy in out_copies + [out_own] + sum(dx_copies, []) + [share_out, share_in]:
        copy.wait()


def layer_call(shards, groups, tok, cot, w_in, w_out, small, bucket, labels, mask):
    width_local, tokens = tok.shape
    width = width_local * shards
    units = w_in.shape[1]
    chunk = tokens // shards
    slot_length = tokens // bucket.shape[0]
    slots = chunk // slot_length
    cols = slot_length
    dma = pltpu.SemaphoreType.DMA
    chips = groups // 2
    side = math.isqrt(chips)
    split = 1 if width // 2 // chips % 16 == 0 else 2
    piece = (width // 2 * split // chips, width // split)
    return pl.pallas_call(
        functools.partial(layer_kernel, shards, groups),
        out_shape=[
            jax.ShapeDtypeStruct((width_local, tokens), BF),
            jax.ShapeDtypeStruct((width_local, tokens), BF),
            jax.ShapeDtypeStruct((2, width, units), BF),
            jax.ShapeDtypeStruct((8, units), F32),
        ],
        in_specs=[ANY] * 5 + [SMEM, VMEM, VMEM],
        out_specs=[ANY, ANY, ANY, VMEM],
        scratch_shapes=[
            pltpu.VMEM((width, chunk), BF),
            pltpu.VMEM((width, chunk), BF),
            pltpu.VMEM((shards, 2 * width, units), BF),
            pltpu.VMEM((shards, 8, units), F32),
            pltpu.VMEM((slots, slot_length, slot_length), BF),
            pltpu.VMEM((slots, slot_length, slot_length), BF),
            pltpu.VMEM((width, width), BF),
            pltpu.VMEM((width, width), BF),
            pltpu.VMEM((width, chunk), F32),
            pltpu.VMEM((1, chunk), F32),
            pltpu.VMEM((width, chunk), BF),
            pltpu.VMEM((shards, units, chunk), BF),
            pltpu.VMEM((shards, units, chunk), BF),
            pltpu.VMEM((width, chunk), F32),
            pltpu.VMEM((1, chunk), F32),
            pltpu.VMEM((width, chunk), BF),
            pltpu.VMEM((width, slot_length), BF),
            pltpu.VMEM((width, slot_length), BF),
            pltpu.VMEM((5, width, 128), F32),
            pltpu.VMEM((shards, units, 128), F32),
            pltpu.VMEM((5, width, 128), F32),
            pltpu.VMEM((1, cols), F32),
            pltpu.VMEM((2, shards, width // 2, width), BF),
            pltpu.VMEM((2, (side - 1) * side, shards) + piece, BF),
            pltpu.VMEM((2, side - 1, shards) + piece, BF),
            pltpu.VMEM((2, shards) + piece, BF),
            pltpu.VMEM((2, shards) + piece, BF),
            pltpu.VMEM((2,) + piece, F32),
            pltpu.VMEM((2,) + piece, BF),
            pltpu.VMEM((shards, 8, units), F32),
            pltpu.VMEM((shards, 8, units), F32),
            pltpu.VMEM((8, units), F32),
            pltpu.VMEM((groups, 8, units), F32),
            dma((3,)),
            dma((3 + slots,)),
        ]
        + [dma((slots, shards))] * 4
        + [dma((shards,))] * 4
        + [dma((shards - 1, 2 * chips))] * 4
        + [dma((shards,))] * 2
        + [dma((slots, shards))] * 2
        + [dma((2, shards))] * 2
        + [dma((2, (side - 1) * side, shards))] * 2
        + [dma((2, side - 1, shards))] * 2
        + [dma((2, shards))] * 2
        + [dma((2, chips))] * 2
        + [dma((2,))] * 2
        + [dma((shards,))] * 2
        + [dma((groups,))] * 2,
        compiler_params=pltpu.CompilerParams(
            collective_id=0, has_side_effects=True, vmem_limit_bytes=VMEM_LIMIT
        ),
        name="layer",
    )(tok, cot, w_in, w_out, small, bucket, labels, mask)


def finish_kernel(scale, low_x, low_w, sums, d_tokens, d_w_in, d_w_out, hits, d_b_in, *rest):
    d_tokens[...] = low_x[...].astype(F32)
    d_w_in[...] = low_w[0].astype(F32)
    d_w_out[...] = low_w[1].astype(F32)

    @pl.when(pl.program_id(0) == 0)
    def _():
        d_b_in[...] = sums[0]
        for i, target in enumerate(rest):
            target[...] = sums[i + 1, : target.shape[0]]
        hits[0, 0] = jnp.sum(sums[6:7, 0:1]) * scale


def finish_call(scale, low_x, low_w, sums):
    width_local, tokens = low_x.shape
    _, width, units = low_w.shape
    steps = 8
    whole = lambda length: pl.BlockSpec((length,), lambda i: (0,))
    return pl.pallas_call(
        functools.partial(finish_kernel, scale),
        grid=(steps,),
        out_shape=[
            jax.ShapeDtypeStruct((width_local, tokens), F32),
            jax.ShapeDtypeStruct((width, units), F32),
            jax.ShapeDtypeStruct((units, width), F32),
            jax.ShapeDtypeStruct((1, 1), F32),
            jax.ShapeDtypeStruct((units,), F32),
        ]
        + [jax.ShapeDtypeStruct((width_local,), F32)] * 5,
        in_specs=[
            pl.BlockSpec((width_local, tokens // steps), lambda i: (0, i)),
            pl.BlockSpec((2, width // steps, units), lambda i: (0, i, 0)),
            pl.BlockSpec((8, units), lambda i: (0, 0)),
        ],
        out_specs=[
            pl.BlockSpec((width_local, tokens // steps), lambda i: (0, i)),
            pl.BlockSpec((width // steps, units), lambda i: (i, 0)),
            pl.BlockSpec((units // steps, width), lambda i: (i, 0)),
            pl.BlockSpec(memory_space=pltpu.SMEM),
            whole(units),
        ]
        + [whole(width_local)] * 5,
        name="finish",
    )(low_x, low_w, sums)


def body(
    tokens,
    bucket,
    w_in,
    b_in,
    w_out,
    b_out,
    gain_one,
    shift_one,
    gain_two,
    shift_two,
    mask,
    labels,
    cotangent,
):
    shards = lax.axis_size("mp")
    groups = lax.axis_size("dp")
    width_local, token_count = tokens.shape
    units = w_in.shape[1]
    vectors = jnp.stack([b_out, gain_one, shift_one, gain_two, shift_two])
    small = jnp.concatenate(
        [b_in[None, :], jnp.pad(vectors, ((0, 2), (0, units - width_local)))], axis=0
    )
    output, d_x, grads, sums = layer_call(
        shards,
        groups,
        tokens,
        cotangent,
        w_in,
        w_out,
        small,
        bucket,
        labels,
        mask,
    )
    d_tokens, d_w_in, d_w_out, hits, d_b_in, *rest = finish_call(
        8.0 / (token_count * groups), d_x, grads, sums
    )
    return (output, d_tokens, d_w_in, d_b_in, d_w_out, *rest, hits[0, 0])


def solution(mesh):
    in_specs = (
        P("mp", "dp"),
        P("dp"),
        P(None, "mp"),
        P("mp"),
        P("mp", None),
        P("mp"),
        P("mp"),
        P("mp"),
        P("mp"),
        P("mp"),
        P("dp"),
        P("dp"),
        P("mp", "dp"),
    )
    out_specs = (
        P("mp", "dp"),
        P("mp", "dp"),
        P(None, "mp"),
        P("mp"),
        P("mp", None),
        P("mp"),
        P("mp"),
        P("mp"),
        P("mp"),
        P("mp"),
        P(),
    )
    return jax.shard_map(body, mesh=mesh, in_specs=in_specs, out_specs=out_specs, check_vma=False)
```

```python
import functools
import math

import jax
import jax.numpy as jnp
from jax import lax
from jax.experimental import pallas as pl
from jax.experimental.pallas import tpu as pltpu
from jax.sharding import PartitionSpec as P

EPSILON = 1e-05
BF = jnp.bfloat16
F32 = jnp.float32
ANY = pl.BlockSpec(memory_space=pl.ANY)
VMEM = pl.BlockSpec(memory_space=pltpu.VMEM)
SMEM = pl.BlockSpec(memory_space=pltpu.SMEM)
VMEM_LIMIT = 67_000_000


def turns(phase):
    quarter = jnp.floor(phase * 4.0 + 0.5)
    angle = (phase - quarter * 0.25) * (2.0 * math.pi)
    square = angle * angle
    cosine = 1.0 + square * (
        -1 / 2 + square * (1 / 24 + square * (-1 / 720 + square * (1 / 40320)))
    )
    sine = angle * (
        1.0
        + square * (-1 / 6 + square * (1 / 120 + square * (-1 / 5040 + square * (1 / 362880))))
    )
    odd = (quarter == 1.0) | (quarter == 3.0)
    first = jnp.where(odd, sine, cosine)
    second = jnp.where(odd, cosine, sine)
    return (
        jnp.where((quarter == 1.0) | (quarter == 2.0), -first, first),
        jnp.where((quarter == 2.0) | (quarter == 3.0), -second, second),
    )


def dot(left, right, left_dim=1, right_dim=0):
    return lax.dot_general(
        left, right, (((left_dim,), (right_dim,)), ((), ())), preferred_element_type=F32
    )


def remote(source, target, send_sem, recv_sem, device):
    return pltpu.make_async_remote_copy(
        src_ref=source,
        dst_ref=target,
        send_sem=send_sem,
        recv_sem=recv_sem,
        device_id=device,
        device_id_type=pl.DeviceIdType.MESH,
    )


def greet(peers):
    barrier = pltpu.get_barrier_semaphore()
    for peer in peers:
        pl.semaphore_signal(barrier, inc=1, device_id=peer, device_id_type=pl.DeviceIdType.MESH)
    pl.semaphore_wait(barrier, len(peers))


def lanes(values):
    return sum(values[:, i : i + 128] for i in range(128, values.shape[1], 128)) + values[:, :128]


def layer_kernel(
    shards,
    groups,
    tok,
    cot,
    w_in,
    w_out,
    small,
    bucket,
    labels,
    mask,
    out,
    dx,
    d_w,
    sums,
    x_all,
    c_all,
    w_all,
    small_all,
    cos_tab,
    sin_tab,
    cos_h,
    sin_h,
    n_one,
    inv_one,
    hid,
    act,
    slope,
    n_two,
    inv_two,
    grad,
    seq_c,
    seq_s,
    vecs,
    bias,
    acc,
    hits,
    near,
    far,
    turn,
    part_low,
    line_in,
    own_part,
    done_low,
    sums_own,
    sums_mp,
    sums_mid,
    sums_dp,
    load_sem,
    own_sem,
    tok_send,
    tok_recv,
    cot_send,
    cot_recv,
    small_send,
    small_recv,
    wz_send,
    wz_recv,
    wp_send,
    wp_recv,
    ws_send,
    ws_recv,
    out_send,
    out_recv,
    dx_send,
    dx_recv,
    near_send,
    near_recv,
    far_send,
    far_recv,
    turn_send,
    turn_recv,
    line_send,
    line_recv,
    done_send,
    done_recv,
    share_send,
    share_recv,
    mp_send,
    mp_recv,
    dp_send,
    dp_recv,
    near_free,
):
    me = lax.axis_index("mp")
    group = lax.axis_index("dp")
    width_local = tok.shape[0]
    width = width_local * shards
    units = w_in.shape[1]
    chunk = tok.shape[1] // shards
    slots = cos_tab.shape[0]
    slot_length = chunk // slots
    part = 2 * width // groups
    chips = groups // 2
    rows = width
    some = width // 2
    cols = slot_length
    ring = range(1, shards)
    others = range(1, chips)

    inner = jnp.where(me < shards // 2, 1, -1)
    at_end = (me == 0) | (me == shards - 1)

    def mp_peer(step):
        return lax.rem(me + step, shards)

    def inward(step):
        return lax.rem(me + step * inner + shards, shards)

    def dp_peer(step):
        return lax.rem(group + 2 * step, groups)

    core = lax.rem(group, 2)
    sibling = {"dp": group + 1 - 2 * core}
    plane = [{"dp": lax.rem(group + q, groups)} for q in range(1, groups)]
    own_w = [
        pltpu.make_async_copy(w_in, w_all.at[0, :width], own_sem.at[0]),
        pltpu.make_async_copy(w_out, w_all.at[0, width:], own_sem.at[1]),
    ]
    my_cols = pl.ds(pl.multiple_of(me * chunk, 128), chunk)
    my_rows = pl.ds(pl.multiple_of(me * width_local, 16), width_local)
    loads = [
        pltpu.make_async_copy(source, target, load_sem.at[i])
        for i, (source, target) in enumerate(
            [
                (small, small_all.at[0]),
                (tok.at[:, my_cols], x_all.at[my_rows]),
                (cot.at[:, my_cols], c_all.at[my_rows]),
            ]
        )
    ]
    for copy in own_w + loads:
        copy.start()

    greet([{"mp": mp_peer(d)} for d in ring] + plane)

    def exchange(source, target, send, recv, slot, steps=(1, 2, 3)):
        copies = []
        for step in steps:
            peer = inward(step)
            d = lax.rem(peer - me + shards, shards)
            first = pl.multiple_of(peer * chunk + slot * slot_length, 128)
            copies.append(
                remote(
                    source.at[:, pl.ds(first, slot_length)],
                    target.at[
                        my_rows, pl.ds(pl.multiple_of(slot * slot_length, 128), slot_length)
                    ],
                    send.at[slot, d],
                    recv.at[slot, d],
                    {"mp": peer},
                )
            )
        return copies

    small_copies = [
        remote(
            small,
            small_all.at[shards - d],
            small_send.at[d],
            small_recv.at[d],
            {"mp": mp_peer(d)},
        )
        for d in ring
    ]
    for copy in small_copies:
        copy.start()
    for copy in own_w:
        copy.wait()
    my_part = pl.ds(pl.multiple_of(group * part, 16), part)

    def weight_copy(shard, target, send):
        place = lax.rem(shard - me + 2 * shards, shards)
        there = lax.rem(shard - target + 2 * shards, shards)
        return remote(
            w_all.at[place, my_part],
            w_all.at[there, my_part],
            wz_send.at[send],
            wz_recv.at[there],
            {"mp": target},
        )

    def weight_wait(place):
        remote(
            w_all.at[0, my_part],
            w_all.at[place, my_part],
            wz_send.at[0],
            wz_recv.at[place],
            {"mp": inward(1)},
        ).wait_recv()

    near_step = jnp.where(at_end, 1, 3)
    far_step = jnp.where(at_end, 2, 1)
    wz = [weight_copy(me, inward(near_step), 1), weight_copy(me, inward(far_step), 0)]
    for copy in wz:
        copy.start()
    for slot in range(slots):
        for copy in exchange(tok, x_all, tok_send, tok_recv, slot, (1, 2)):
            copy.start()

        @pl.when(at_end)
        def _():
            for copy in exchange(tok, x_all, tok_send, tok_recv, slot, (3,)):
                copy.start()

    def pass_on(step, send):
        return weight_copy(inward(step), inward(3), send)

    side = math.isqrt(chips)
    chip_x, chip_y = lax.rem(group // 2, side), group // 2 // side
    halves = (pl.ds(0, units // 2), pl.ds(units // 2, units // 2))
    arrival = [
        lax.rem(step * inner + shards, shards)
        for step in (1, jnp.where(at_end, 2, 3), jnp.where(at_end, 3, 2))
    ]

    def at_chip(x, y):
        return (lax.rem(y + side, side) * side + lax.rem(x + side, side)) * 2 + core

    def weights_of(n, who, across):
        rows_of = pl.ds(pl.multiple_of(who * part, 16), part)
        return w_all.at[arrival[n], rows_of, across]

    def plane_copy(n, who, across, to, sem):
        at = weights_of(n, who, across)
        return remote(at, at, wp_send.at[n, sem], wp_recv.at[n, sem], to)

    def to_sibling(n, who, across, sem):
        at = weights_of(n, who, across)
        return remote(at, at, ws_send.at[n, sem], ws_recv.at[n, sem], sibling)

    first_plane, second_plane = [[], [], []], [[], [], []]
    first_ws, second_ws = [[], [], []], [[], [], []]
    own_ws = [to_sibling(n, group, pl.ds(0, units), 0) for n in range(3)]
    for n in range(3):
        for h, across in enumerate(halves):
            for p in range(1, side):
                step_x, step_y = (p, 0) if h == 0 else (0, p)
                to = {"dp": at_chip(chip_x + step_x, chip_y + step_y)}
                first_plane[n].append(plane_copy(n, group, across, to, h * chips + p))
                who = at_chip(chip_x - step_x, chip_y - step_y)
                first_ws[n].append(to_sibling(n, who, across, 1 + h * (side - 1) + p - 1))
                for q in range(side):
                    if h == 0:
                        source, to = at_chip(chip_x + q, chip_y), at_chip(chip_x, chip_y + p)
                        who = at_chip(chip_x + q, chip_y - p)
                    else:
                        source, to = at_chip(chip_x, chip_y + q), at_chip(chip_x + p, chip_y)
                        who = at_chip(chip_x - p, chip_y + q)
                    sem = h * chips + side * p + q
                    second_plane[n].append(plane_copy(n, source, across, {"dp": to}, sem))
                    sem = 1 + 2 * (side - 1) + (h * (side - 1) + p - 1) * side + q
                    second_ws[n].append(to_sibling(n, who, across, sem))

    def line_arrived(n):
        weight_wait(arrival[n])
        for copy in first_plane[n]:
            copy.start()
        own_ws[n].start()

    def first_arrived(n):
        for copy in first_plane[n]:
            copy.wait_recv()
        for copy in second_plane[n] + first_ws[n]:
            copy.start()

    def second_arrived(n):
        for copy in second_plane[n]:
            copy.wait_recv()
        for copy in second_ws[n]:
            copy.start()

    turn_rows = min(64, slot_length)

    @pl.loop(0, width // turn_rows)
    def _(i):
        row = pl.ds(pl.multiple_of(i * turn_rows, 16), turn_rows)
        shape = (turn_rows, width)
        product = (
            (lax.broadcasted_iota(jnp.int32, shape, 0) + i * turn_rows)
            * lax.broadcasted_iota(jnp.int32, shape, 1)
        ).astype(F32)
        phase = product * (1.0 / width)
        phase = (product - jnp.floor(phase) * width) * (1.0 / width)
        cosine, sine = turns(phase)
        cos_h[row] = (cosine * (1.0 / math.sqrt(width))).astype(BF)
        sin_h[row] = (sine * (1.0 / math.sqrt(width))).astype(BF)

    @pl.loop(0, slots * slot_length // turn_rows)
    def _(i):
        slot = i // (slot_length // turn_rows)
        first = lax.rem(i, slot_length // turn_rows) * turn_rows
        row = pl.ds(pl.multiple_of(first, 16), turn_rows)
        shape = (turn_rows, slot_length)
        which = bucket[me * slots + slot]
        length = jnp.where(which == 0, slot_length // 4, slot_length // 2)
        length = jnp.where(which == 2, slot_length, length)
        at = lax.broadcasted_iota(jnp.int32, shape, 0) + first
        to = lax.broadcasted_iota(jnp.int32, shape, 1)
        inner = length - 1
        phase = ((at & inner) * (to & inner)) & inner
        scale = jnp.full((1, 1), length, jnp.int32).astype(F32)
        cosine, sine = turns(phase.astype(F32) / scale)
        scale = jnp.where((at ^ to) < length, lax.rsqrt(scale), 0.0)
        cos_tab[slot, row] = (cosine * scale).astype(BF)
        sin_tab[slot, row] = (sine * scale).astype(BF)


    line_arrived(0)

    @pl.when(jnp.logical_not(at_end))
    def _():
        pass_on(1, 2).start()

    line_arrived(1)
    first_arrived(0)
    line_arrived(2)

    @pl.when(jnp.logical_not(at_end))
    def _():
        pass_on(2, 3).start()
        for slot in range(slots):
            for copy in exchange(tok, x_all, tok_send, tok_recv, slot, (3,)):
                copy.start()

    first_arrived(1)
    first_arrived(2)

    for copy in loads:
        copy.wait()
    for copy in small_copies:
        copy.wait_recv()
    for r in range(shards):
        shard = lax.rem(me + r, shards)
        at = pl.ds(pl.multiple_of(shard * width_local, 8), width_local)
        bias[r] = jnp.broadcast_to(small_all[r, 0:1, :units], (128, units)).T
        for i in range(5):
            line = small_all[r, i + 1 : i + 2, : (width_local + 127) // 128 * 128]
            vecs[i, at] = jnp.broadcast_to(line, (128, line.shape[1])).T[:width_local]

    for slot in range(slots):
        at = pl.ds(pl.multiple_of(slot * slot_length, 128), slot_length)
        for copy in exchange(tok, x_all, tok_send, tok_recv, slot):
            copy.wait_recv()

        if slot == slots - 1:
            for later in range(slots):
                for copy in exchange(cot, c_all, cot_send, cot_recv, later):
                    copy.start()

        seq_c[...] = dot(x_all[:, at], cos_tab[slot]).astype(BF)
        seq_s[...] = dot(x_all[:, at], sin_tab[slot]).astype(BF)

        @pl.loop(0, width // rows)
        def _(i):
            row = pl.ds(pl.multiple_of(i * rows, rows), rows)
            mixing = dot(cos_h[row], seq_c[...]) - dot(sin_h[row], seq_s[...])
            n_one[row, at] = x_all[row, at].astype(F32) + mixing

        @pl.loop(0, slot_length // 128)
        def _(i):
            col = pl.ds(pl.multiple_of(slot * slot_length + i * 128, 128), 128)
            value = n_one[:, col]
            centered = value - jnp.mean(value, axis=0, keepdims=True)
            inverse = lax.rsqrt(jnp.mean(centered * centered, axis=0, keepdims=True) + EPSILON)
            normed = centered * inverse
            n_one[:, col] = normed
            inv_one[:, col] = inverse
            hid[:, col] = (normed * vecs[1] + vecs[2]).astype(BF)

        if slot == 0:
            for n in range(3):
                second_arrived(n)

    def first_matmul(r):
        @pl.loop(0, units // some)
        def _(i):
            row = pl.ds(pl.multiple_of(i * some, some), some)
            pre = dot(w_all[r, pl.ds(0, width), row], hid[...], 0, 0) + bias[r, row, 0:1]
            cdf = 0.5 + 0.5 * lax.erf(pre * (1.0 / math.sqrt(2.0)))
            pdf = jnp.exp(-0.5 * pre * pre) * (1.0 / math.sqrt(2.0 * math.pi))
            act[r, row] = (pre * cdf).astype(BF)
            slope[r, row] = (cdf + pre * pdf).astype(BF)

    first_matmul(0)
    ws = sum(first_ws + second_ws, own_ws)
    for copy in ws:
        copy.wait_recv()
    pl.loop(1, shards)(first_matmul)

    hits[...] = jnp.zeros_like(hits)
    acc[...] = jnp.zeros_like(acc)

    @pl.loop(0, chunk // cols)
    def _(i):
        col = pl.ds(pl.multiple_of(i * cols, cols), cols)
        second = n_one[:, col] * vecs[1, :, 0:1] + vecs[2, :, 0:1] + vecs[0, :, 0:1]
        total = dot(w_all[0, pl.ds(width, units)], act[0, :, col], 0, 0)
        for r in ring:
            total += dot(w_all[r, pl.ds(width, units)], act[r, :, col], 0, 0)
        second += total
        centered = second - jnp.mean(second, axis=0, keepdims=True)
        inverse = lax.rsqrt(jnp.mean(centered * centered, axis=0, keepdims=True) + EPSILON)
        normed = centered * inverse
        n_two[:, col] = normed
        inv_two[:, col] = inverse
        result = normed * vecs[3, :, 0:1] + vecs[4, :, 0:1]
        x_all[:, col] = result.astype(BF)
        feature = lax.broadcasted_iota(jnp.int32, (width, cols), 0)
        here = pl.ds(pl.multiple_of(me * chunk + i * cols, cols), cols)
        chosen = feature == labels[here].reshape(1, cols)
        picked = jnp.sum(jnp.where(chosen, result, 0.0), axis=0, keepdims=True)
        soft = 1.0 / (1.0 + jnp.exp(-2.0 * picked))
        hits[...] += jnp.where(mask[here].reshape(1, cols) == 1, soft, 0.0)

    def send_back(source, target, send, recv, first, length):
        copies = []
        for d in ring:
            peer = mp_peer(d)
            copies.append(
                remote(
                    source.at[
                        pl.ds(pl.multiple_of(peer * width_local, 16), width_local),
                        pl.ds(first, length),
                    ],
                    target.at[:, pl.ds(pl.multiple_of(me * chunk + first, 128), length)],
                    send.at[d],
                    recv.at[d],
                    {"mp": peer},
                )
            )
        return copies

    out_copies = [
        send_back(x_all, out, out_send.at[slot], out_recv.at[slot], slot * slot_length, slot_length)
        for slot in range(slots)
    ]
    out_own = pltpu.make_async_copy(x_all.at[my_rows], out.at[:, my_cols], own_sem.at[0])

    cot_copies = sum((exchange(cot, c_all, cot_send, cot_recv, s) for s in range(slots)), [])
    tok_copies = sum((exchange(tok, x_all, tok_send, tok_recv, s) for s in range(slots)), [])
    def norm_two_back(slot):
        col = pl.ds(slot * slot_length, slot_length)
        upstream = c_all[:, col].astype(F32)
        normed = n_two[:, col]
        scaled = upstream * vecs[3, :, 0:1]
        first = jnp.mean(scaled, axis=0, keepdims=True)
        both = jnp.mean(scaled * normed, axis=0, keepdims=True)
        grad_two = inv_two[:, col] * (scaled - first - normed * both)
        n_two[:, col] = grad_two
        low = grad_two.astype(BF)
        grad[:, col] = low
        acc[0] += lanes(low.astype(F32))
        acc[3] += lanes(upstream * normed)
        acc[4] += lanes(upstream)

    def act_back(slot):
        col = pl.ds(slot * slot_length, slot_length)

        @pl.loop(0, shards)
        def _(r):
            grad_act = dot(w_all[r, pl.ds(width, units)], grad[:, col])
            low = (grad_act * slope[r, :, col].astype(F32)).astype(BF)
            slope[r, :, col] = low
            if slot == 0:
                bias[r] = lanes(low.astype(F32))
            else:
                bias[r] += lanes(low.astype(F32))

    def hidden_back(slot):
        col = pl.ds(slot * slot_length, slot_length)
        total = dot(w_all[0, pl.ds(0, width)], slope[0, :, col])
        for r in ring:
            total += dot(w_all[r, pl.ds(0, width)], slope[r, :, col])
        upstream = n_two[:, col] + total
        normed = n_one[:, col]
        scaled = upstream * vecs[1, :, 0:1]
        first = jnp.mean(scaled, axis=0, keepdims=True)
        both = jnp.mean(scaled * normed, axis=0, keepdims=True)
        grad_one = inv_one[:, col] * (scaled - first - normed * both)
        n_two[:, col] = grad_one
        c_all[:, col] = grad_one.astype(BF)
        acc[1] += lanes(upstream * normed)
        acc[2] += lanes(upstream)

    def transform_back(slot):
        at = pl.ds(slot * slot_length, slot_length)

        @pl.loop(0, width // rows)
        def _(i):
            row = pl.ds(pl.multiple_of(i * rows, rows), rows)
            seq_c[row] = dot(cos_h[row], c_all[:, at]).astype(BF)
            seq_s[row] = -dot(sin_h[row], c_all[:, at]).astype(BF)

        @pl.loop(0, width // rows)
        def _(i):
            row = pl.ds(pl.multiple_of(i * rows, rows), rows)
            back = dot(seq_c[row], cos_tab[slot]) + dot(seq_s[row], sin_tab[slot])
            c_all[row, at] = (n_two[row, at] + back).astype(BF)

        copies = send_back(
            c_all, dx, dx_send.at[slot], dx_recv.at[slot], slot * slot_length, slot_length
        )
        copies.append(
            pltpu.make_async_copy(
                c_all.at[my_rows, at],
                dx.at[
                    :,
                    pl.ds(pl.multiple_of(me * chunk + slot * slot_length, 128), slot_length),
                ],
                own_sem.at[1 + slot],
            )
        )
        return copies

    def cotangent_here(slot):
        for copy in exchange(cot, c_all, cot_send, cot_recv, slot):
            copy.wait_recv()
        norm_two_back(slot)

    cotangent_here(0)
    act_back(0)
    hidden_back(0)
    dx_copies = [transform_back(0)]
    for slot in range(1, slots):
        cotangent_here(slot)
    for copy in sum(out_copies, dx_copies[0] + [out_own]):
        copy.start()

    half = width // 2
    split = 1 if half // chips % 16 == 0 else 2
    piece_rows = half * split // chips
    piece_cols = width // split
    keep = pl.ds(pl.multiple_of(core * half, 16), half)
    give = pl.ds(pl.multiple_of((1 - core) * half, 16), half)

    def piece(x, y):
        chip = lax.rem(y, side) * side + lax.rem(x, side)
        first = core * half + chip // split * piece_rows
        return (
            pl.ds(pl.multiple_of(first, 16), piece_rows),
            pl.ds(pl.multiple_of(lax.rem(chip, split) * piece_cols, 128), piece_cols),
        )

    d_out = act.at[:, :, pl.ds(0, width)]
    d_in = w_all.at[:, pl.ds(width, units)]

    def near_copy(x, r):
        source = (d_in, d_out)[x]
        return remote(
            source.at[r, give], near.at[r], near_send.at[x, r], near_recv.at[x, r], sibling
        )

    def far_copies(x, r):
        copies = []
        for p in range(1, side):
            peer = at_chip(
                chip_x + jnp.where(r < 2, p, 0), chip_y + jnp.where(r < 2, 0, p)
            )
            for q in range(side):
                at, across = piece(
                    chip_x + jnp.where(r < 2, p, q), chip_y + jnp.where(r < 2, q, p)
                )
                n = (p - 1) * side + q
                copies.append(
                    remote(
                        (d_in, d_out)[x].at[r, at, across],
                        far.at[x, n, r],
                        far_send.at[x, n, r],
                        far_recv.at[x, n, r],
                        {"dp": peer},
                    )
                )
        return copies

    def turn_copies(x, r):
        copies = []
        for q in range(1, side):
            to = chip_x + jnp.where(r < 2, 0, q), chip_y + jnp.where(r < 2, q, 0)
            at, across = piece(*to)
            copies.append(
                remote(
                    (d_in, d_out)[x].at[r, at, across],
                    turn.at[x, q - 1, r],
                    turn_send.at[x, q - 1, r],
                    turn_recv.at[x, q - 1, r],
                    {"dp": at_chip(*to)},
                )
            )
        return copies

    def add_near(x, r):
        source = (d_in, d_out)[x]
        near_copy(x, r).wait_recv()
        source[r, keep] = (source[r, keep].astype(F32) + near[r].astype(F32)).astype(BF)
        for copy in far_copies(x, r):
            copy.start()

    def in_turn(i):
        return lax.rem(i, 2) * 2 + i // 2

    def reduce_blocks(x, compute):
        @pl.loop(0, shards)
        def _(i):
            compute(in_turn(i))
            near_copy(x, in_turn(i)).start()

            @pl.when(i > 0)
            def _():
                add_near(x, in_turn(i - 1))

        add_near(x, shards - 1)

    def far_sum(x, r, q):
        at, across = piece(
            chip_x + jnp.where(r < 2, 0, q), chip_y + jnp.where(r < 2, q, 0)
        )
        total = (d_in, d_out)[x][r, at, across].astype(F32)
        for p in range(1, side):
            total += far[x, (p - 1) * side + q, r].astype(F32)
        return total

    def add_far(x):
        @pl.loop(0, shards)
        def _(i):
            r = in_turn(i)
            for copy in far_copies(x, r):
                copy.wait_recv()
            for q in range(1, side):
                at, across = piece(
                    chip_x + jnp.where(r < 2, 0, q), chip_y + jnp.where(r < 2, q, 0)
                )
                (d_in, d_out)[x][r, at, across] = far_sum(x, r, q).astype(BF)
            for copy in turn_copies(x, r):
                copy.start()

    my_at, my_across = piece(chip_x, chip_y)

    def add_turn(x):
        @pl.loop(0, shards)
        def _(r):
            for copy in turn_copies(x, r):
                copy.wait_recv()
            total = far_sum(x, r, 0)
            for q in range(1, side):
                total += turn[x, q - 1, r].astype(F32)
            part_low[x, r] = total.astype(BF)

            @pl.when(r == 0)
            def _():
                own_part[x] = total

        @pl.when(at_end)
        def _():
            for step, place in ((2, 2), (3, 3), (1, 0)):
                line_copy(x, step, inward(1), place).start()

        @pl.when(jnp.logical_not(at_end))
        def _():
            line_copy(x, 3, inward(3), 0).start()

    def line_copy(x, step, target, place):
        return remote(
            part_low.at[x, lax.rem(step * inner + shards, shards)],
            line_in.at[x, place],
            line_send.at[x, step],
            line_recv.at[x, place],
            {"mp": target},
        )

    def line_on(x):
        @pl.when(jnp.logical_not(at_end))
        def _():
            for step in (1, 2):
                line_copy(x, step, inward(step), step + 1).wait_recv()
                r = lax.rem(step * inner + shards, shards)
                part_low[x, r] = (
                    part_low[x, r].astype(F32) + line_in[x, step + 1].astype(F32)
                ).astype(BF)
                line_copy(x, step, inward(step), 1).start()

    def add_line(x):
        for place in (0, 1):
            line_copy(x, 1, inward(1), place).wait_recv()
        total = own_part[x] + line_in[x, 0].astype(F32) + line_in[x, 1].astype(F32)
        done_low[x] = total.astype(BF)
        target = d_w.at[x, my_at, my_across]
        copies = [
            remote(
                done_low.at[x], target, done_send.at[x, k], done_recv.at[x, k], {"dp": dp_peer(k)}
            )
            for k in others
        ]
        own = pltpu.make_async_copy(done_low.at[x], target, own_sem.at[1 + slots + x])
        for copy in copies + [own]:
            copy.start()
        return copies, own

    def share(x, copies, own):
        own.wait()
        for copy in copies:
            copy.wait_recv()
        copy = remote(
            d_w.at[x, keep], d_w.at[x, keep], share_send.at[x], share_recv.at[x], sibling
        )
        copy.start()
        return copy

    def second_weight(r):
        @pl.loop(0, units // rows)
        def _(i):
            row = pl.ds(pl.multiple_of(i * rows, rows), rows)
            d_out[r, row] = dot(act[r, row], grad[...], 1, 1).astype(BF)

    second_slots = range(1, slots)
    reduce_blocks(1, second_weight)
    pl.semaphore_signal(
        near_free, inc=1, device_id=sibling, device_id_type=pl.DeviceIdType.MESH
    )
    for slot in second_slots:
        act_back(slot)

    for copy in wz + sum(first_plane + second_plane, ws):
        copy.wait_send()

    @pl.when(jnp.logical_not(at_end))
    def _():
        pass_on(1, 2).wait_send()
        pass_on(2, 3).wait_send()

    def first_weight(r):
        @pl.loop(0, width // rows)
        def _(i):
            row = pl.ds(pl.multiple_of(i * rows, rows), rows)
            d_in[r, row] = dot(hid[row], slope[r], 1, 1).astype(BF)

    pl.semaphore_wait(near_free, 1)
    reduce_blocks(0, first_weight)
    add_far(1)
    for slot in second_slots:
        hidden_back(slot)
        dx_copies.append(transform_back(slot))
    add_turn(1)
    add_far(0)

    lane = lax.broadcasted_iota(jnp.int32, (width_local, 128), 1)
    total_hits = jnp.sum(hits[...], axis=1, keepdims=True)
    for r in range(shards):
        shard = lax.rem(me + r, shards)
        at = pl.ds(pl.multiple_of(shard * width_local, 8), width_local)
        sums_own[r, 0:1] = jnp.broadcast_to(
            jnp.sum(bias[r], axis=1, keepdims=True), (units, 128)
        ).T[0:1]
        line = jnp.where(lane == 6, total_hits, 0.0)
        for i in range(5):
            line += jnp.where(lane == i + 1, jnp.sum(acc[i, at], axis=1, keepdims=True), 0.0)
        spare = (-width_local) % 128
        if spare:
            line = jnp.concatenate([line, jnp.zeros((spare, 128), F32)], axis=0)
        sums_own[r, 1:8, : width_local + spare] = line.T[1:8]
        sums_own[r, 1:8, width_local + spare :] = jnp.zeros((7, units - width_local - spare), F32)
    mp_sums = [
        remote(sums_own.at[d], sums_mp.at[me], mp_send.at[d], mp_recv.at[d], {"mp": mp_peer(d)})
        for d in ring
    ]
    for copy in mp_sums:
        copy.start()
    sums_mp[me] = sums_own[0]

    add_turn(0)
    line_on(1)
    line_on(0)
    for copies in dx_copies[1:]:
        for copy in copies:
            copy.start()
    done_out, own_out = add_line(1)
    for copy in mp_sums:
        copy.wait_recv()
    sums_mid[...] = sum(sums_mp[s] for s in range(shards))
    dp_sums = [
        remote(sums_mid, sums_dp.at[group], dp_send.at[q], dp_recv.at[q], peer)
        for q, peer in enumerate(plane)
    ]
    for copy in dp_sums:
        copy.start()
    sums_dp[group] = sums_mid[...]
    done_in, own_in = add_line(0)
    share_out = share(1, done_out, own_out)
    for copy in dp_sums:
        copy.wait_recv()
    sums[...] = sum(sums_dp[q] for q in range(groups))
    share_in = share(0, done_in, own_in)

    @pl.loop(0, shards)
    def _(r):
        for x in range(2):
            for copy in [near_copy(x, r)] + far_copies(x, r) + turn_copies(x, r):
                copy.wait_send()

            @pl.when(r > 0)
            def _():
                line_copy(x, r, inward(1), 0).wait_send()

    for copy in small_copies + tok_copies + cot_copies + mp_sums + dp_sums:
        copy.wait_send()
    for copy in done_out + done_in:
        copy.wait_send()
    for copy in sum(out_copies + dx_copies, [out_own, share_out, share_in]):
        copy.wait()


def layer_call(shards, groups, tok, cot, w_in, w_out, small, bucket, labels, mask):
    width_local, tokens = tok.shape
    width = width_local * shards
    units = w_in.shape[1]
    chunk = tokens // shards
    slot_length = tokens // bucket.shape[0]
    slots = chunk // slot_length
    cols = slot_length
    dma = pltpu.SemaphoreType.DMA
    chips = groups // 2
    side = math.isqrt(chips)
    split = 1 if width // 2 // chips % 16 == 0 else 2
    piece = (width // 2 * split // chips, width // split)
    return pl.pallas_call(
        functools.partial(layer_kernel, shards, groups),
        out_shape=[
            jax.ShapeDtypeStruct((width_local, tokens), BF),
            jax.ShapeDtypeStruct((width_local, tokens), BF),
            jax.ShapeDtypeStruct((2, width, units), BF),
            jax.ShapeDtypeStruct((8, units), F32),
        ],
        in_specs=[ANY] * 5 + [SMEM, VMEM, VMEM],
        out_specs=[ANY, ANY, ANY, VMEM],
        scratch_shapes=[
            pltpu.VMEM((width, chunk), BF),
            pltpu.VMEM((width, chunk), BF),
            pltpu.VMEM((shards, 2 * width, units), BF),
            pltpu.VMEM((shards, 8, units), F32),
            pltpu.VMEM((slots, slot_length, slot_length), BF),
            pltpu.VMEM((slots, slot_length, slot_length), BF),
            pltpu.VMEM((width, width), BF),
            pltpu.VMEM((width, width), BF),
            pltpu.VMEM((width, chunk), F32),
            pltpu.VMEM((1, chunk), F32),
            pltpu.VMEM((width, chunk), BF),
            pltpu.VMEM((shards, units, chunk), BF),
            pltpu.VMEM((shards, units, chunk), BF),
            pltpu.VMEM((width, chunk), F32),
            pltpu.VMEM((1, chunk), F32),
            pltpu.VMEM((width, chunk), BF),
            pltpu.VMEM((width, slot_length), BF),
            pltpu.VMEM((width, slot_length), BF),
            pltpu.VMEM((5, width, 128), F32),
            pltpu.VMEM((shards, units, 128), F32),
            pltpu.VMEM((5, width, 128), F32),
            pltpu.VMEM((1, cols), F32),
            pltpu.VMEM((shards, width // 2, width), BF),
            pltpu.VMEM((2, (side - 1) * side, shards) + piece, BF),
            pltpu.VMEM((2, side - 1, shards) + piece, BF),
            pltpu.VMEM((2, shards) + piece, BF),
            pltpu.VMEM((2, shards) + piece, BF),
            pltpu.VMEM((2,) + piece, F32),
            pltpu.VMEM((2,) + piece, BF),
            pltpu.VMEM((shards, 8, units), F32),
            pltpu.VMEM((shards, 8, units), F32),
            pltpu.VMEM((8, units), F32),
            pltpu.VMEM((groups, 8, units), F32),
            dma((3,)),
            dma((3 + slots,)),
        ]
        + [dma((slots, shards))] * 4
        + [dma((shards,))] * 4
        + [dma((shards - 1, 2 * chips))] * 4
        + [dma((slots, shards))] * 4
        + [dma((2, shards))] * 2
        + [dma((2, (side - 1) * side, shards))] * 2
        + [dma((2, side - 1, shards))] * 2
        + [dma((2, shards))] * 2
        + [dma((2, chips))] * 2
        + [dma((2,))] * 2
        + [dma((shards,))] * 2
        + [dma((groups,))] * 2
        + [pltpu.SemaphoreType.REGULAR],
        compiler_params=pltpu.CompilerParams(
            collective_id=0, has_side_effects=True, vmem_limit_bytes=VMEM_LIMIT
        ),
        name="layer",
    )(tok, cot, w_in, w_out, small, bucket, labels, mask)


def finish_kernel(scale, low_x, low_w, sums, d_tokens, d_w_in, d_w_out, hits, d_b_in, *rest):
    d_tokens[...] = low_x[...].astype(F32)
    d_w_in[...] = low_w[0].astype(F32)
    d_w_out[...] = low_w[1].astype(F32)

    @pl.when(pl.program_id(0) == 0)
    def _():
        d_b_in[...] = sums[0]
        for i, target in enumerate(rest):
            target[...] = sums[i + 1, : target.shape[0]]
        hits[0, 0] = jnp.sum(sums[6:7, 0:1]) * scale


def finish_call(scale, low_x, low_w, sums):
    width_local, tokens = low_x.shape
    _, width, units = low_w.shape
    steps = 8
    whole = lambda length: pl.BlockSpec((length,), lambda i: (0,))
    return pl.pallas_call(
        functools.partial(finish_kernel, scale),
        grid=(steps,),
        out_shape=[
            jax.ShapeDtypeStruct((width_local, tokens), F32),
            jax.ShapeDtypeStruct((width, units), F32),
            jax.ShapeDtypeStruct((units, width), F32),
            jax.ShapeDtypeStruct((1, 1), F32),
            jax.ShapeDtypeStruct((units,), F32),
        ]
        + [jax.ShapeDtypeStruct((width_local,), F32)] * 5,
        in_specs=[
            pl.BlockSpec((width_local, tokens // steps), lambda i: (0, i)),
            pl.BlockSpec((2, width // steps, units), lambda i: (0, i, 0)),
            pl.BlockSpec((8, units), lambda i: (0, 0)),
        ],
        out_specs=[
            pl.BlockSpec((width_local, tokens // steps), lambda i: (0, i)),
            pl.BlockSpec((width // steps, units), lambda i: (i, 0)),
            pl.BlockSpec((units // steps, width), lambda i: (i, 0)),
            pl.BlockSpec(memory_space=pltpu.SMEM),
            whole(units),
        ]
        + [whole(width_local)] * 5,
        name="finish",
    )(low_x, low_w, sums)


def body(
    tokens,
    bucket,
    w_in,
    b_in,
    w_out,
    b_out,
    gain_one,
    shift_one,
    gain_two,
    shift_two,
    mask,
    labels,
    cotangent,
):
    shards = lax.axis_size("mp")
    groups = lax.axis_size("dp")
    width_local, token_count = tokens.shape
    units = w_in.shape[1]
    vectors = jnp.stack([b_out, gain_one, shift_one, gain_two, shift_two])
    small = jnp.concatenate(
        [b_in[None, :], jnp.pad(vectors, ((0, 2), (0, units - width_local)))], axis=0
    )
    output, d_x, grads, sums = layer_call(
        shards,
        groups,
        tokens,
        cotangent,
        w_in,
        w_out,
        small,
        bucket,
        labels,
        mask,
    )
    d_tokens, d_w_in, d_w_out, hits, d_b_in, *rest = finish_call(
        8.0 / (token_count * groups), d_x, grads, sums
    )
    return (output, d_tokens, d_w_in, d_b_in, d_w_out, *rest, hits[0, 0])


def solution(mesh):
    in_specs = (
        P("mp", "dp"),
        P("dp"),
        P(None, "mp"),
        P("mp"),
        P("mp", None),
        P("mp"),
        P("mp"),
        P("mp"),
        P("mp"),
        P("mp"),
        P("dp"),
        P("dp"),
        P("mp", "dp"),
    )
    out_specs = (
        P("mp", "dp"),
        P("mp", "dp"),
        P(None, "mp"),
        P("mp"),
        P("mp", None),
        P("mp"),
        P("mp"),
        P("mp"),
        P("mp"),
        P("mp"),
        P(),
    )
    return jax.shard_map(body, mesh=mesh, in_specs=in_specs, out_specs=out_specs, check_vma=False)
```

```python
import functools
import math

import jax
import jax.numpy as jnp
from jax import lax
from jax.experimental import pallas as pl
from jax.experimental.pallas import tpu as pltpu
from jax.sharding import PartitionSpec as P

EPSILON = 1e-05
BF = jnp.bfloat16
F32 = jnp.float32
ANY = pl.BlockSpec(memory_space=pl.ANY)
VMEM = pl.BlockSpec(memory_space=pltpu.VMEM)
SMEM = pl.BlockSpec(memory_space=pltpu.SMEM)
VMEM_LIMIT = 67_000_000


def turns(phase):
    quarter = jnp.floor(phase * 4.0 + 0.5)
    angle = (phase - quarter * 0.25) * (2.0 * math.pi)
    square = angle * angle
    cosine = 1.0 + square * (
        -1 / 2 + square * (1 / 24 + square * (-1 / 720 + square * (1 / 40320)))
    )
    sine = angle * (
        1.0
        + square * (-1 / 6 + square * (1 / 120 + square * (-1 / 5040 + square * (1 / 362880))))
    )
    odd = (quarter == 1.0) | (quarter == 3.0)
    first = jnp.where(odd, sine, cosine)
    second = jnp.where(odd, cosine, sine)
    return (
        jnp.where((quarter == 1.0) | (quarter == 2.0), -first, first),
        jnp.where((quarter == 2.0) | (quarter == 3.0), -second, second),
    )


def dot(left, right, left_dim=1, right_dim=0):
    return lax.dot_general(
        left, right, (((left_dim,), (right_dim,)), ((), ())), preferred_element_type=F32
    )


def remote(source, target, send_sem, recv_sem, device):
    return pltpu.make_async_remote_copy(
        src_ref=source,
        dst_ref=target,
        send_sem=send_sem,
        recv_sem=recv_sem,
        device_id=device,
        device_id_type=pl.DeviceIdType.MESH,
    )


def greet(peers):
    barrier = pltpu.get_barrier_semaphore()
    for peer in peers:
        pl.semaphore_signal(barrier, inc=1, device_id=peer, device_id_type=pl.DeviceIdType.MESH)
    pl.semaphore_wait(barrier, len(peers))


def lanes(values):
    return sum(values[:, i : i + 128] for i in range(128, values.shape[1], 128)) + values[:, :128]


def layer_kernel(
    shards,
    groups,
    tok,
    cot,
    w_in,
    w_out,
    vectors,
    bucket,
    labels,
    mask,
    out,
    dx,
    d_w,
    sums,
    x_all,
    c_all,
    w_all,
    small_all,
    cos_tab,
    sin_tab,
    cos_h,
    sin_h,
    n_one,
    inv_one,
    hid,
    act,
    slope,
    n_two,
    inv_two,
    grad,
    seq_c,
    seq_s,
    vecs,
    bias,
    acc,
    hits,
    near,
    far,
    turn,
    part_low,
    line_in,
    own_part,
    done_low,
    sums_own,
    sums_mp,
    sums_mid,
    sums_dp,
    load_sem,
    own_sem,
    tok_send,
    tok_recv,
    cot_send,
    cot_recv,
    small_send,
    small_recv,
    wz_send,
    wz_recv,
    wp_send,
    wp_recv,
    ws_send,
    ws_recv,
    out_send,
    out_recv,
    dx_send,
    dx_recv,
    near_send,
    near_recv,
    far_send,
    far_recv,
    turn_send,
    turn_recv,
    line_send,
    line_recv,
    done_send,
    done_recv,
    share_send,
    share_recv,
    mp_send,
    mp_recv,
    dp_send,
    dp_recv,
    near_free,
):
    me = lax.axis_index("mp")
    group = lax.axis_index("dp")
    width_local = tok.shape[0]
    width = width_local * shards
    units = w_in.shape[1]
    chunk = tok.shape[1] // shards
    slots = cos_tab.shape[0]
    slot_length = chunk // slots
    part = 2 * width // groups
    chips = groups // 2
    rows = width
    some = width // 2
    cols = slot_length
    ring = range(1, shards)
    others = range(1, chips)

    inner = jnp.where(me < shards // 2, 1, -1)
    at_end = (me == 0) | (me == shards - 1)

    def mp_peer(step):
        return lax.rem(me + step, shards)

    def inward(step):
        return lax.rem(me + step * inner + shards, shards)

    def dp_peer(step):
        return lax.rem(group + 2 * step, groups)

    core = lax.rem(group, 2)
    sibling = {"dp": group + 1 - 2 * core}
    plane = [{"dp": lax.rem(group + q, groups)} for q in range(1, groups)]
    own_w = [
        pltpu.make_async_copy(w_in, w_all.at[0, :width], own_sem.at[0]),
        pltpu.make_async_copy(w_out, w_all.at[0, width:], own_sem.at[1]),
    ]
    my_cols = pl.ds(pl.multiple_of(me * chunk, 128), chunk)
    my_rows = pl.ds(pl.multiple_of(me * width_local, 16), width_local)
    loads = [
        pltpu.make_async_copy(source, target, load_sem.at[i])
        for i, (source, target) in enumerate(
            [
                (tok.at[:, my_cols], x_all.at[my_rows]),
                (cot.at[:, my_cols], c_all.at[my_rows]),
            ]
        )
    ]
    for copy in own_w + loads:
        copy.start()

    small_all[0] = jnp.zeros((8, units), F32)
    for i, vector in enumerate(vectors):
        length = vector.shape[0]
        small_all[0, i : i + 1, :length] = vector[...].reshape(1, length)
    greet([{"mp": mp_peer(d)} for d in ring] + plane)

    def exchange(source, target, send, recv, slot, steps=(1, 2, 3)):
        copies = []
        for step in steps:
            peer = inward(step)
            d = lax.rem(peer - me + shards, shards)
            first = pl.multiple_of(peer * chunk + slot * slot_length, 128)
            copies.append(
                remote(
                    source.at[:, pl.ds(first, slot_length)],
                    target.at[
                        my_rows, pl.ds(pl.multiple_of(slot * slot_length, 128), slot_length)
                    ],
                    send.at[slot, d],
                    recv.at[slot, d],
                    {"mp": peer},
                )
            )
        return copies

    small_copies = [
        remote(
            small_all.at[0],
            small_all.at[shards - d],
            small_send.at[d],
            small_recv.at[d],
            {"mp": mp_peer(d)},
        )
        for d in ring
    ]
    for copy in small_copies:
        copy.start()
    for copy in own_w:
        copy.wait()
    my_part = pl.ds(pl.multiple_of(group * part, 16), part)

    def weight_copy(shard, target, send):
        place = lax.rem(shard - me + 2 * shards, shards)
        there = lax.rem(shard - target + 2 * shards, shards)
        return remote(
            w_all.at[place, my_part],
            w_all.at[there, my_part],
            wz_send.at[send],
            wz_recv.at[there],
            {"mp": target},
        )

    def weight_wait(place):
        remote(
            w_all.at[0, my_part],
            w_all.at[place, my_part],
            wz_send.at[0],
            wz_recv.at[place],
            {"mp": inward(1)},
        ).wait_recv()

    near_step = jnp.where(at_end, 1, 3)
    far_step = jnp.where(at_end, 2, 1)
    wz = [weight_copy(me, inward(near_step), 1), weight_copy(me, inward(far_step), 0)]
    for copy in wz:
        copy.start()
    for slot in range(slots):
        for copy in exchange(tok, x_all, tok_send, tok_recv, slot, (1, 2)):
            copy.start()

        @pl.when(at_end)
        def _():
            for copy in exchange(tok, x_all, tok_send, tok_recv, slot, (3,)):
                copy.start()

    def pass_on(step, send):
        return weight_copy(inward(step), inward(3), send)

    side = math.isqrt(chips)
    chip_x, chip_y = lax.rem(group // 2, side), group // 2 // side
    halves = (pl.ds(0, units // 2), pl.ds(units // 2, units // 2))
    arrival = [
        lax.rem(step * inner + shards, shards)
        for step in (1, jnp.where(at_end, 2, 3), jnp.where(at_end, 3, 2))
    ]

    def at_chip(x, y):
        return (lax.rem(y + side, side) * side + lax.rem(x + side, side)) * 2 + core

    def weights_of(n, who, across):
        rows_of = pl.ds(pl.multiple_of(who * part, 16), part)
        return w_all.at[arrival[n], rows_of, across]

    def plane_copy(n, who, across, to, sem):
        at = weights_of(n, who, across)
        return remote(at, at, wp_send.at[n, sem], wp_recv.at[n, sem], to)

    def to_sibling(n, who, across, sem):
        at = weights_of(n, who, across)
        return remote(at, at, ws_send.at[n, sem], ws_recv.at[n, sem], sibling)

    first_plane, second_plane = [[], [], []], [[], [], []]
    first_ws, second_ws = [[], [], []], [[], [], []]
    own_ws = [to_sibling(n, group, pl.ds(0, units), 0) for n in range(3)]
    for n in range(3):
        for h, across in enumerate(halves):
            for p in range(1, side):
                step_x, step_y = (p, 0) if h == 0 else (0, p)
                to = {"dp": at_chip(chip_x + step_x, chip_y + step_y)}
                first_plane[n].append(plane_copy(n, group, across, to, h * chips + p))
                who = at_chip(chip_x - step_x, chip_y - step_y)
                first_ws[n].append(to_sibling(n, who, across, 1 + h * (side - 1) + p - 1))
                for q in range(side):
                    if h == 0:
                        source, to = at_chip(chip_x + q, chip_y), at_chip(chip_x, chip_y + p)
                        who = at_chip(chip_x + q, chip_y - p)
                    else:
                        source, to = at_chip(chip_x, chip_y + q), at_chip(chip_x + p, chip_y)
                        who = at_chip(chip_x - p, chip_y + q)
                    sem = h * chips + side * p + q
                    second_plane[n].append(plane_copy(n, source, across, {"dp": to}, sem))
                    sem = 1 + 2 * (side - 1) + (h * (side - 1) + p - 1) * side + q
                    second_ws[n].append(to_sibling(n, who, across, sem))

    def line_arrived(n):
        weight_wait(arrival[n])
        for copy in first_plane[n]:
            copy.start()
        own_ws[n].start()

    def first_arrived(n):
        for copy in first_plane[n]:
            copy.wait_recv()
        for copy in second_plane[n] + first_ws[n]:
            copy.start()

    def second_arrived(n):
        for copy in second_plane[n]:
            copy.wait_recv()
        for copy in second_ws[n]:
            copy.start()

    turn_rows = min(64, slot_length)

    @pl.loop(0, width // turn_rows)
    def _(i):
        row = pl.ds(pl.multiple_of(i * turn_rows, 16), turn_rows)
        shape = (turn_rows, width)
        product = (
            (lax.broadcasted_iota(jnp.int32, shape, 0) + i * turn_rows)
            * lax.broadcasted_iota(jnp.int32, shape, 1)
        ).astype(F32)
        phase = product * (1.0 / width)
        phase = (product - jnp.floor(phase) * width) * (1.0 / width)
        cosine, sine = turns(phase)
        cos_h[row] = (cosine * (1.0 / math.sqrt(width))).astype(BF)
        sin_h[row] = (sine * (1.0 / math.sqrt(width))).astype(BF)

    @pl.loop(0, slots * slot_length // turn_rows)
    def _(i):
        slot = i // (slot_length // turn_rows)
        first = lax.rem(i, slot_length // turn_rows) * turn_rows
        row = pl.ds(pl.multiple_of(first, 16), turn_rows)
        shape = (turn_rows, slot_length)
        which = bucket[me * slots + slot]
        length = jnp.where(which == 0, slot_length // 4, slot_length // 2)
        length = jnp.where(which == 2, slot_length, length)
        at = lax.broadcasted_iota(jnp.int32, shape, 0) + first
        to = lax.broadcasted_iota(jnp.int32, shape, 1)
        inner = length - 1
        phase = ((at & inner) * (to & inner)) & inner
        scale = jnp.full((1, 1), length, jnp.int32).astype(F32)
        cosine, sine = turns(phase.astype(F32) / scale)
        scale = jnp.where((at ^ to) < length, lax.rsqrt(scale), 0.0)
        cos_tab[slot, row] = (cosine * scale).astype(BF)
        sin_tab[slot, row] = (sine * scale).astype(BF)


    line_arrived(0)

    @pl.when(jnp.logical_not(at_end))
    def _():
        pass_on(1, 2).start()

    line_arrived(1)
    first_arrived(0)
    line_arrived(2)

    @pl.when(jnp.logical_not(at_end))
    def _():
        pass_on(2, 3).start()
        for slot in range(slots):
            for copy in exchange(tok, x_all, tok_send, tok_recv, slot, (3,)):
                copy.start()

    first_arrived(1)
    first_arrived(2)

    for copy in loads:
        copy.wait()
    for copy in small_copies:
        copy.wait_recv()
    for r in range(shards):
        shard = lax.rem(me + r, shards)
        at = pl.ds(pl.multiple_of(shard * width_local, 8), width_local)
        bias[r] = jnp.broadcast_to(small_all[r, 0:1, :units], (128, units)).T
        for i in range(5):
            line = small_all[r, i + 1 : i + 2, : (width_local + 127) // 128 * 128]
            vecs[i, at] = jnp.broadcast_to(line, (128, line.shape[1])).T[:width_local]

    for slot in range(slots):
        at = pl.ds(pl.multiple_of(slot * slot_length, 128), slot_length)
        for copy in exchange(tok, x_all, tok_send, tok_recv, slot):
            copy.wait_recv()

        if slot == slots - 1:
            for later in range(slots):
                for copy in exchange(cot, c_all, cot_send, cot_recv, later):
                    copy.start()

        seq_c[...] = dot(x_all[:, at], cos_tab[slot]).astype(BF)
        seq_s[...] = dot(x_all[:, at], sin_tab[slot]).astype(BF)

        @pl.loop(0, width // rows)
        def _(i):
            row = pl.ds(pl.multiple_of(i * rows, rows), rows)
            mixing = dot(cos_h[row], seq_c[...]) - dot(sin_h[row], seq_s[...])
            n_one[row, at] = x_all[row, at].astype(F32) + mixing

        @pl.loop(0, slot_length // 128)
        def _(i):
            col = pl.ds(pl.multiple_of(slot * slot_length + i * 128, 128), 128)
            value = n_one[:, col]
            centered = value - jnp.mean(value, axis=0, keepdims=True)
            inverse = lax.rsqrt(jnp.mean(centered * centered, axis=0, keepdims=True) + EPSILON)
            normed = centered * inverse
            n_one[:, col] = normed
            inv_one[:, col] = inverse
            hid[:, col] = (normed * vecs[1] + vecs[2]).astype(BF)

        if slot == 0:
            for n in range(3):
                second_arrived(n)

    def first_matmul(r):
        @pl.loop(0, units // some)
        def _(i):
            row = pl.ds(pl.multiple_of(i * some, some), some)
            pre = dot(w_all[r, pl.ds(0, width), row], hid[...], 0, 0) + bias[r, row, 0:1]
            cdf = 0.5 + 0.5 * lax.erf(pre * (1.0 / math.sqrt(2.0)))
            pdf = jnp.exp(-0.5 * pre * pre) * (1.0 / math.sqrt(2.0 * math.pi))
            act[r, row] = (pre * cdf).astype(BF)
            slope[r, row] = (cdf + pre * pdf).astype(BF)

    first_matmul(0)
    ws = sum(first_ws + second_ws, own_ws)
    for copy in ws:
        copy.wait_recv()
    pl.loop(1, shards)(first_matmul)

    hits[...] = jnp.zeros_like(hits)
    acc[...] = jnp.zeros_like(acc)

    @pl.loop(0, chunk // cols)
    def _(i):
        col = pl.ds(pl.multiple_of(i * cols, cols), cols)
        second = n_one[:, col] * vecs[1, :, 0:1] + vecs[2, :, 0:1] + vecs[0, :, 0:1]
        total = dot(w_all[0, pl.ds(width, units)], act[0, :, col], 0, 0)
        for r in ring:
            total += dot(w_all[r, pl.ds(width, units)], act[r, :, col], 0, 0)
        second += total
        centered = second - jnp.mean(second, axis=0, keepdims=True)
        inverse = lax.rsqrt(jnp.mean(centered * centered, axis=0, keepdims=True) + EPSILON)
        normed = centered * inverse
        n_two[:, col] = normed
        inv_two[:, col] = inverse
        result = normed * vecs[3, :, 0:1] + vecs[4, :, 0:1]
        x_all[:, col] = result.astype(BF)
        feature = lax.broadcasted_iota(jnp.int32, (width, cols), 0)
        here = pl.ds(pl.multiple_of(me * chunk + i * cols, cols), cols)
        chosen = feature == labels[here].reshape(1, cols)
        picked = jnp.sum(jnp.where(chosen, result, 0.0), axis=0, keepdims=True)
        soft = 1.0 / (1.0 + jnp.exp(-2.0 * picked))
        hits[...] += jnp.where(mask[here].reshape(1, cols) == 1, soft, 0.0)

    def send_back(source, target, send, recv, first, length):
        copies = []
        for d in ring:
            peer = mp_peer(d)
            copies.append(
                remote(
                    source.at[
                        pl.ds(pl.multiple_of(peer * width_local, 16), width_local),
                        pl.ds(first, length),
                    ],
                    target.at[:, pl.ds(pl.multiple_of(me * chunk + first, 128), length)],
                    send.at[d],
                    recv.at[d],
                    {"mp": peer},
                )
            )
        return copies

    out_copies = [
        send_back(x_all, out, out_send.at[slot], out_recv.at[slot], slot * slot_length, slot_length)
        for slot in range(slots)
    ]
    out_own = pltpu.make_async_copy(x_all.at[my_rows], out.at[:, my_cols], own_sem.at[0])

    cot_copies = sum((exchange(cot, c_all, cot_send, cot_recv, s) for s in range(slots)), [])
    tok_copies = sum((exchange(tok, x_all, tok_send, tok_recv, s) for s in range(slots)), [])
    def norm_two_back(slot):
        col = pl.ds(slot * slot_length, slot_length)
        upstream = c_all[:, col].astype(F32)
        normed = n_two[:, col]
        scaled = upstream * vecs[3, :, 0:1]
        first = jnp.mean(scaled, axis=0, keepdims=True)
        both = jnp.mean(scaled * normed, axis=0, keepdims=True)
        grad_two = inv_two[:, col] * (scaled - first - normed * both)
        n_two[:, col] = grad_two
        low = grad_two.astype(BF)
        grad[:, col] = low
        acc[0] += lanes(low.astype(F32))
        acc[3] += lanes(upstream * normed)
        acc[4] += lanes(upstream)

    def act_back(slot):
        col = pl.ds(slot * slot_length, slot_length)

        @pl.loop(0, shards)
        def _(r):
            grad_act = dot(w_all[r, pl.ds(width, units)], grad[:, col])
            low = (grad_act * slope[r, :, col].astype(F32)).astype(BF)
            slope[r, :, col] = low
            if slot == 0:
                bias[r] = lanes(low.astype(F32))
            else:
                bias[r] += lanes(low.astype(F32))

    def hidden_back(slot):
        col = pl.ds(slot * slot_length, slot_length)
        total = dot(w_all[0, pl.ds(0, width)], slope[0, :, col])
        for r in ring:
            total += dot(w_all[r, pl.ds(0, width)], slope[r, :, col])
        upstream = n_two[:, col] + total
        normed = n_one[:, col]
        scaled = upstream * vecs[1, :, 0:1]
        first = jnp.mean(scaled, axis=0, keepdims=True)
        both = jnp.mean(scaled * normed, axis=0, keepdims=True)
        grad_one = inv_one[:, col] * (scaled - first - normed * both)
        n_two[:, col] = grad_one
        c_all[:, col] = grad_one.astype(BF)
        acc[1] += lanes(upstream * normed)
        acc[2] += lanes(upstream)

    def transform_back(slot):
        at = pl.ds(slot * slot_length, slot_length)

        @pl.loop(0, width // rows)
        def _(i):
            row = pl.ds(pl.multiple_of(i * rows, rows), rows)
            seq_c[row] = dot(cos_h[row], c_all[:, at]).astype(BF)
            seq_s[row] = -dot(sin_h[row], c_all[:, at]).astype(BF)

        @pl.loop(0, width // rows)
        def _(i):
            row = pl.ds(pl.multiple_of(i * rows, rows), rows)
            back = dot(seq_c[row], cos_tab[slot]) + dot(seq_s[row], sin_tab[slot])
            c_all[row, at] = (n_two[row, at] + back).astype(BF)

        copies = send_back(
            c_all, dx, dx_send.at[slot], dx_recv.at[slot], slot * slot_length, slot_length
        )
        copies.append(
            pltpu.make_async_copy(
                c_all.at[my_rows, at],
                dx.at[
                    :,
                    pl.ds(pl.multiple_of(me * chunk + slot * slot_length, 128), slot_length),
                ],
                own_sem.at[1 + slot],
            )
        )
        return copies

    def cotangent_here(slot):
        for copy in exchange(cot, c_all, cot_send, cot_recv, slot):
            copy.wait_recv()
        norm_two_back(slot)

    cotangent_here(0)
    act_back(0)
    hidden_back(0)
    dx_copies = [transform_back(0)]
    for slot in range(1, slots):
        cotangent_here(slot)
    for copy in sum(out_copies, dx_copies[0] + [out_own]):
        copy.start()

    half = width // 2
    split = 1 if half // chips % 16 == 0 else 2
    piece_rows = half * split // chips
    piece_cols = width // split
    keep = pl.ds(pl.multiple_of(core * half, 16), half)
    give = pl.ds(pl.multiple_of((1 - core) * half, 16), half)

    def piece(x, y):
        chip = lax.rem(y, side) * side + lax.rem(x, side)
        first = core * half + chip // split * piece_rows
        return (
            pl.ds(pl.multiple_of(first, 16), piece_rows),
            pl.ds(pl.multiple_of(lax.rem(chip, split) * piece_cols, 128), piece_cols),
        )

    d_out = act.at[:, :, pl.ds(0, width)]
    d_in = w_all.at[:, pl.ds(width, units)]

    def near_copy(x, r):
        source = (d_in, d_out)[x]
        return remote(
            source.at[r, give], near.at[r], near_send.at[x, r], near_recv.at[x, r], sibling
        )

    def far_copies(x, r):
        copies = []
        for p in range(1, side):
            peer = at_chip(
                chip_x + jnp.where(r < 2, p, 0), chip_y + jnp.where(r < 2, 0, p)
            )
            for q in range(side):
                at, across = piece(
                    chip_x + jnp.where(r < 2, p, q), chip_y + jnp.where(r < 2, q, p)
                )
                n = (p - 1) * side + q
                copies.append(
                    remote(
                        (d_in, d_out)[x].at[r, at, across],
                        far.at[x, n, r],
                        far_send.at[x, n, r],
                        far_recv.at[x, n, r],
                        {"dp": peer},
                    )
                )
        return copies

    def turn_copies(x, r):
        copies = []
        for q in range(1, side):
            to = chip_x + jnp.where(r < 2, 0, q), chip_y + jnp.where(r < 2, q, 0)
            at, across = piece(*to)
            copies.append(
                remote(
                    (d_in, d_out)[x].at[r, at, across],
                    turn.at[x, q - 1, r],
                    turn_send.at[x, q - 1, r],
                    turn_recv.at[x, q - 1, r],
                    {"dp": at_chip(*to)},
                )
            )
        return copies

    def add_near(x, r):
        source = (d_in, d_out)[x]
        near_copy(x, r).wait_recv()
        source[r, keep] = (source[r, keep].astype(F32) + near[r].astype(F32)).astype(BF)
        for copy in far_copies(x, r):
            copy.start()

    def in_turn(i):
        return lax.rem(i, 2) * 2 + i // 2

    def reduce_blocks(x, compute):
        @pl.loop(0, shards)
        def _(i):
            compute(in_turn(i))
            near_copy(x, in_turn(i)).start()

            @pl.when(i > 0)
            def _():
                add_near(x, in_turn(i - 1))

        add_near(x, shards - 1)

    def far_sum(x, r, q):
        at, across = piece(
            chip_x + jnp.where(r < 2, 0, q), chip_y + jnp.where(r < 2, q, 0)
        )
        total = (d_in, d_out)[x][r, at, across].astype(F32)
        for p in range(1, side):
            total += far[x, (p - 1) * side + q, r].astype(F32)
        return total

    def add_far(x):
        @pl.loop(0, shards)
        def _(i):
            r = in_turn(i)
            for copy in far_copies(x, r):
                copy.wait_recv()
            for q in range(1, side):
                at, across = piece(
                    chip_x + jnp.where(r < 2, 0, q), chip_y + jnp.where(r < 2, q, 0)
                )
                (d_in, d_out)[x][r, at, across] = far_sum(x, r, q).astype(BF)
            for copy in turn_copies(x, r):
                copy.start()

    my_at, my_across = piece(chip_x, chip_y)

    def add_turn(x):
        @pl.loop(0, shards)
        def _(r):
            for copy in turn_copies(x, r):
                copy.wait_recv()
            total = far_sum(x, r, 0)
            for q in range(1, side):
                total += turn[x, q - 1, r].astype(F32)
            part_low[x, r] = total.astype(BF)

            @pl.when(r == 0)
            def _():
                own_part[x] = total

        @pl.when(at_end)
        def _():
            for step, place in ((2, 2), (3, 3), (1, 0)):
                line_copy(x, step, inward(1), place).start()

        @pl.when(jnp.logical_not(at_end))
        def _():
            line_copy(x, 3, inward(3), 0).start()

    def line_copy(x, step, target, place):
        return remote(
            part_low.at[x, lax.rem(step * inner + shards, shards)],
            line_in.at[x, place],
            line_send.at[x, step],
            line_recv.at[x, place],
            {"mp": target},
        )

    def line_on(x):
        @pl.when(jnp.logical_not(at_end))
        def _():
            for step in (1, 2):
                line_copy(x, step, inward(step), step + 1).wait_recv()
                r = lax.rem(step * inner + shards, shards)
                part_low[x, r] = (
                    part_low[x, r].astype(F32) + line_in[x, step + 1].astype(F32)
                ).astype(BF)
                line_copy(x, step, inward(step), 1).start()

    def add_line(x):
        for place in (0, 1):
            line_copy(x, 1, inward(1), place).wait_recv()
        total = own_part[x] + line_in[x, 0].astype(F32) + line_in[x, 1].astype(F32)
        done_low[x] = total.astype(BF)
        target = d_w.at[x, my_at, my_across]
        copies = [
            remote(
                done_low.at[x], target, done_send.at[x, k], done_recv.at[x, k], {"dp": dp_peer(k)}
            )
            for k in others
        ]
        own = pltpu.make_async_copy(done_low.at[x], target, own_sem.at[1 + slots + x])
        for copy in copies + [own]:
            copy.start()
        return copies, own

    def share(x, copies, own):
        own.wait()
        for copy in copies:
            copy.wait_recv()
        copy = remote(
            d_w.at[x, keep], d_w.at[x, keep], share_send.at[x], share_recv.at[x], sibling
        )
        copy.start()
        return copy

    def second_weight(r):
        @pl.loop(0, units // rows)
        def _(i):
            row = pl.ds(pl.multiple_of(i * rows, rows), rows)
            d_out[r, row] = dot(act[r, row], grad[...], 1, 1).astype(BF)

    second_slots = range(1, slots)
    reduce_blocks(1, second_weight)
    pl.semaphore_signal(
        near_free, inc=1, device_id=sibling, device_id_type=pl.DeviceIdType.MESH
    )
    for slot in second_slots:
        act_back(slot)

    for copy in wz + sum(first_plane + second_plane, ws):
        copy.wait_send()

    @pl.when(jnp.logical_not(at_end))
    def _():
        pass_on(1, 2).wait_send()
        pass_on(2, 3).wait_send()

    def first_weight(r):
        @pl.loop(0, width // rows)
        def _(i):
            row = pl.ds(pl.multiple_of(i * rows, rows), rows)
            d_in[r, row] = dot(hid[row], slope[r], 1, 1).astype(BF)

    pl.semaphore_wait(near_free, 1)
    reduce_blocks(0, first_weight)
    add_far(1)
    for slot in second_slots:
        hidden_back(slot)
        dx_copies.append(transform_back(slot))
    add_turn(1)
    add_far(0)

    lane = lax.broadcasted_iota(jnp.int32, (width_local, 128), 1)
    total_hits = jnp.sum(hits[...], axis=1, keepdims=True)
    for r in range(shards):
        shard = lax.rem(me + r, shards)
        at = pl.ds(pl.multiple_of(shard * width_local, 8), width_local)
        sums_own[r, 0:1] = jnp.broadcast_to(
            jnp.sum(bias[r], axis=1, keepdims=True), (units, 128)
        ).T[0:1]
        line = jnp.where(lane == 6, total_hits, 0.0)
        for i in range(5):
            line += jnp.where(lane == i + 1, jnp.sum(acc[i, at], axis=1, keepdims=True), 0.0)
        spare = (-width_local) % 128
        if spare:
            line = jnp.concatenate([line, jnp.zeros((spare, 128), F32)], axis=0)
        sums_own[r, 1:8, : width_local + spare] = line.T[1:8]
        sums_own[r, 1:8, width_local + spare :] = jnp.zeros((7, units - width_local - spare), F32)
    mp_sums = [
        remote(sums_own.at[d], sums_mp.at[me], mp_send.at[d], mp_recv.at[d], {"mp": mp_peer(d)})
        for d in ring
    ]
    for copy in mp_sums:
        copy.start()
    sums_mp[me] = sums_own[0]

    add_turn(0)
    line_on(1)
    line_on(0)
    for copies in dx_copies[1:]:
        for copy in copies:
            copy.start()
    done_out, own_out = add_line(1)
    for copy in mp_sums:
        copy.wait_recv()
    sums_mid[...] = sum(sums_mp[s] for s in range(shards))
    dp_sums = [
        remote(sums_mid, sums_dp.at[group], dp_send.at[q], dp_recv.at[q], peer)
        for q, peer in enumerate(plane)
    ]
    for copy in dp_sums:
        copy.start()
    sums_dp[group] = sums_mid[...]
    done_in, own_in = add_line(0)
    share_out = share(1, done_out, own_out)
    for copy in dp_sums:
        copy.wait_recv()
    sums[...] = sum(sums_dp[q] for q in range(groups))
    share_in = share(0, done_in, own_in)

    @pl.loop(0, shards)
    def _(r):
        for x in range(2):
            for copy in [near_copy(x, r)] + far_copies(x, r) + turn_copies(x, r):
                copy.wait_send()

            @pl.when(r > 0)
            def _():
                line_copy(x, r, inward(1), 0).wait_send()

    for copy in small_copies + tok_copies + cot_copies + mp_sums + dp_sums:
        copy.wait_send()
    for copy in done_out + done_in:
        copy.wait_send()
    for copy in sum(out_copies + dx_copies, [out_own, share_out, share_in]):
        copy.wait()


def layer_call(shards, groups, tok, cot, w_in, w_out, vectors, bucket, labels, mask):
    width_local, tokens = tok.shape
    width = width_local * shards
    units = w_in.shape[1]
    chunk = tokens // shards
    slot_length = tokens // bucket.shape[0]
    slots = chunk // slot_length
    cols = slot_length
    dma = pltpu.SemaphoreType.DMA
    chips = groups // 2
    side = math.isqrt(chips)
    split = 1 if width // 2 // chips % 16 == 0 else 2
    piece = (width // 2 * split // chips, width // split)
    return pl.pallas_call(
        functools.partial(layer_kernel, shards, groups),
        out_shape=[
            jax.ShapeDtypeStruct((width_local, tokens), BF),
            jax.ShapeDtypeStruct((width_local, tokens), BF),
            jax.ShapeDtypeStruct((2, width, units), BF),
            jax.ShapeDtypeStruct((8, units), F32),
        ],
        in_specs=[ANY] * 4 + [[VMEM] * 6, SMEM, VMEM, VMEM],
        out_specs=[ANY, ANY, ANY, VMEM],
        scratch_shapes=[
            pltpu.VMEM((width, chunk), BF),
            pltpu.VMEM((width, chunk), BF),
            pltpu.VMEM((shards, 2 * width, units), BF),
            pltpu.VMEM((shards, 8, units), F32),
            pltpu.VMEM((slots, slot_length, slot_length), BF),
            pltpu.VMEM((slots, slot_length, slot_length), BF),
            pltpu.VMEM((width, width), BF),
            pltpu.VMEM((width, width), BF),
            pltpu.VMEM((width, chunk), F32),
            pltpu.VMEM((1, chunk), F32),
            pltpu.VMEM((width, chunk), BF),
            pltpu.VMEM((shards, units, chunk), BF),
            pltpu.VMEM((shards, units, chunk), BF),
            pltpu.VMEM((width, chunk), F32),
            pltpu.VMEM((1, chunk), F32),
            pltpu.VMEM((width, chunk), BF),
            pltpu.VMEM((width, slot_length), BF),
            pltpu.VMEM((width, slot_length), BF),
            pltpu.VMEM((5, width, 128), F32),
            pltpu.VMEM((shards, units, 128), F32),
            pltpu.VMEM((5, width, 128), F32),
            pltpu.VMEM((1, cols), F32),
            pltpu.VMEM((shards, width // 2, width), BF),
            pltpu.VMEM((2, (side - 1) * side, shards) + piece, BF),
            pltpu.VMEM((2, side - 1, shards) + piece, BF),
            pltpu.VMEM((2, shards) + piece, BF),
            pltpu.VMEM((2, shards) + piece, BF),
            pltpu.VMEM((2,) + piece, F32),
            pltpu.VMEM((2,) + piece, BF),
            pltpu.VMEM((shards, 8, units), F32),
            pltpu.VMEM((shards, 8, units), F32),
            pltpu.VMEM((8, units), F32),
            pltpu.VMEM((groups, 8, units), F32),
            dma((2,)),
            dma((3 + slots,)),
        ]
        + [dma((slots, shards))] * 4
        + [dma((shards,))] * 4
        + [dma((shards - 1, 2 * chips))] * 4
        + [dma((slots, shards))] * 4
        + [dma((2, shards))] * 2
        + [dma((2, (side - 1) * side, shards))] * 2
        + [dma((2, side - 1, shards))] * 2
        + [dma((2, shards))] * 2
        + [dma((2, chips))] * 2
        + [dma((2,))] * 2
        + [dma((shards,))] * 2
        + [dma((groups,))] * 2
        + [pltpu.SemaphoreType.REGULAR],
        compiler_params=pltpu.CompilerParams(
            collective_id=0, has_side_effects=True, vmem_limit_bytes=VMEM_LIMIT
        ),
        name="layer",
    )(tok, cot, w_in, w_out, vectors, bucket, labels, mask)


def finish_kernel(scale, low_x, low_w, sums, d_tokens, d_w_in, d_w_out, hits, d_b_in, *rest):
    d_tokens[...] = low_x[...].astype(F32)
    d_w_in[...] = low_w[0].astype(F32)
    d_w_out[...] = low_w[1].astype(F32)

    @pl.when(pl.program_id(0) == 0)
    def _():
        d_b_in[...] = sums[0]
        for i, target in enumerate(rest):
            target[...] = sums[i + 1, : target.shape[0]]
        hits[0, 0] = jnp.sum(sums[6:7, 0:1]) * scale


def finish_call(scale, low_x, low_w, sums):
    width_local, tokens = low_x.shape
    _, width, units = low_w.shape
    steps = 4
    whole = lambda length: pl.BlockSpec((length,), lambda i: (0,))
    return pl.pallas_call(
        functools.partial(finish_kernel, scale),
        grid=(steps,),
        out_shape=[
            jax.ShapeDtypeStruct((width_local, tokens), F32),
            jax.ShapeDtypeStruct((width, units), F32),
            jax.ShapeDtypeStruct((units, width), F32),
            jax.ShapeDtypeStruct((1, 1), F32),
            jax.ShapeDtypeStruct((units,), F32),
        ]
        + [jax.ShapeDtypeStruct((width_local,), F32)] * 5,
        in_specs=[
            pl.BlockSpec((width_local, tokens // steps), lambda i: (0, i)),
            pl.BlockSpec((2, width // steps, units), lambda i: (0, i, 0)),
            pl.BlockSpec((8, units), lambda i: (0, 0)),
        ],
        out_specs=[
            pl.BlockSpec((width_local, tokens // steps), lambda i: (0, i)),
            pl.BlockSpec((width // steps, units), lambda i: (i, 0)),
            pl.BlockSpec((units // steps, width), lambda i: (i, 0)),
            pl.BlockSpec(memory_space=pltpu.SMEM),
            whole(units),
        ]
        + [whole(width_local)] * 5,
        name="finish",
    )(low_x, low_w, sums)


def body(
    tokens,
    bucket,
    w_in,
    b_in,
    w_out,
    b_out,
    gain_one,
    shift_one,
    gain_two,
    shift_two,
    mask,
    labels,
    cotangent,
):
    shards = lax.axis_size("mp")
    groups = lax.axis_size("dp")
    width_local, token_count = tokens.shape
    vectors = [b_in, b_out, gain_one, shift_one, gain_two, shift_two]
    output, d_x, grads, sums = layer_call(
        shards,
        groups,
        tokens,
        cotangent,
        w_in,
        w_out,
        vectors,
        bucket,
        labels,
        mask,
    )
    d_tokens, d_w_in, d_w_out, hits, d_b_in, *rest = finish_call(
        8.0 / (token_count * groups), d_x, grads, sums
    )
    return (output, d_tokens, d_w_in, d_b_in, d_w_out, *rest, hits[0, 0])


def solution(mesh):
    in_specs = (
        P("mp", "dp"),
        P("dp"),
        P(None, "mp"),
        P("mp"),
        P("mp", None),
        P("mp"),
        P("mp"),
        P("mp"),
        P("mp"),
        P("mp"),
        P("dp"),
        P("dp"),
        P("mp", "dp"),
    )
    out_specs = (
        P("mp", "dp"),
        P("mp", "dp"),
        P(None, "mp"),
        P("mp"),
        P("mp", None),
        P("mp"),
        P("mp"),
        P("mp"),
        P("mp"),
        P("mp"),
        P(),
    )
    return jax.shard_map(body, mesh=mesh, in_specs=in_specs, out_specs=out_specs, check_vma=False)
```

```python
import functools
import math

import jax
import jax.numpy as jnp
from jax import lax
from jax.experimental import pallas as pl
from jax.experimental.pallas import tpu as pltpu
from jax.sharding import PartitionSpec as P

EPSILON = 1e-05
BF = jnp.bfloat16
F32 = jnp.float32
ANY = pl.BlockSpec(memory_space=pl.ANY)
VMEM = pl.BlockSpec(memory_space=pltpu.VMEM)
SMEM = pl.BlockSpec(memory_space=pltpu.SMEM)
VMEM_LIMIT = 67_000_000


def turns(phase):
    quarter = jnp.floor(phase * 4.0 + 0.5)
    angle = (phase - quarter * 0.25) * (2.0 * math.pi)
    square = angle * angle
    cosine = 1.0 + square * (
        -1 / 2 + square * (1 / 24 + square * (-1 / 720 + square * (1 / 40320)))
    )
    sine = angle * (
        1.0
        + square * (-1 / 6 + square * (1 / 120 + square * (-1 / 5040 + square * (1 / 362880))))
    )
    odd = (quarter == 1.0) | (quarter == 3.0)
    first = jnp.where(odd, sine, cosine)
    second = jnp.where(odd, cosine, sine)
    return (
        jnp.where((quarter == 1.0) | (quarter == 2.0), -first, first),
        jnp.where((quarter == 2.0) | (quarter == 3.0), -second, second),
    )


def dot(left, right, left_dim=1, right_dim=0):
    return lax.dot_general(
        left, right, (((left_dim,), (right_dim,)), ((), ())), preferred_element_type=F32
    )


def remote(source, target, send_sem, recv_sem, device):
    return pltpu.make_async_remote_copy(
        src_ref=source,
        dst_ref=target,
        send_sem=send_sem,
        recv_sem=recv_sem,
        device_id=device,
        device_id_type=pl.DeviceIdType.MESH,
    )


def greet(peers):
    barrier = pltpu.get_barrier_semaphore()
    for peer in peers:
        pl.semaphore_signal(barrier, inc=1, device_id=peer, device_id_type=pl.DeviceIdType.MESH)
    pl.semaphore_wait(barrier, len(peers))


def lanes(values):
    return sum(values[:, i : i + 128] for i in range(128, values.shape[1], 128)) + values[:, :128]


def layer_kernel(
    shards,
    groups,
    tok,
    cot,
    w_in,
    w_out,
    vectors,
    bucket,
    labels,
    mask,
    out,
    dx,
    d_w,
    sums,
    x_all,
    c_all,
    w_all,
    small_all,
    cos_tab,
    sin_tab,
    cos_h,
    sin_h,
    n_one,
    inv_one,
    hid,
    act,
    slope,
    n_two,
    inv_two,
    grad,
    seq_c,
    seq_s,
    vecs,
    bias,
    acc,
    hits,
    near,
    far,
    turn,
    part_low,
    line_in,
    own_part,
    done_low,
    sums_own,
    sums_mp,
    sums_mid,
    sums_dp,
    load_sem,
    own_sem,
    tok_send,
    tok_recv,
    cot_send,
    cot_recv,
    small_send,
    small_recv,
    wz_send,
    wz_recv,
    wp_send,
    wp_recv,
    ws_send,
    ws_recv,
    out_send,
    out_recv,
    dx_send,
    dx_recv,
    near_send,
    near_recv,
    far_send,
    far_recv,
    turn_send,
    turn_recv,
    line_send,
    line_recv,
    done_send,
    done_recv,
    share_send,
    share_recv,
    mp_send,
    mp_recv,
    dp_send,
    dp_recv,
    near_free,
):
    me = lax.axis_index("mp")
    group = lax.axis_index("dp")
    width_local = tok.shape[0]
    width = width_local * shards
    units = w_in.shape[1]
    chunk = tok.shape[1] // shards
    slots = cos_tab.shape[0]
    slot_length = chunk // slots
    part = 2 * width // groups
    chips = groups // 2
    rows = width
    some = width // 2
    cols = slot_length
    ring = range(1, shards)
    others = range(1, chips)

    inner = jnp.where(me < shards // 2, 1, -1)
    at_end = (me == 0) | (me == shards - 1)

    def mp_peer(step):
        return lax.rem(me + step, shards)

    def inward(step):
        return lax.rem(me + step * inner + shards, shards)

    def dp_peer(step):
        return lax.rem(group + 2 * step, groups)

    core = lax.rem(group, 2)
    sibling = {"dp": group + 1 - 2 * core}
    plane = [{"dp": lax.rem(group + q, groups)} for q in range(1, groups)]
    own_w = [
        pltpu.make_async_copy(w_in, w_all.at[0, :width], own_sem.at[0]),
        pltpu.make_async_copy(w_out, w_all.at[0, width:], own_sem.at[1]),
    ]
    my_cols = pl.ds(pl.multiple_of(me * chunk, 128), chunk)
    my_rows = pl.ds(pl.multiple_of(me * width_local, 16), width_local)
    loads = [
        pltpu.make_async_copy(source, target, load_sem.at[i])
        for i, (source, target) in enumerate(
            [
                (tok.at[:, my_cols], x_all.at[my_rows]),
                (cot.at[:, my_cols], c_all.at[my_rows]),
            ]
        )
    ]
    for copy in own_w + loads:
        copy.start()

    small_all[0] = jnp.zeros((8, units), F32)
    for i, vector in enumerate(vectors):
        length = vector.shape[0]
        small_all[0, i : i + 1, :length] = vector[...].reshape(1, length)
    greet([{"mp": mp_peer(d)} for d in ring] + plane)

    def exchange(source, target, send, recv, slot, steps=(1, 2, 3)):
        copies = []
        for step in steps:
            peer = inward(step)
            d = lax.rem(peer - me + shards, shards)
            first = pl.multiple_of(peer * chunk + slot * slot_length, 128)
            copies.append(
                remote(
                    source.at[:, pl.ds(first, slot_length)],
                    target.at[
                        my_rows, pl.ds(pl.multiple_of(slot * slot_length, 128), slot_length)
                    ],
                    send.at[slot, d],
                    recv.at[slot, d],
                    {"mp": peer},
                )
            )
        return copies

    small_copies = [
        remote(
            small_all.at[0],
            small_all.at[shards - d],
            small_send.at[d],
            small_recv.at[d],
            {"mp": mp_peer(d)},
        )
        for d in ring
    ]
    for copy in small_copies:
        copy.start()
    for copy in own_w:
        copy.wait()
    my_part = pl.ds(pl.multiple_of(group * part, 16), part)

    def weight_copy(shard, target, send):
        place = lax.rem(shard - me + 2 * shards, shards)
        there = lax.rem(shard - target + 2 * shards, shards)
        return remote(
            w_all.at[place, my_part],
            w_all.at[there, my_part],
            wz_send.at[send],
            wz_recv.at[there],
            {"mp": target},
        )

    def weight_wait(place):
        remote(
            w_all.at[0, my_part],
            w_all.at[place, my_part],
            wz_send.at[0],
            wz_recv.at[place],
            {"mp": inward(1)},
        ).wait_recv()

    near_step = jnp.where(at_end, 1, 3)
    far_step = jnp.where(at_end, 2, 1)
    wz = [weight_copy(me, inward(near_step), 1), weight_copy(me, inward(far_step), 0)]
    for copy in wz:
        copy.start()
    for slot in range(slots):
        for copy in exchange(tok, x_all, tok_send, tok_recv, slot, (1, 2)):
            copy.start()

        @pl.when(at_end)
        def _():
            for copy in exchange(tok, x_all, tok_send, tok_recv, slot, (3,)):
                copy.start()

    def pass_on(step, send):
        return weight_copy(inward(step), inward(3), send)

    side = math.isqrt(chips)
    chip_x, chip_y = lax.rem(group // 2, side), group // 2 // side
    halves = (pl.ds(0, units // 2), pl.ds(units // 2, units // 2))
    arrival = [
        lax.rem(step * inner + shards, shards)
        for step in (1, jnp.where(at_end, 2, 3), jnp.where(at_end, 3, 2))
    ]

    def at_chip(x, y):
        return (lax.rem(y + side, side) * side + lax.rem(x + side, side)) * 2 + core

    def weights_of(n, who, across):
        rows_of = pl.ds(pl.multiple_of(who * part, 16), part)
        return w_all.at[arrival[n], rows_of, across]

    def plane_copy(n, who, across, to, sem):
        at = weights_of(n, who, across)
        return remote(at, at, wp_send.at[n, sem], wp_recv.at[n, sem], to)

    def to_sibling(n, who, across, sem):
        at = weights_of(n, who, across)
        return remote(at, at, ws_send.at[n, sem], ws_recv.at[n, sem], sibling)

    first_plane, second_plane = [[], [], []], [[], [], []]
    first_ws, second_ws = [[], [], []], [[], [], []]
    own_ws = [to_sibling(n, group, pl.ds(0, units), 0) for n in range(3)]
    for n in range(3):
        for h, across in enumerate(halves):
            for p in range(1, side):
                step_x, step_y = (p, 0) if h == 0 else (0, p)
                to = {"dp": at_chip(chip_x + step_x, chip_y + step_y)}
                first_plane[n].append(plane_copy(n, group, across, to, h * chips + p))
                who = at_chip(chip_x - step_x, chip_y - step_y)
                first_ws[n].append(to_sibling(n, who, across, 1 + h * (side - 1) + p - 1))
                for q in range(side):
                    if h == 0:
                        source, to = at_chip(chip_x + q, chip_y), at_chip(chip_x, chip_y + p)
                        who = at_chip(chip_x + q, chip_y - p)
                    else:
                        source, to = at_chip(chip_x, chip_y + q), at_chip(chip_x + p, chip_y)
                        who = at_chip(chip_x - p, chip_y + q)
                    sem = h * chips + side * p + q
                    second_plane[n].append(plane_copy(n, source, across, {"dp": to}, sem))
                    sem = 1 + 2 * (side - 1) + (h * (side - 1) + p - 1) * side + q
                    second_ws[n].append(to_sibling(n, who, across, sem))

    def line_arrived(n):
        weight_wait(arrival[n])
        for copy in first_plane[n]:
            copy.start()
        own_ws[n].start()

    def first_arrived(n):
        for copy in first_plane[n]:
            copy.wait_recv()
        for copy in second_plane[n] + first_ws[n]:
            copy.start()

    def second_arrived(n):
        for copy in second_plane[n]:
            copy.wait_recv()
        for copy in second_ws[n]:
            copy.start()

    turn_rows = min(64, slot_length)

    @pl.loop(0, width // turn_rows)
    def _(i):
        row = pl.ds(pl.multiple_of(i * turn_rows, 16), turn_rows)
        shape = (turn_rows, width)
        product = (
            (lax.broadcasted_iota(jnp.int32, shape, 0) + i * turn_rows)
            * lax.broadcasted_iota(jnp.int32, shape, 1)
        ).astype(F32)
        phase = product * (1.0 / width)
        phase = (product - jnp.floor(phase) * width) * (1.0 / width)
        cosine, sine = turns(phase)
        cos_h[row] = (cosine * (1.0 / math.sqrt(width))).astype(BF)
        sin_h[row] = (sine * (1.0 / math.sqrt(width))).astype(BF)

    @pl.loop(0, slots * slot_length // turn_rows)
    def _(i):
        slot = i // (slot_length // turn_rows)
        first = lax.rem(i, slot_length // turn_rows) * turn_rows
        row = pl.ds(pl.multiple_of(first, 16), turn_rows)
        shape = (turn_rows, slot_length)
        which = bucket[me * slots + slot]
        length = jnp.where(which == 0, slot_length // 4, slot_length // 2)
        length = jnp.where(which == 2, slot_length, length)
        at = lax.broadcasted_iota(jnp.int32, shape, 0) + first
        to = lax.broadcasted_iota(jnp.int32, shape, 1)
        inner = length - 1
        phase = ((at & inner) * (to & inner)) & inner
        scale = jnp.full((1, 1), length, jnp.int32).astype(F32)
        cosine, sine = turns(phase.astype(F32) / scale)
        scale = jnp.where((at ^ to) < length, lax.rsqrt(scale), 0.0)
        cos_tab[slot, row] = (cosine * scale).astype(BF)
        sin_tab[slot, row] = (sine * scale).astype(BF)


    line_arrived(0)

    @pl.when(jnp.logical_not(at_end))
    def _():
        pass_on(1, 2).start()

    line_arrived(1)
    first_arrived(0)
    line_arrived(2)

    @pl.when(jnp.logical_not(at_end))
    def _():
        pass_on(2, 3).start()
        for slot in range(slots):
            for copy in exchange(tok, x_all, tok_send, tok_recv, slot, (3,)):
                copy.start()

    first_arrived(1)
    first_arrived(2)

    for copy in loads:
        copy.wait()
    for copy in small_copies:
        copy.wait_recv()
    for r in range(shards):
        shard = lax.rem(me + r, shards)
        at = pl.ds(pl.multiple_of(shard * width_local, 8), width_local)
        bias[r] = jnp.broadcast_to(small_all[r, 0:1, :units], (128, units)).T
        for i in range(5):
            line = small_all[r, i + 1 : i + 2, : (width_local + 127) // 128 * 128]
            vecs[i, at] = jnp.broadcast_to(line, (128, line.shape[1])).T[:width_local]

    for slot in range(slots):
        at = pl.ds(pl.multiple_of(slot * slot_length, 128), slot_length)
        for copy in exchange(tok, x_all, tok_send, tok_recv, slot):
            copy.wait_recv()

        if slot == slots - 1:
            for later in range(slots):
                for copy in exchange(cot, c_all, cot_send, cot_recv, later):
                    copy.start()

        seq_c[...] = dot(x_all[:, at], cos_tab[slot]).astype(BF)
        seq_s[...] = dot(x_all[:, at], sin_tab[slot]).astype(BF)

        @pl.loop(0, width // rows)
        def _(i):
            row = pl.ds(pl.multiple_of(i * rows, rows), rows)
            mixing = dot(cos_h[row], seq_c[...]) - dot(sin_h[row], seq_s[...])
            n_one[row, at] = x_all[row, at].astype(F32) + mixing

        @pl.loop(0, slot_length // 128)
        def _(i):
            col = pl.ds(pl.multiple_of(slot * slot_length + i * 128, 128), 128)
            value = n_one[:, col]
            centered = value - jnp.mean(value, axis=0, keepdims=True)
            inverse = lax.rsqrt(jnp.mean(centered * centered, axis=0, keepdims=True) + EPSILON)
            normed = centered * inverse
            n_one[:, col] = normed
            inv_one[:, col] = inverse
            hid[:, col] = (normed * vecs[1] + vecs[2]).astype(BF)

        if slot == 0:
            for n in range(3):
                second_arrived(n)

    def first_matmul(r):
        @pl.loop(0, units // some)
        def _(i):
            row = pl.ds(pl.multiple_of(i * some, some), some)
            pre = dot(w_all[r, pl.ds(0, width), row], hid[...], 0, 0) + bias[r, row, 0:1]
            cdf = 0.5 + 0.5 * lax.erf(pre * (1.0 / math.sqrt(2.0)))
            pdf = jnp.exp(-0.5 * pre * pre) * (1.0 / math.sqrt(2.0 * math.pi))
            act[r, row] = (pre * cdf).astype(BF)
            slope[r, row] = (cdf + pre * pdf).astype(BF)

    first_matmul(0)
    ws = sum(first_ws + second_ws, own_ws)
    for copy in ws:
        copy.wait_recv()
    pl.loop(1, shards)(first_matmul)

    hits[...] = jnp.zeros_like(hits)
    acc[...] = jnp.zeros_like(acc)

    @pl.loop(0, chunk // cols)
    def _(i):
        col = pl.ds(pl.multiple_of(i * cols, cols), cols)
        second = n_one[:, col] * vecs[1, :, 0:1] + vecs[2, :, 0:1] + vecs[0, :, 0:1]
        total = dot(w_all[0, pl.ds(width, units)], act[0, :, col], 0, 0)
        for r in ring:
            total += dot(w_all[r, pl.ds(width, units)], act[r, :, col], 0, 0)
        second += total
        centered = second - jnp.mean(second, axis=0, keepdims=True)
        inverse = lax.rsqrt(jnp.mean(centered * centered, axis=0, keepdims=True) + EPSILON)
        normed = centered * inverse
        n_two[:, col] = normed
        inv_two[:, col] = inverse
        result = normed * vecs[3, :, 0:1] + vecs[4, :, 0:1]
        x_all[:, col] = result.astype(BF)
        feature = lax.broadcasted_iota(jnp.int32, (width, cols), 0)
        here = pl.ds(pl.multiple_of(me * chunk + i * cols, cols), cols)
        chosen = feature == labels[here].reshape(1, cols)
        picked = jnp.sum(jnp.where(chosen, result, 0.0), axis=0, keepdims=True)
        soft = 1.0 / (1.0 + jnp.exp(-2.0 * picked))
        hits[...] += jnp.where(mask[here].reshape(1, cols) == 1, soft, 0.0)

    def send_back(source, target, send, recv, first, length):
        copies = []
        for d in ring:
            peer = mp_peer(d)
            copies.append(
                remote(
                    source.at[
                        pl.ds(pl.multiple_of(peer * width_local, 16), width_local),
                        pl.ds(first, length),
                    ],
                    target.at[:, pl.ds(pl.multiple_of(me * chunk + first, 128), length)],
                    send.at[d],
                    recv.at[d],
                    {"mp": peer},
                )
            )
        return copies

    out_copies = [
        send_back(x_all, out, out_send.at[slot], out_recv.at[slot], slot * slot_length, slot_length)
        for slot in range(slots)
    ]
    out_own = pltpu.make_async_copy(x_all.at[my_rows], out.at[:, my_cols], own_sem.at[0])

    cot_copies = sum((exchange(cot, c_all, cot_send, cot_recv, s) for s in range(slots)), [])
    tok_copies = sum((exchange(tok, x_all, tok_send, tok_recv, s) for s in range(slots)), [])
    def norm_two_back(slot):
        col = pl.ds(slot * slot_length, slot_length)
        upstream = c_all[:, col].astype(F32)
        normed = n_two[:, col]
        scaled = upstream * vecs[3, :, 0:1]
        first = jnp.mean(scaled, axis=0, keepdims=True)
        both = jnp.mean(scaled * normed, axis=0, keepdims=True)
        grad_two = inv_two[:, col] * (scaled - first - normed * both)
        n_two[:, col] = grad_two
        low = grad_two.astype(BF)
        grad[:, col] = low
        acc[0] += lanes(low.astype(F32))
        acc[3] += lanes(upstream * normed)
        acc[4] += lanes(upstream)

    def act_back(slot):
        col = pl.ds(slot * slot_length, slot_length)

        @pl.loop(0, shards)
        def _(r):
            grad_act = dot(w_all[r, pl.ds(width, units)], grad[:, col])
            low = (grad_act * slope[r, :, col].astype(F32)).astype(BF)
            slope[r, :, col] = low
            if slot == 0:
                bias[r] = lanes(low.astype(F32))
            else:
                bias[r] += lanes(low.astype(F32))

    def hidden_back(slot):
        col = pl.ds(slot * slot_length, slot_length)
        total = dot(w_all[0, pl.ds(0, width)], slope[0, :, col])
        for r in ring:
            total += dot(w_all[r, pl.ds(0, width)], slope[r, :, col])
        upstream = n_two[:, col] + total
        normed = n_one[:, col]
        scaled = upstream * vecs[1, :, 0:1]
        first = jnp.mean(scaled, axis=0, keepdims=True)
        both = jnp.mean(scaled * normed, axis=0, keepdims=True)
        grad_one = inv_one[:, col] * (scaled - first - normed * both)
        n_two[:, col] = grad_one
        c_all[:, col] = grad_one.astype(BF)
        acc[1] += lanes(upstream * normed)
        acc[2] += lanes(upstream)

    def transform_back(slot):
        at = pl.ds(slot * slot_length, slot_length)

        @pl.loop(0, width // rows)
        def _(i):
            row = pl.ds(pl.multiple_of(i * rows, rows), rows)
            seq_c[row] = dot(cos_h[row], c_all[:, at]).astype(BF)
            seq_s[row] = -dot(sin_h[row], c_all[:, at]).astype(BF)

        @pl.loop(0, width // rows)
        def _(i):
            row = pl.ds(pl.multiple_of(i * rows, rows), rows)
            back = dot(seq_c[row], cos_tab[slot]) + dot(seq_s[row], sin_tab[slot])
            c_all[row, at] = (n_two[row, at] + back).astype(BF)

        copies = send_back(
            c_all, dx, dx_send.at[slot], dx_recv.at[slot], slot * slot_length, slot_length
        )
        copies.append(
            pltpu.make_async_copy(
                c_all.at[my_rows, at],
                dx.at[
                    :,
                    pl.ds(pl.multiple_of(me * chunk + slot * slot_length, 128), slot_length),
                ],
                own_sem.at[1 + slot],
            )
        )
        return copies

    def cotangent_here(slot):
        for copy in exchange(cot, c_all, cot_send, cot_recv, slot):
            copy.wait_recv()
        norm_two_back(slot)

    cotangent_here(0)
    act_back(0)
    hidden_back(0)
    dx_copies = [transform_back(0)]
    for slot in range(1, slots):
        cotangent_here(slot)
    for copy in sum(out_copies, dx_copies[0] + [out_own]):
        copy.start()

    half = width // 2
    split = 1 if half // chips % 16 == 0 else 2
    piece_rows = half * split // chips
    piece_cols = width // split
    keep = pl.ds(pl.multiple_of(core * half, 16), half)
    give = pl.ds(pl.multiple_of((1 - core) * half, 16), half)

    def piece(x, y):
        chip = lax.rem(y, side) * side + lax.rem(x, side)
        first = core * half + chip // split * piece_rows
        return (
            pl.ds(pl.multiple_of(first, 16), piece_rows),
            pl.ds(pl.multiple_of(lax.rem(chip, split) * piece_cols, 128), piece_cols),
        )

    d_out = act.at[:, :, pl.ds(0, width)]
    d_in = w_all.at[:, pl.ds(width, units)]

    def near_copy(x, r):
        source = (d_in, d_out)[x]
        return remote(
            source.at[r, give], near.at[r], near_send.at[x, r], near_recv.at[x, r], sibling
        )

    def far_copies(x, r):
        copies = []
        for p in range(1, side):
            peer = at_chip(
                chip_x + jnp.where(r < 2, p, 0), chip_y + jnp.where(r < 2, 0, p)
            )
            for q in range(side):
                at, across = piece(
                    chip_x + jnp.where(r < 2, p, q), chip_y + jnp.where(r < 2, q, p)
                )
                n = (p - 1) * side + q
                copies.append(
                    remote(
                        (d_in, d_out)[x].at[r, at, across],
                        far.at[x, n, r],
                        far_send.at[x, n, r],
                        far_recv.at[x, n, r],
                        {"dp": peer},
                    )
                )
        return copies

    def turn_copies(x, r):
        copies = []
        for q in range(1, side):
            to = chip_x + jnp.where(r < 2, 0, q), chip_y + jnp.where(r < 2, q, 0)
            at, across = piece(*to)
            copies.append(
                remote(
                    (d_in, d_out)[x].at[r, at, across],
                    turn.at[x, q - 1, r],
                    turn_send.at[x, q - 1, r],
                    turn_recv.at[x, q - 1, r],
                    {"dp": at_chip(*to)},
                )
            )
        return copies

    def add_near(x, r):
        source = (d_in, d_out)[x]
        near_copy(x, r).wait_recv()
        source[r, keep] = (source[r, keep].astype(F32) + near[r].astype(F32)).astype(BF)
        for copy in far_copies(x, r):
            copy.start()

    def in_turn(i):
        return lax.rem(i, 2) * 2 + i // 2

    def reduce_blocks(x, compute):
        @pl.loop(0, shards)
        def _(i):
            compute(in_turn(i))
            near_copy(x, in_turn(i)).start()

            @pl.when(i > 0)
            def _():
                add_near(x, in_turn(i - 1))

        add_near(x, shards - 1)

    def far_sum(x, r, q):
        at, across = piece(
            chip_x + jnp.where(r < 2, 0, q), chip_y + jnp.where(r < 2, q, 0)
        )
        total = (d_in, d_out)[x][r, at, across].astype(F32)
        for p in range(1, side):
            total += far[x, (p - 1) * side + q, r].astype(F32)
        return total

    def add_far(x):
        @pl.loop(0, shards)
        def _(i):
            r = in_turn(i)
            for copy in far_copies(x, r):
                copy.wait_recv()
            for q in range(1, side):
                at, across = piece(
                    chip_x + jnp.where(r < 2, 0, q), chip_y + jnp.where(r < 2, q, 0)
                )
                (d_in, d_out)[x][r, at, across] = far_sum(x, r, q).astype(BF)
            for copy in turn_copies(x, r):
                copy.start()

    my_at, my_across = piece(chip_x, chip_y)

    def add_turn(x):
        @pl.loop(0, shards)
        def _(r):
            for copy in turn_copies(x, r):
                copy.wait_recv()
            total = far_sum(x, r, 0)
            for q in range(1, side):
                total += turn[x, q - 1, r].astype(F32)
            part_low[x, r] = total.astype(BF)

            @pl.when(r == 0)
            def _():
                own_part[x] = total

        @pl.when(at_end)
        def _():
            for step, place in ((2, 2), (3, 3), (1, 0)):
                line_copy(x, step, inward(1), place).start()

        @pl.when(jnp.logical_not(at_end))
        def _():
            line_copy(x, 3, inward(3), 0).start()

    def line_copy(x, step, target, place):
        return remote(
            part_low.at[x, lax.rem(step * inner + shards, shards)],
            line_in.at[x, place],
            line_send.at[x, step],
            line_recv.at[x, place],
            {"mp": target},
        )

    def line_on(x):
        @pl.when(jnp.logical_not(at_end))
        def _():
            for step in (1, 2):
                line_copy(x, step, inward(step), step + 1).wait_recv()
                r = lax.rem(step * inner + shards, shards)
                part_low[x, r] = (
                    part_low[x, r].astype(F32) + line_in[x, step + 1].astype(F32)
                ).astype(BF)
                line_copy(x, step, inward(step), 1).start()

    def add_line(x):
        for place in (0, 1):
            line_copy(x, 1, inward(1), place).wait_recv()
        total = own_part[x] + line_in[x, 0].astype(F32) + line_in[x, 1].astype(F32)
        done_low[x] = total.astype(BF)
        target = d_w.at[x, my_at, my_across]
        copies = [
            remote(
                done_low.at[x], target, done_send.at[x, k], done_recv.at[x, k], {"dp": dp_peer(k)}
            )
            for k in others
        ]
        own = pltpu.make_async_copy(done_low.at[x], target, own_sem.at[1 + slots + x])
        for copy in copies + [own]:
            copy.start()
        return copies, own

    def share(x, copies, own):
        own.wait()
        for copy in copies:
            copy.wait_recv()
        copy = remote(
            d_w.at[x, keep], d_w.at[x, keep], share_send.at[x], share_recv.at[x], sibling
        )
        copy.start()
        return copy

    def second_weight(r):
        @pl.loop(0, units // rows)
        def _(i):
            row = pl.ds(pl.multiple_of(i * rows, rows), rows)
            d_out[r, row] = dot(act[r, row], grad[...], 1, 1).astype(BF)

    second_slots = range(1, slots)
    reduce_blocks(1, second_weight)
    pl.semaphore_signal(
        near_free, inc=1, device_id=sibling, device_id_type=pl.DeviceIdType.MESH
    )
    for slot in second_slots:
        act_back(slot)

    for copy in wz + sum(first_plane + second_plane, ws):
        copy.wait_send()

    @pl.when(jnp.logical_not(at_end))
    def _():
        pass_on(1, 2).wait_send()
        pass_on(2, 3).wait_send()

    def first_weight(r):
        @pl.loop(0, width // rows)
        def _(i):
            row = pl.ds(pl.multiple_of(i * rows, rows), rows)
            d_in[r, row] = dot(hid[row], slope[r], 1, 1).astype(BF)

    pl.semaphore_wait(near_free, 1)
    reduce_blocks(0, first_weight)
    add_far(1)
    for slot in second_slots:
        hidden_back(slot)
        if slot == 1:
            add_turn(1)
        dx_copies.append(transform_back(slot))
    add_far(0)

    lane = lax.broadcasted_iota(jnp.int32, (width_local, 128), 1)
    total_hits = jnp.sum(hits[...], axis=1, keepdims=True)
    for r in range(shards):
        shard = lax.rem(me + r, shards)
        at = pl.ds(pl.multiple_of(shard * width_local, 8), width_local)
        sums_own[r, 0:1] = jnp.broadcast_to(
            jnp.sum(bias[r], axis=1, keepdims=True), (units, 128)
        ).T[0:1]
        line = jnp.where(lane == 6, total_hits, 0.0)
        for i in range(5):
            line += jnp.where(lane == i + 1, jnp.sum(acc[i, at], axis=1, keepdims=True), 0.0)
        spare = (-width_local) % 128
        if spare:
            line = jnp.concatenate([line, jnp.zeros((spare, 128), F32)], axis=0)
        sums_own[r, 1:8, : width_local + spare] = line.T[1:8]
        sums_own[r, 1:8, width_local + spare :] = jnp.zeros((7, units - width_local - spare), F32)
    mp_sums = [
        remote(sums_own.at[d], sums_mp.at[me], mp_send.at[d], mp_recv.at[d], {"mp": mp_peer(d)})
        for d in ring
    ]
    for copy in mp_sums:
        copy.start()
    sums_mp[me] = sums_own[0]

    add_turn(0)
    line_on(1)
    line_on(0)
    for copies in dx_copies[1:]:
        for copy in copies:
            copy.start()
    done_out, own_out = add_line(1)
    for copy in mp_sums:
        copy.wait_recv()
    sums_mid[...] = sum(sums_mp[s] for s in range(shards))
    dp_sums = [
        remote(sums_mid, sums_dp.at[group], dp_send.at[q], dp_recv.at[q], peer)
        for q, peer in enumerate(plane)
    ]
    for copy in dp_sums:
        copy.start()
    sums_dp[group] = sums_mid[...]
    done_in, own_in = add_line(0)
    share_out = share(1, done_out, own_out)
    for copy in dp_sums:
        copy.wait_recv()
    sums[...] = sum(sums_dp[q] for q in range(groups))
    share_in = share(0, done_in, own_in)

    @pl.loop(0, shards)
    def _(r):
        for x in range(2):
            for copy in [near_copy(x, r)] + far_copies(x, r) + turn_copies(x, r):
                copy.wait_send()

            @pl.when(r > 0)
            def _():
                line_copy(x, r, inward(1), 0).wait_send()

    for copy in small_copies + tok_copies + cot_copies + mp_sums + dp_sums:
        copy.wait_send()
    for copy in done_out + done_in:
        copy.wait_send()
    for copy in sum(out_copies + dx_copies, [out_own, share_out, share_in]):
        copy.wait()


def layer_call(shards, groups, tok, cot, w_in, w_out, vectors, bucket, labels, mask):
    width_local, tokens = tok.shape
    width = width_local * shards
    units = w_in.shape[1]
    chunk = tokens // shards
    slot_length = tokens // bucket.shape[0]
    slots = chunk // slot_length
    cols = slot_length
    dma = pltpu.SemaphoreType.DMA
    chips = groups // 2
    side = math.isqrt(chips)
    split = 1 if width // 2 // chips % 16 == 0 else 2
    piece = (width // 2 * split // chips, width // split)
    return pl.pallas_call(
        functools.partial(layer_kernel, shards, groups),
        out_shape=[
            jax.ShapeDtypeStruct((width_local, tokens), BF),
            jax.ShapeDtypeStruct((width_local, tokens), BF),
            jax.ShapeDtypeStruct((2, width, units), BF),
            jax.ShapeDtypeStruct((8, units), F32),
        ],
        in_specs=[ANY] * 4 + [[VMEM] * 6, SMEM, VMEM, VMEM],
        out_specs=[ANY, ANY, ANY, VMEM],
        scratch_shapes=[
            pltpu.VMEM((width, chunk), BF),
            pltpu.VMEM((width, chunk), BF),
            pltpu.VMEM((shards, 2 * width, units), BF),
            pltpu.VMEM((shards, 8, units), F32),
            pltpu.VMEM((slots, slot_length, slot_length), BF),
            pltpu.VMEM((slots, slot_length, slot_length), BF),
            pltpu.VMEM((width, width), BF),
            pltpu.VMEM((width, width), BF),
            pltpu.VMEM((width, chunk), F32),
            pltpu.VMEM((1, chunk), F32),
            pltpu.VMEM((width, chunk), BF),
            pltpu.VMEM((shards, units, chunk), BF),
            pltpu.VMEM((shards, units, chunk), BF),
            pltpu.VMEM((width, chunk), F32),
            pltpu.VMEM((1, chunk), F32),
            pltpu.VMEM((width, chunk), BF),
            pltpu.VMEM((width, slot_length), BF),
            pltpu.VMEM((width, slot_length), BF),
            pltpu.VMEM((5, width, 128), F32),
            pltpu.VMEM((shards, units, 128), F32),
            pltpu.VMEM((5, width, 128), F32),
            pltpu.VMEM((1, cols), F32),
            pltpu.VMEM((shards, width // 2, width), BF),
            pltpu.VMEM((2, (side - 1) * side, shards) + piece, BF),
            pltpu.VMEM((2, side - 1, shards) + piece, BF),
            pltpu.VMEM((2, shards) + piece, BF),
            pltpu.VMEM((2, shards) + piece, BF),
            pltpu.VMEM((2,) + piece, F32),
            pltpu.VMEM((2,) + piece, BF),
            pltpu.VMEM((shards, 8, units), F32),
            pltpu.VMEM((shards, 8, units), F32),
            pltpu.VMEM((8, units), F32),
            pltpu.VMEM((groups, 8, units), F32),
            dma((2,)),
            dma((3 + slots,)),
        ]
        + [dma((slots, shards))] * 4
        + [dma((shards,))] * 4
        + [dma((shards - 1, 2 * chips))] * 4
        + [dma((slots, shards))] * 4
        + [dma((2, shards))] * 2
        + [dma((2, (side - 1) * side, shards))] * 2
        + [dma((2, side - 1, shards))] * 2
        + [dma((2, shards))] * 2
        + [dma((2, chips))] * 2
        + [dma((2,))] * 2
        + [dma((shards,))] * 2
        + [dma((groups,))] * 2
        + [pltpu.SemaphoreType.REGULAR],
        compiler_params=pltpu.CompilerParams(
            collective_id=0, has_side_effects=True, vmem_limit_bytes=VMEM_LIMIT
        ),
        name="layer",
    )(tok, cot, w_in, w_out, vectors, bucket, labels, mask)


def finish_kernel(scale, low_x, low_w, sums, d_tokens, d_w_in, d_w_out, hits, d_b_in, *rest):
    d_tokens[...] = low_x[...].astype(F32)
    d_w_in[...] = low_w[0].astype(F32)
    d_w_out[...] = low_w[1].astype(F32)

    @pl.when(pl.program_id(0) == 0)
    def _():
        d_b_in[...] = sums[0]
        for i, target in enumerate(rest):
            target[...] = sums[i + 1, : target.shape[0]]
        hits[0, 0] = jnp.sum(sums[6:7, 0:1]) * scale


def finish_call(scale, low_x, low_w, sums):
    width_local, tokens = low_x.shape
    _, width, units = low_w.shape
    steps = 4
    whole = lambda length: pl.BlockSpec((length,), lambda i: (0,))
    return pl.pallas_call(
        functools.partial(finish_kernel, scale),
        grid=(steps,),
        out_shape=[
            jax.ShapeDtypeStruct((width_local, tokens), F32),
            jax.ShapeDtypeStruct((width, units), F32),
            jax.ShapeDtypeStruct((units, width), F32),
            jax.ShapeDtypeStruct((1, 1), F32),
            jax.ShapeDtypeStruct((units,), F32),
        ]
        + [jax.ShapeDtypeStruct((width_local,), F32)] * 5,
        in_specs=[
            pl.BlockSpec((width_local, tokens // steps), lambda i: (0, i)),
            pl.BlockSpec((2, width // steps, units), lambda i: (0, i, 0)),
            pl.BlockSpec((8, units), lambda i: (0, 0)),
        ],
        out_specs=[
            pl.BlockSpec((width_local, tokens // steps), lambda i: (0, i)),
            pl.BlockSpec((width // steps, units), lambda i: (i, 0)),
            pl.BlockSpec((units // steps, width), lambda i: (i, 0)),
            pl.BlockSpec(memory_space=pltpu.SMEM),
            whole(units),
        ]
        + [whole(width_local)] * 5,
        name="finish",
    )(low_x, low_w, sums)


def body(
    tokens,
    bucket,
    w_in,
    b_in,
    w_out,
    b_out,
    gain_one,
    shift_one,
    gain_two,
    shift_two,
    mask,
    labels,
    cotangent,
):
    shards = lax.axis_size("mp")
    groups = lax.axis_size("dp")
    width_local, token_count = tokens.shape
    vectors = [b_in, b_out, gain_one, shift_one, gain_two, shift_two]
    output, d_x, grads, sums = layer_call(
        shards,
        groups,
        tokens,
        cotangent,
        w_in,
        w_out,
        vectors,
        bucket,
        labels,
        mask,
    )
    d_tokens, d_w_in, d_w_out, hits, d_b_in, *rest = finish_call(
        8.0 / (token_count * groups), d_x, grads, sums
    )
    return (output, d_tokens, d_w_in, d_b_in, d_w_out, *rest, hits[0, 0])


def solution(mesh):
    in_specs = (
        P("mp", "dp"),
        P("dp"),
        P(None, "mp"),
        P("mp"),
        P("mp", None),
        P("mp"),
        P("mp"),
        P("mp"),
        P("mp"),
        P("mp"),
        P("dp"),
        P("dp"),
        P("mp", "dp"),
    )
    out_specs = (
        P("mp", "dp"),
        P("mp", "dp"),
        P(None, "mp"),
        P("mp"),
        P("mp", None),
        P("mp"),
        P("mp"),
        P("mp"),
        P("mp"),
        P("mp"),
        P(),
    )
    return jax.shard_map(body, mesh=mesh, in_specs=in_specs, out_specs=out_specs, check_vma=False)
```
